32 devices in a mesh: req: 8 (over z, x), kv: 4 (over y, core).
Axes of the slice: x: 2, y: 2, z: 4, core: 2. Of those that a mesh axis runs over, the one named last changes fastest.
Arguments:
- activations: bfloat16 [1024, 8192], P('kv', 'req'), may hold values from -210 to 210
- input_gain: bfloat16 [8192], P('req'), may hold values from 0.25 to 1.75
- qkv_weight: bfloat16 [8192, 8, 1280], P('req', 'kv'), may hold values from -0.0625 to 0.0625
- out_weight: bfloat16 [8, 1024, 8192], P('kv', None, 'req'), may hold values from -0.1875 to 0.1875
- post_gain: bfloat16 [8192], P('req'), may hold values from 0.25 to 1.75
- cache_entries: bfloat16 [40, 4096, 8, 256], P('req', None, 'kv'), may hold values from -140 to 140
- new_lengths: int32 [8, 5], replicated, may hold values from 1 to 96, 128 in all within a row
- cache_lengths: int32 [8, 5], replicated, may hold values from 1 to 4096, as said below
- request_slot: int32 [40], replicated, may hold values from 0 to 39, each once
Outputs:
- projected: bfloat16 [1024, 8192], P('kv', 'req')
- normed: bfloat16 [1024, 8192], P('kv', 'req')
- appended: bfloat16 [1024, 8, 256], P('req', 'kv')
The draws below stay inside these ranges and needn't reach their ends.
Inputs may be any that keep to these rules, and one draw needn't show every extreme that they name: `new_lengths`: the 5 requests of one block bring 128 new tokens together; in every block one request brings exactly 96. `cache_lengths`: A request's cache holds fewer than 256 positions or exactly 4096; some request holds 4096. Each number once; request q of the arrival order sits in block request_slot[q] // 5, slot request_slot[q] % 5.
All inputs are finite; a program needn't handle non-finite values.
Results may differ from the reference program's by a relative error of at most 0.012.
The reference program's roundings to bfloat16 on the way count: a program that leaves them out, or rounds other values in their place, can miss the bound.
Values may be sent and summed in bfloat16 or wider, within the bound.
A program may use at most 512 MiB of HBM per device.

```python
import math
import jax
import jax.numpy as jnp
import numpy as np
from jax import lax

D = 8192
HQ = 64
KVH = 8
HD = 128
GROUP = 8
REQ_BLK = 5
TOK_BLK = 128
MOST_NEW = 96
SLOT = 4096
SHORT = 256
TOKENS = 1024
REQS = 40
N_REQ = 8


def draw_activations(key, part):
    first_key, second_key, third_key = jax.random.split(key, 3)
    columns = jnp.arange(D, dtype=jnp.float32) / D
    rising = math.log(3.0)
    values = jnp.clip(jax.random.normal(first_key, (TOKENS, D), jnp.float32), -5.0, 5.0)
    column_scale = jnp.exp(rising * columns + jax.random.uniform(second_key, (D,), jnp.float32, -1.0, 1.0))
    row_scale = jnp.exp(jax.random.uniform(third_key, (TOKENS, 1), jnp.float32, 0.0, math.log(10.0)))
    return (values * column_scale[None, :] * row_scale * 0.5).astype(jnp.bfloat16)


def draw_cache_entries(key, part):
    first_key, second_key = jax.random.split(key, 2)
    grid_shape = (REQS, SLOT, KVH, HD)
    stored_keys = 2.0 * jnp.clip(jax.random.normal(first_key, grid_shape, jnp.float32), -5.0, 5.0)
    stored_values = jnp.clip(jax.random.normal(second_key, grid_shape, jnp.float32), -5.0, 5.0)
    return jnp.concatenate([stored_keys, stored_values], axis=-1).astype(jnp.bfloat16)


def draw_cache_lengths(key, part):
    first_key, second_key, third_key = jax.random.split(key, 3)
    grid_shape = (N_REQ, REQ_BLK)
    short_len = jax.random.randint(first_key, grid_shape, 1, SHORT)
    longer = jax.random.randint(second_key, grid_shape, 0, 8) == 0
    chosen = jax.random.randint(third_key, (), 0, N_REQ * REQ_BLK)
    flat_pick = jnp.arange(N_REQ * REQ_BLK, dtype=jnp.int32).reshape(grid_shape) == chosen
    return jnp.where(longer | flat_pick, SLOT, short_len).astype(jnp.int32)


def block_scale(stream_key, shape, cuts, low, largest):
    gain = 1.0
    for dim, parts in cuts:
        draws = jax.random.uniform(jax.random.fold_in(jax.random.fold_in(stream_key, 6), dim), (parts,), jnp.float32, low / len(cuts), largest / len(cuts))
        gain = gain * jnp.repeat(jnp.exp(draws), shape[dim] // parts).reshape((-1,) + (1,) * (len(shape) - 1 - dim))
    return gain


def profile(amount, total, reach, skew):
    weights = [(1 << 20) // math.isqrt(standing ** skew) + 1 for standing in range(2, amount + 1)]
    surplus, given = total - reach - (amount - 1), [1] * (amount - 1)
    while surplus > 0:
        candidates = [i for i in range(amount - 1) if given[i] < reach]
        whole, left = sum([weights[i] for i in candidates]), surplus
        for i in candidates:
            more = min(reach - given[i], max(1, left * weights[i] // whole), surplus)
            given[i] = given[i] + more
            surplus = surplus - more
    return np.array([reach] + given)


def uneven_parts(key, amount, total, most, lean):
    if amount == 2:
        one = jax.random.randint(key, (), max(1, total - most), min(most, total - 1) + 1)
        return jnp.stack([one, total - one])
    lengths = jnp.asarray(profile(amount, total, most, lean), jnp.int32)
    couples = (amount - 1) // 2
    source_of, sink = lengths[1:1 + 2 * couples:2], lengths[2:2 + 2 * couples:2]
    slack = jnp.minimum(source_of - 1, most - sink)
    passed = jax.random.randint(jax.random.fold_in(key, 1), (couples,), 0, 1 << 20) % (slack + 1)
    lengths = lengths.at[1:1 + 2 * couples:2].set(source_of - passed).at[2:2 + 2 * couples:2].set(sink + passed)
    return lengths[jax.random.permutation(jax.random.fold_in(key, 2), amount)]


def normal_values(own_key, dims, scale, bound, cuts=(), held_as=jnp.bfloat16):
    factor_of = block_scale(own_key, dims, cuts, -0.22, 0.18) if cuts else 1.0
    drawn = jax.random.normal(own_key, dims, jnp.float32) * scale * factor_of
    return jnp.minimum(jnp.maximum(drawn, -bound), bound).astype(held_as)


def setup_inputs(seed: int = 0) -> dict:
    seeds = jax.random.split(jax.random.key(seed), 10)
    return {
        "activations": draw_activations(jax.random.fold_in(seeds[9], 71), 0),
        "input_gain": jnp.clip(1.0 + 0.15 * jax.random.normal(seeds[1], (D,), jnp.float32), 0.25, 1.75).astype(jnp.bfloat16),
        "qkv_weight": normal_values(seeds[2], (D, KVH, (GROUP + 2) * HD), D ** -0.5, 0.0625, ((0, 8), (1, 4))),
        "out_weight": normal_values(seeds[3], (KVH, GROUP * HD, D), (GROUP * HD) ** -0.5, 0.1875, ((0, 4), (2, 8))),
        "post_gain": jnp.clip(1.0 + 0.15 * jax.random.normal(seeds[4], (D,), jnp.float32), 0.25, 1.75).astype(jnp.bfloat16),
        "cache_entries": draw_cache_entries(jax.random.fold_in(seeds[9], 71), 0),
        "new_lengths": jax.vmap(lambda own: uneven_parts(own, REQ_BLK, TOK_BLK, MOST_NEW, 2))(jax.random.split(seeds[6], N_REQ)).reshape((N_REQ, REQ_BLK)).astype(jnp.int32),
        "cache_lengths": draw_cache_lengths(jax.random.fold_in(seeds[9], 71), 0),
        "request_slot": jax.random.permutation(seeds[8], REQS).astype(jnp.int32),
    }


epsilon_norm = 1e-05
rope_base = 500000.0

def layout(new_lengths, cache_lengths, request_slot, block_tokens):
    blocks, per_block = new_lengths.shape
    request_total = blocks * per_block
    token_total = blocks * block_tokens
    slot_ids = jnp.arange(request_total, dtype=jnp.int32)
    new_flat = new_lengths.reshape(request_total).astype(jnp.int32)
    cache_flat = cache_lengths.reshape(request_total).astype(jnp.int32)
    chosen = (request_slot[:, None] == slot_ids[None, :]).astype(jnp.int32)
    arrival_len = lax.optimization_barrier(jnp.sum(chosen * new_flat[None, :], axis=1)).astype(jnp.int32)
    arrival_start = (jnp.cumsum(arrival_len) - arrival_len).astype(jnp.int32)
    inside = (jnp.cumsum(new_lengths, axis=1) - new_lengths).astype(jnp.int32)
    slot_start = (inside + block_tokens * jnp.arange(blocks, dtype=jnp.int32)[:, None]).reshape(request_total).astype(jnp.int32)
    slot_arrival_start = lax.optimization_barrier(jnp.sum(chosen * arrival_start[:, None], axis=0)).astype(jnp.int32)
    positions = jnp.arange(token_total, dtype=jnp.int32)
    slot_of_row = (lax.optimization_barrier(jnp.sum((slot_start[None, :] <= positions[:, None]).astype(jnp.int32), axis=1)) - 1).astype(jnp.int32)
    row_pick = (slot_of_row[:, None] == slot_ids[None, :]).astype(jnp.int32)
    offset_row = (positions - lax.optimization_barrier(jnp.sum(row_pick * slot_start[None, :], axis=1))).astype(jnp.int32)
    token_of_row = (lax.optimization_barrier(jnp.sum(row_pick * slot_arrival_start[None, :], axis=1)) + offset_row).astype(jnp.int32)
    pos_of_row = (lax.optimization_barrier(jnp.sum(row_pick * cache_flat[None, :], axis=1)) + offset_row).astype(jnp.int32)
    arrival_of_token = (lax.optimization_barrier(jnp.sum((arrival_start[None, :] <= positions[:, None]).astype(jnp.int32), axis=1)) - 1).astype(jnp.int32)
    token_pick = (arrival_of_token[:, None] == slot_ids[None, :]).astype(jnp.int32)
    slot_of_token = lax.optimization_barrier(jnp.sum(token_pick * request_slot[None, :], axis=1)).astype(jnp.int32)
    offset_token = (positions - lax.optimization_barrier(jnp.sum(token_pick * arrival_start[None, :], axis=1))).astype(jnp.int32)
    token_slot_pick = (slot_of_token[:, None] == slot_ids[None, :]).astype(jnp.int32)
    row_of_token = (lax.optimization_barrier(jnp.sum(token_slot_pick * slot_start[None, :], axis=1)) + offset_token).astype(jnp.int32)
    pos_of_token = (lax.optimization_barrier(jnp.sum(token_slot_pick * cache_flat[None, :], axis=1)) + offset_token).astype(jnp.int32)
    return (token_of_row, row_of_token, pos_of_row, pos_of_token, slot_of_row, offset_row, slot_start)

def rotate(partial_sums, positions, group_size, head_size):
    half_size = head_size // 2
    frequency = jnp.exp(-(jnp.arange(half_size, dtype=jnp.float32) * (2.0 / head_size)) * math.log(rope_base))
    angles = positions.astype(jnp.float32)[:, None] * frequency[None, :]
    cosine = jnp.cos(angles)[:, None, None, :]
    sine_part = jnp.sin(angles)[:, None, None, :]
    turned = partial_sums[:, :, :group_size + 1, :]
    first_half = turned[..., :half_size]
    second_half = turned[..., half_size:]
    turned = jnp.concatenate([first_half * cosine - second_half * sine_part, second_half * cosine + first_half * sine_part], axis=-1)
    return jnp.concatenate([turned, partial_sums[:, :, group_size + 1:, :]], axis=2)

def reference(activations, input_gain, qkv_weight, out_weight, post_gain, cache_entries, new_lengths, cache_lengths, request_slot):
    group_size = HQ // KVH
    inputs_f32 = activations.astype(jnp.float32)
    normed_in = (inputs_f32 * lax.rsqrt(lax.optimization_barrier(jnp.mean(inputs_f32 * inputs_f32, axis=1, keepdims=True)) + epsilon_norm) * input_gain.astype(jnp.float32)[None, :]).astype(jnp.bfloat16)
    token_of_row, row_of_token, pos_of_row, pos_of_token, slot_of_row, offset_row, slot_start = layout(new_lengths, cache_lengths, request_slot, TOK_BLK)
    qkv_sums = jnp.dot(normed_in, qkv_weight.reshape(D, KVH * (group_size + 2) * HD), preferred_element_type=jnp.float32)
    rotated = rotate(qkv_sums.reshape(TOKENS, KVH, group_size + 2, HD), pos_of_token, group_size, HD).astype(jnp.bfloat16)
    block_rows = jnp.take(rotated, token_of_row, axis=0)
    appended = block_rows[:, :, group_size:, :].reshape(TOKENS, KVH, 2 * HD)
    new_flat = new_lengths.reshape(REQS).astype(jnp.int32)
    cache_flat = cache_lengths.reshape(REQS).astype(jnp.int32)
    score_scale = 1.0 / math.sqrt(HD)

    def one_slot(slot_index):
        block_index = slot_index // REQ_BLK
        offsets = jnp.arange(MOST_NEW, dtype=jnp.int32)
        picked = jnp.minimum(slot_start[slot_index] + offsets, block_index * TOK_BLK + TOK_BLK - 1).astype(jnp.int32)
        slot_rows = jnp.take(block_rows, picked, axis=0).astype(jnp.float32)
        queries = slot_rows[:, :, :group_size, :]
        new_keys = slot_rows[:, :, group_size, :]
        new_values = slot_rows[:, :, group_size + 1, :]
        stored = lax.dynamic_index_in_dim(cache_entries, slot_index, 0, keepdims=False).astype(jnp.float32)
        cached_count = cache_flat[slot_index]
        new_count = new_flat[slot_index]
        cache_scores = jnp.einsum('ihgd,khd->hgik', queries, stored[..., :HD]) * score_scale
        cache_valid = jnp.arange(SLOT, dtype=jnp.int32) < cached_count
        cache_scores = jnp.where(cache_valid[None, None, None, :], cache_scores, -jnp.inf)
        new_valid = (offsets[None, :] <= offsets[:, None]) & (offsets[None, :] < new_count)
        new_scores = jnp.einsum('ihgd,jhd->hgij', queries, new_keys) * score_scale
        new_scores = jnp.where(new_valid[None, None], new_scores, -jnp.inf)
        highest = jnp.maximum(lax.optimization_barrier(jnp.max(cache_scores, axis=-1)), lax.optimization_barrier(jnp.max(new_scores, axis=-1)))
        cache_weights = jnp.exp(cache_scores - highest[..., None])
        new_weights = jnp.exp(new_scores - highest[..., None])
        totals = lax.optimization_barrier(jnp.sum(cache_weights, axis=-1)) + lax.optimization_barrier(jnp.sum(new_weights, axis=-1))
        cache_rounded = lax.optimization_barrier(cache_weights.astype(jnp.bfloat16)).astype(jnp.float32)
        new_rounded = lax.optimization_barrier(new_weights.astype(jnp.bfloat16)).astype(jnp.float32)
        summed = jnp.einsum('hgik,khd->ihgd', cache_rounded, stored[..., HD:]) + jnp.einsum('hgij,jhd->ihgd', new_rounded, new_values)
        return (summed / jnp.transpose(totals, (2, 0, 1))[..., None]).astype(jnp.bfloat16)
    stacked = lax.map(one_slot, jnp.arange(REQS, dtype=jnp.int32))
    flat_rows = stacked.reshape(REQS * MOST_NEW, KVH * group_size * HD)
    attention = jnp.take(flat_rows, (slot_of_row * MOST_NEW + offset_row).astype(jnp.int32), axis=0)
    token_attention = jnp.take(attention, row_of_token, axis=0)
    projection = jnp.dot(token_attention, out_weight.reshape(KVH * group_size * HD, D), preferred_element_type=jnp.float32)
    projected = projection.astype(jnp.bfloat16)
    residual = inputs_f32 + projection
    normed = (residual * lax.rsqrt(lax.optimization_barrier(jnp.mean(residual * residual, axis=1, keepdims=True)) + epsilon_norm) * post_gain.astype(jnp.float32)[None, :]).astype(jnp.bfloat16)
    return (projected, normed, appended)
```

```python
import functools
import math

import jax
import jax.numpy as jnp
from jax import lax
from jax.experimental import pallas as pl
from jax.experimental.pallas import tpu as pltpu
from jax.sharding import PartitionSpec as P

epsilon_norm = 1e-05
rope_base = 500000.0


def sums_before(values):
    count = values.shape[1]
    earlier = jnp.arange(count)[:, None] < jnp.arange(count)[None, :]
    return jnp.sum(jnp.where(earlier[None], values[:, :, None], 0), axis=1)


def layout(new_lengths, cache_lengths, request_slot, block_tokens):
    blocks, per_block = new_lengths.shape
    request_total = blocks * per_block
    token_total = blocks * block_tokens
    slot_ids = jnp.arange(request_total, dtype=jnp.int32)
    new_flat = new_lengths.reshape(request_total)
    cache_flat = cache_lengths.reshape(request_total)
    chosen = (request_slot[:, None] == slot_ids[None, :]).astype(jnp.int32)
    arrival_len = jnp.sum(chosen * new_flat[None, :], axis=1)
    arrival_start = sums_before(arrival_len[None])[0]
    inside = sums_before(new_lengths)
    slot_start = (inside + block_tokens * jnp.arange(blocks, dtype=jnp.int32)[:, None]).reshape(
        request_total
    )
    slot_arrival_start = jnp.sum(chosen * arrival_start[:, None], axis=0)
    positions = jnp.arange(token_total, dtype=jnp.int32)
    slot_of_row = jnp.sum((slot_start[None, :] <= positions[:, None]).astype(jnp.int32), axis=1) - 1
    row_pick = (slot_of_row[:, None] == slot_ids[None, :]).astype(jnp.int32)
    offset_row = positions - jnp.sum(row_pick * slot_start[None, :], axis=1)
    token_of_row = jnp.sum(row_pick * slot_arrival_start[None, :], axis=1) + offset_row
    pos_of_row = jnp.sum(row_pick * cache_flat[None, :], axis=1) + offset_row
    arrival_of_token = (
        jnp.sum((arrival_start[None, :] <= positions[:, None]).astype(jnp.int32), axis=1) - 1
    )
    token_pick = (arrival_of_token[:, None] == slot_ids[None, :]).astype(jnp.int32)
    slot_of_token = jnp.sum(token_pick * request_slot[None, :], axis=1)
    offset_token = positions - jnp.sum(token_pick * arrival_start[None, :], axis=1)
    token_slot_pick = (slot_of_token[:, None] == slot_ids[None, :]).astype(jnp.int32)
    row_of_token = jnp.sum(token_slot_pick * slot_start[None, :], axis=1) + offset_token
    return (token_of_row, row_of_token, pos_of_row, slot_of_row, offset_row)


def attention_kernel(
    group_size, key_block, cached_ref, new_ref, q_ref, key_ref, value_ref, stored_ref, out_ref, keys, values, scores
):
    slot = pl.program_id(0)
    cached_count = cached_ref[slot]
    new_count = new_ref[slot]
    heads, rows_all, head_size = q_ref.shape[1:]
    most_new = key_ref.shape[2]
    slot_length = stored_ref.shape[1]
    chunk = min(256, rows_all)
    chunk_tokens = chunk // group_size
    block_count = (cached_count + key_block - 1) // key_block
    scale = math.log2(math.e) / math.sqrt(head_size)

    def split_heads(index, carry):
        at = pl.ds(pl.multiple_of(index * key_block, key_block), key_block)
        for head in range(heads):
            piece = stored_ref[0, at, head, :]
            keys[head, at, :] = piece[:, :head_size]
            values[head, at, :] = piece[:, head_size:]
        return carry

    lax.fori_loop(0, block_count, split_heads, 0)

    def lane_fold(op, value):
        folded = value[:, :head_size]
        for part in range(1, value.shape[1] // head_size):
            folded = op(folded, value[:, part * head_size : (part + 1) * head_size])
        return folded

    contract_last = (((1,), (1,)), ((), ()))
    for head in range(heads):
        for part in range(rows_all // chunk):

            @pl.when(part * chunk_tokens < new_count)
            def _(head=head, part=part):
                rows = pl.ds(part * chunk, chunk)
                query = q_ref[0, head, rows, :]
                columns = lax.broadcasted_iota(jnp.int32, (chunk, most_new), 1)
                offsets = part * chunk_tokens + (
                    lax.broadcasted_iota(jnp.int32, (chunk, most_new), 0) // group_size
                )
                own = lax.dot_general(
                    query, key_ref[0, head], contract_last, preferred_element_type=jnp.float32
                )
                own = jnp.where((columns <= offsets) & (columns < new_count), own, -jnp.inf)
                places = lax.broadcasted_iota(jnp.int32, (chunk, key_block), 1)

                def fill(index, highest):
                    first = pl.multiple_of(index * key_block, key_block)
                    found = lax.dot_general(
                        query,
                        keys[head, pl.ds(first, key_block), :],
                        contract_last,
                        preferred_element_type=jnp.float32,
                    )
                    found = jnp.where(places < cached_count - first, found, -jnp.inf)
                    scores[:, pl.ds(first, key_block)] = found
                    return jnp.maximum(highest, lane_fold(jnp.maximum, found))

                highest = lax.fori_loop(
                    0, block_count, fill, jnp.full((chunk, head_size), -jnp.inf, jnp.float32)
                )
                top = jnp.maximum(
                    jnp.max(highest, axis=1, keepdims=True), jnp.max(own, axis=1, keepdims=True)
                )
                own_weights = jnp.exp2((own - top) * scale)
                summed = jnp.dot(
                    own_weights.astype(jnp.bfloat16),
                    value_ref[0, head],
                    preferred_element_type=jnp.float32,
                )

                def accumulate(index, pair):
                    first = pl.multiple_of(index * key_block, key_block)
                    weights = jnp.exp2((scores[:, pl.ds(first, key_block)] - top) * scale)
                    added = jnp.dot(
                        weights.astype(jnp.bfloat16),
                        values[head, pl.ds(first, key_block), :],
                        preferred_element_type=jnp.float32,
                    )
                    return (pair[0] + lane_fold(jnp.add, weights), pair[1] + added)

                totals, summed = lax.fori_loop(
                    0,
                    block_count,
                    accumulate,
                    (jnp.zeros((chunk, head_size), jnp.float32), summed),
                )
                total = jnp.sum(totals, axis=1, keepdims=True) + jnp.sum(
                    own_weights, axis=1, keepdims=True
                )
                out_ref[0, head, rows, :] = (summed / total).astype(out_ref.dtype)


def block_attention(queries, new_keys, new_values, stored, cached_counts, new_counts, group_size):
    slots, heads, rows, head_size = queries.shape
    most_new = new_keys.shape[2]
    slot_length = stored.shape[1]
    key_block = min(512, slot_length)
    grid_spec = pltpu.PrefetchScalarGridSpec(
        num_scalar_prefetch=2,
        grid=(slots,),
        in_specs=[
            pl.BlockSpec((1, heads, rows, head_size), lambda s, c, n: (s, 0, 0, 0)),
            pl.BlockSpec((1, heads, most_new, head_size), lambda s, c, n: (s, 0, 0, 0)),
            pl.BlockSpec((1, heads, most_new, head_size), lambda s, c, n: (s, 0, 0, 0)),
            pl.BlockSpec((1, slot_length, heads, 2 * head_size), lambda s, c, n: (s, 0, 0, 0)),
        ],
        out_specs=pl.BlockSpec((1, heads, rows, head_size), lambda s, c, n: (s, 0, 0, 0)),
        scratch_shapes=[
            pltpu.VMEM((heads, slot_length, head_size), jnp.bfloat16),
            pltpu.VMEM((heads, slot_length, head_size), jnp.bfloat16),
            pltpu.VMEM((min(256, rows), slot_length), jnp.float32),
        ],
    )
    return pl.pallas_call(
        functools.partial(attention_kernel, group_size, key_block),
        grid_spec=grid_spec,
        out_shape=jax.ShapeDtypeStruct(queries.shape, jnp.bfloat16),
        compiler_params=pltpu.CompilerParams(vmem_limit_bytes=48 << 20),
    )(cached_counts, new_counts, queries, new_keys, new_values, stored)


MESH = pl.DeviceIdType.MESH


def chosen_of(index, table):
    found = jnp.int32(table[0])
    for place in range(1, len(table)):
        found = jnp.where(index == place, jnp.int32(table[place]), found)
    return found


def ring_of(count):
    across = 1
    while 4 * across * across <= count:
        across *= 2
    along = count // across
    ring = [place * across for place in range(along)]
    for turn, place in enumerate(reversed(range(along))):
        row = [place * across + step for step in range(1, across)]
        ring += row if turn % 2 == 0 else row[::-1]
    ahead = [0] * count
    behind = [0] * count
    place_of = [0] * count
    for i in range(count):
        ahead[ring[i]] = ring[(i + 1) % count]
        behind[ring[i]] = ring[(i - 1) % count]
        place_of[ring[i]] = i
    return ring, ahead, behind, place_of


def enter(req_count, kv_count):
    req = lax.axis_index("req")
    kv = lax.axis_index("kv")
    barrier = pltpu.get_barrier_semaphore()
    for step in range(1, req_count):
        pl.semaphore_signal(
            barrier, inc=1, device_id=(lax.rem(req + step, req_count), kv), device_id_type=MESH
        )
    for step in range(1, kv_count):
        pl.semaphore_signal(
            barrier, inc=1, device_id=(req, lax.rem(kv + step, kv_count)), device_id_type=MESH
        )
    pl.semaphore_wait(barrier, req_count + kv_count - 2)
    return req, kv


def column_to_row(column):
    count = column.shape[0]
    here = lax.broadcasted_iota(jnp.int32, (count, count), 0)
    there = lax.broadcasted_iota(jnp.int32, (count, count), 1)
    return jnp.sum(jnp.where(here == there, column, 0.0), axis=0, keepdims=True)


def row_to_column(row):
    count = row.shape[1]
    here = lax.broadcasted_iota(jnp.int32, (count, count), 0)
    there = lax.broadcasted_iota(jnp.int32, (count, count), 1)
    return jnp.sum(jnp.where(here == there, row, 0.0), axis=1, keepdims=True)


def partner(kv, dy, dc, ny):
    return lax.rem(kv // 2 + dy, ny) * 2 + lax.rem(kv + dc, 2)


def qkv_kernel(
    sizes,
    x_hbm,
    gain_ref,
    tok_ref,
    w_hbm,
    cos_ref,
    sin_ref,
    out_ref,
    x_all,
    w_all,
    normed,
    squares,
    squares_in,
    totals_in,
    land,
    leave,
    steps_in,
    steps_out,
    local_sem,
    square_sem,
    total_sem,
    gather_sem,
    share_sem,
    ring_sem,
    step_sem,
):
    req_count, kv_count, group_size, head_size, pieces, ahead_of, behind_of = sizes
    ny = kv_count // 2
    shard = x_hbm.shape[0]
    width = x_hbm.shape[1]
    block = out_ref.shape[0]
    w_copy = pltpu.make_async_copy(w_hbm, w_all, local_sem.at[0])
    x_copy = pltpu.make_async_copy(x_hbm, x_all.at[0], local_sem.at[1])
    x_copy.start()
    w_copy.start()
    req, kv = enter(req_count, kv_count)
    x_copy.wait()
    chunk = shard // 2

    def gather_copy(dy, part):
        rows = pl.ds(part * chunk, chunk)
        return pltpu.make_async_remote_copy(
            src_ref=x_all.at[0, rows],
            dst_ref=x_all.at[2 * dy, rows],
            send_sem=gather_sem.at[0, dy, part],
            recv_sem=gather_sem.at[1, dy, part],
            device_id=(req, partner(kv, dy, 0, ny)),
            device_id_type=MESH,
        )

    def share_copy(dy, part):
        rows = pl.ds(part * chunk, chunk)
        return pltpu.make_async_remote_copy(
            src_ref=x_all.at[2 * dy, rows],
            dst_ref=x_all.at[2 * dy + 1, rows],
            send_sem=share_sem.at[0, dy, part],
            recv_sem=share_sem.at[1, dy, part],
            device_id=(req, partner(kv, 0, 1, ny)),
            device_id_type=MESH,
        )

    def square_copy(step):
        return pltpu.make_async_remote_copy(
            src_ref=squares.at[0],
            dst_ref=squares_in.at[step],
            send_sem=square_sem.at[0, step],
            recv_sem=square_sem.at[1, step],
            device_id=(lax.rem(req + step, req_count), kv),
            device_id_type=MESH,
        )

    def total_copy(dy, dc):
        slot = 2 * dy + dc
        return pltpu.make_async_remote_copy(
            src_ref=squares.at[1],
            dst_ref=totals_in.at[slot],
            send_sem=total_sem.at[0, slot],
            recv_sem=total_sem.at[1, slot],
            device_id=(req, partner(kv, dy, dc, ny)),
            device_id_type=MESH,
        )

    for part in range(2):
        for dy in range(1, ny):
            gather_copy(dy, part).start()
    x_own = x_all[0].astype(jnp.float32)
    own = column_to_row(jnp.sum(x_own * x_own, axis=1, keepdims=True))
    squares[0] = jnp.broadcast_to(own, squares.shape[1:])
    for step in range(1, req_count):
        square_copy(step).start()
    for part in range(2):
        share_copy(0, part).start()
    total = squares[0]
    for step in range(1, req_count):
        square_copy(step).wait_recv()
        total = total + squares_in[step]
    squares[1] = total
    others = [(dy, dc) for dy in range(ny) for dc in range(2) if dy or dc]
    for dy, dc in others:
        total_copy(dy, dc).start()
    rate_rows = [None] * kv_count
    rate_rows[0] = lax.rsqrt(total[0:1] / (width * req_count) + epsilon_norm)
    for dy, dc in others:
        total_copy(dy, dc).wait_recv()
        rate_rows[2 * dy + dc] = lax.rsqrt(
            totals_in[2 * dy + dc, 0:1] / (width * req_count) + epsilon_norm
        )
    for part in range(2):
        for dy in range(1, ny):
            gather_copy(dy, part).wait_recv()
            share_copy(dy, part).start()
    for dy in range(ny):
        for part in range(2):
            share_copy(dy, part).wait_recv()
    w_copy.wait()
    rows_of_all = x_all[...].reshape(kv_count * shard, width)

    def normalise(k):
        at = pl.ds(pl.multiple_of(k * block, block), block)
        wanted = tok_ref[at, :]
        picks = []
        rate = jnp.zeros((block, 1), jnp.float32)
        for slot in range(kv_count):
            places = lax.broadcasted_iota(jnp.int32, (block, shard), 1) + slot * shard
            pick = wanted == places
            rate = rate + jnp.sum(jnp.where(pick, rate_rows[slot], 0.0), axis=1, keepdims=True)
            picks.append(jnp.where(pick, 1.0, 0.0).astype(jnp.bfloat16))
        rows = jnp.dot(
            jnp.concatenate(picks, axis=1), rows_of_all, preferred_element_type=jnp.float32
        )
        normed[at, :] = (rows * rate * gain_ref[...]).astype(jnp.bfloat16)

    def product(k, first, last):
        at = pl.ds(pl.multiple_of(k * block, block), block)
        return jnp.dot(normed[at, :], w_all[:, first:last], preferred_element_type=jnp.float32)

    targets = (chosen_of(req, ahead_of), chosen_of(req, behind_of))

    def ring_copy(step, piece):
        way, first, last = pieces[piece]
        columns = pl.ds(first, last - first)
        return pltpu.make_async_remote_copy(
            src_ref=leave.at[step, :, columns],
            dst_ref=land.at[step, :, columns],
            send_sem=ring_sem.at[0, step, piece],
            recv_sem=ring_sem.at[1, step, piece],
            device_id=(targets[way], kv),
            device_id_type=MESH,
        )

    def step_copy(step, piece):
        return pltpu.make_async_remote_copy(
            src_ref=steps_out.at[step, piece],
            dst_ref=steps_in.at[step, piece],
            send_sem=step_sem.at[0, step, piece],
            recv_sem=step_sem.at[1, step, piece],
            device_id=(targets[pieces[piece][0]], kv),
            device_id_type=MESH,
        )

    def pass_on(step, piece, value):
        way, first, last = pieces[piece]
        top = jnp.maximum(jnp.max(jnp.abs(value), axis=1, keepdims=True), 1e-30)
        steps_out[step, piece] = jnp.broadcast_to(
            column_to_row(top * (1.0 / 32767.0)), steps_out.shape[2:]
        )
        step_copy(step, piece).start()
        codes = jnp.floor(value * (32767.0 / top) + 0.5).astype(jnp.int32)
        leave[step, :, first:last] = codes.astype(jnp.int16)
        ring_copy(step, piece).start()

    def arrived(step, piece):
        way, first, last = pieces[piece]
        step_copy(step, piece).wait_recv()
        unit = row_to_column(steps_in[step, piece, 0:1])
        ring_copy(step, piece).wait_recv()
        codes = land[step, :, first:last].astype(jnp.int32)
        return codes.astype(jnp.float32) * unit

    order = sorted(range(len(pieces)), key=lambda p: p % 2)
    normalise(req_count - 1)
    normalise(1)
    for piece in range(len(pieces)):
        way, first, last = pieces[piece]
        pass_on(0, piece, product(1 if way else req_count - 1, first, last))

    def rest(k, carry):
        normalise(lax.rem(k, req_count))
        return carry

    lax.fori_loop(2, req_count - 1, rest, 0)
    normalise(0)

    def one_step(step, carry):
        for piece in order:
            way, first, last = pieces[piece]
            k = 2 + step if way else req_count - 2 - step
            added = product(k, first, last)
            pass_on(step + 1, piece, arrived(step, piece) + added)
        return carry

    lax.fori_loop(0, req_count - 2, one_step, 0)
    half = head_size // 2
    for piece in order:
        way, first, last = pieces[piece]
        added = product(0, first, last)
        summed = arrived(req_count - 2, piece) + added
        for place in range((last - first) // head_size):
            vector = summed[:, place * head_size : (place + 1) * head_size]
            start = first + place * head_size
            if (start // head_size) % (group_size + 2) <= group_size:
                vector = vector * cos_ref[...] + pltpu.roll(vector, half, 1) * sin_ref[...]
            out_ref[:, start : start + head_size] = vector.astype(jnp.bfloat16)

    for dy in range(1, ny):
        for part in range(2):
            gather_copy(dy, part).wait_send()
    for dy in range(ny):
        for part in range(2):
            share_copy(dy, part).wait_send()
    for step in range(1, req_count):
        square_copy(step).wait_send()
    for dy, dc in others:
        total_copy(dy, dc).wait_send()

    def sent(step, carry):
        for piece in range(len(pieces)):
            ring_copy(step, piece).wait_send()
            step_copy(step, piece).wait_send()
        return carry

    lax.fori_loop(0, req_count - 1, sent, 0)


def qkv_call(x, gain, tok, weight, cosine, sine, group_size, head_size):
    req_count = lax.axis_size("req")
    kv_count = lax.axis_size("kv")
    ring, ahead_of, behind_of, place_of = ring_of(req_count)
    shard, width = x.shape
    columns = weight.shape[1]
    block = shard * kv_count // req_count
    vectors = columns // head_size
    half = vectors // 2
    pieces = []
    for way in range(2):
        middle = way * half + (half + 1) // 2
        pieces.append((way, way * half * head_size, middle * head_size))
        pieces.append((way, middle * head_size, (way + 1) * half * head_size))
    sizes = (req_count, kv_count, group_size, head_size, pieces, ahead_of, behind_of)
    vmem = pl.BlockSpec(memory_space=pltpu.VMEM)
    anywhere = pl.BlockSpec(memory_space=pl.ANY)
    dma = pltpu.SemaphoreType.DMA
    return pl.pallas_call(
        functools.partial(qkv_kernel, sizes),
        out_shape=jax.ShapeDtypeStruct((block, columns), jnp.bfloat16),
        in_specs=[anywhere, vmem, vmem, anywhere, vmem, vmem],
        out_specs=vmem,
        scratch_shapes=[
            pltpu.VMEM((kv_count, shard, width), jnp.bfloat16),
            pltpu.VMEM((width, columns), jnp.bfloat16),
            pltpu.VMEM((kv_count * shard, width), jnp.bfloat16),
            pltpu.VMEM((2, 8, shard), jnp.float32),
            pltpu.VMEM((req_count, 8, shard), jnp.float32),
            pltpu.VMEM((kv_count, 8, shard), jnp.float32),
            pltpu.VMEM((req_count - 1, block, columns), jnp.int16),
            pltpu.VMEM((req_count - 1, block, columns), jnp.int16),
            pltpu.VMEM((req_count - 1, len(pieces), 8, block), jnp.float32),
            pltpu.VMEM((req_count - 1, len(pieces), 8, block), jnp.float32),
            dma((2,)),
            dma((2, req_count)),
            dma((2, kv_count)),
            dma((2, kv_count // 2, 2)),
            dma((2, kv_count // 2, 2)),
            dma((2, req_count - 1, len(pieces))),
            dma((2, req_count - 1, len(pieces))),
        ],
        compiler_params=pltpu.CompilerParams(
            collective_id=0, has_side_effects=True, vmem_limit_bytes=56 << 20
        ),
    )(x, gain, tok, weight, cosine, sine)


def out_kernel(
    sizes,
    att_hbm,
    w_hbm,
    x_ref,
    gain_ref,
    row_ref,
    projected_ref,
    normed_ref,
    att,
    w_all,
    products,
    mine,
    lent,
    borrowed,
    crossing,
    crossed,
    squares,
    squares_in,
    local_sem,
    ring_sem,
    lend_sem,
    cross_sem,
    square_sem,
):
    req_count, kv_count, ahead_of, behind_of = sizes
    ny = kv_count // 2
    block = att_hbm.shape[0]
    inner = att_hbm.shape[1]
    shard, width = x_ref.shape
    att_copy = pltpu.make_async_copy(att_hbm, att.at[0], local_sem.at[0])
    w_copy = pltpu.make_async_copy(w_hbm, w_all, local_sem.at[1])
    att_copy.start()
    w_copy.start()
    req, kv = enter(req_count, kv_count)
    att_copy.wait()
    targets = (chosen_of(req, ahead_of), chosen_of(req, behind_of))
    half_way = req_count // 2
    wide = inner // 2

    def ring_copy(step, way, part):
        source = (lax.rem(req_count - step + 1, req_count), step - 1)[way]
        target = (req_count - step, step)[way]
        columns = pl.ds(part * wide, wide)
        return pltpu.make_async_remote_copy(
            src_ref=att.at[source, :, columns],
            dst_ref=att.at[target, :, columns],
            send_sem=ring_sem.at[0, step, way, part],
            recv_sem=ring_sem.at[1, step, way, part],
            device_id=(targets[way], kv),
            device_id_type=MESH,
        )

    def multiply(k):
        at = pl.ds(k * block, block)
        products[at, :] = jnp.dot(
            att[k], w_all[...], preferred_element_type=jnp.float32
        ).astype(jnp.bfloat16)

    for part in range(2):
        for way in range(2):
            if half_way > 1 or part == way:
                ring_copy(1, way, part).start()
    w_copy.wait()
    multiply(0)
    for step in range(1, half_way):
        for part in range(2):
            for way in range(2):
                ring_copy(step, way, part).wait_recv()
                if step + 1 < half_way or part == way:
                    ring_copy(step + 1, way, part).start()
        multiply(req_count - step)
        multiply(step)
    for way in range(2):
        ring_copy(half_way, way, way).wait_recv()
    multiply(half_way)

    rows_total = req_count * block

    def gathered(dy, dc, part):
        count = shard // 2
        wanted = row_ref[2 * dy + dc, part * count : (part + 1) * count, :]
        places = lax.broadcasted_iota(jnp.int32, (count, rows_total), 1)
        pick = jnp.where(wanted == places, 1.0, 0.0).astype(jnp.bfloat16)
        return jnp.dot(pick, products[...], preferred_element_type=jnp.float32)

    def lend_copy(dy, part):
        count = shard // 2
        rows = pl.ds(part * count, count)
        return pltpu.make_async_remote_copy(
            src_ref=lent.at[dy, rows],
            dst_ref=borrowed.at[dy, rows],
            send_sem=lend_sem.at[0, dy, part],
            recv_sem=lend_sem.at[1, dy, part],
            device_id=(req, partner(kv, 0, 1, ny)),
            device_id_type=MESH,
        )

    def cross_copy(dy, part):
        count = shard // 2
        rows = pl.ds(part * count, count)
        return pltpu.make_async_remote_copy(
            src_ref=crossing.at[dy, rows],
            dst_ref=crossed.at[dy, rows],
            send_sem=cross_sem.at[0, dy, part],
            recv_sem=cross_sem.at[1, dy, part],
            device_id=(req, partner(kv, dy, 0, ny)),
            device_id_type=MESH,
        )

    def part_rows(part):
        return slice(part * (shard // 2), (part + 1) * (shard // 2))

    turns = [(dy, part) for dy in list(range(1, ny)) + [0] for part in range(2)]
    for dy, part in turns:
        lent[dy, part_rows(part)] = gathered(dy, 1, part).astype(jnp.bfloat16)
        lend_copy(dy, part).start()
        if dy:
            own = gathered(dy, 0, part)
            lend_copy(dy, part).wait_recv()
            crossing[dy, part_rows(part)] = (
                own + borrowed[dy, part_rows(part)].astype(jnp.float32)
            ).astype(jnp.bfloat16)
            cross_copy(dy, part).start()
    for part in range(2):
        mine[part_rows(part)] = gathered(0, 0, part)
    sums = []
    for part in range(2):
        lend_copy(0, part).wait_recv()
        projection = mine[part_rows(part)] + borrowed[0, part_rows(part)].astype(jnp.float32)
        for dy in range(1, ny):
            cross_copy(dy, part).wait_recv()
            projection = projection + crossed[dy, part_rows(part)].astype(jnp.float32)
        projected_ref[part_rows(part)] = projection.astype(jnp.bfloat16)
        residual = x_ref[part_rows(part)].astype(jnp.float32) + projection
        mine[part_rows(part)] = residual
        sums.append(column_to_row(jnp.sum(residual * residual, axis=1, keepdims=True)))
    squares[...] = jnp.broadcast_to(jnp.concatenate(sums, axis=1), squares.shape)

    def square_copy(step):
        return pltpu.make_async_remote_copy(
            src_ref=squares,
            dst_ref=squares_in.at[step],
            send_sem=square_sem.at[0, step],
            recv_sem=square_sem.at[1, step],
            device_id=(lax.rem(req + step, req_count), kv),
            device_id_type=MESH,
        )

    for step in range(1, req_count):
        square_copy(step).start()
    total = squares[...]
    for step in range(1, req_count):
        square_copy(step).wait_recv()
        total = total + squares_in[step]
    rate = row_to_column(lax.rsqrt(total[0:1] / (width * req_count) + epsilon_norm))
    normed_ref[...] = (mine[...] * rate * gain_ref[...]).astype(jnp.bfloat16)

    for step in range(1, half_way + 1):
        for part in range(2):
            for way in range(2):
                if step < half_way or part == way:
                    ring_copy(step, way, part).wait_send()
    for dy, part in turns:
        lend_copy(dy, part).wait_send()
        if dy:
            cross_copy(dy, part).wait_send()
    for step in range(1, req_count):
        square_copy(step).wait_send()


def out_call(attention, weight, x, gain, rows):
    req_count = lax.axis_size("req")
    kv_count = lax.axis_size("kv")
    ring, ahead_of, behind_of, place_of = ring_of(req_count)
    block, inner = attention.shape
    shard, width = x.shape
    ny = kv_count // 2
    vmem = pl.BlockSpec(memory_space=pltpu.VMEM)
    anywhere = pl.BlockSpec(memory_space=pl.ANY)
    dma = pltpu.SemaphoreType.DMA
    made = jax.ShapeDtypeStruct((shard, width), jnp.bfloat16)
    return pl.pallas_call(
        functools.partial(out_kernel, (req_count, kv_count, ahead_of, behind_of)),
        out_shape=(made, made),
        in_specs=[anywhere, anywhere, vmem, vmem, vmem],
        out_specs=(vmem, vmem),
        scratch_shapes=[
            pltpu.VMEM((req_count, block, inner), jnp.bfloat16),
            pltpu.VMEM((inner, width), jnp.bfloat16),
            pltpu.VMEM((req_count * block, width), jnp.bfloat16),
            pltpu.VMEM((shard, width), jnp.float32),
            pltpu.VMEM((ny, shard, width), jnp.bfloat16),
            pltpu.VMEM((ny, shard, width), jnp.bfloat16),
            pltpu.VMEM((ny, shard, width), jnp.bfloat16),
            pltpu.VMEM((ny, shard, width), jnp.bfloat16),
            pltpu.VMEM((8, shard), jnp.float32),
            pltpu.VMEM((req_count, 8, shard), jnp.float32),
            dma((2,)),
            dma((2, req_count // 2 + 1, 2, 2)),
            dma((2, ny, 2)),
            dma((2, ny, 2)),
            dma((2, req_count)),
        ],
        compiler_params=pltpu.CompilerParams(
            collective_id=1, has_side_effects=True, vmem_limit_bytes=56 << 20
        ),
    )(attention, weight, x, gain, rows)


def per_device(
    activations,
    input_gain,
    qkv_weight,
    out_weight,
    post_gain,
    cache_entries,
    new_lengths,
    cache_lengths,
    request_slot,
):
    req_count = lax.axis_size("req")
    kv_count = lax.axis_size("kv")
    shard, width_slice = activations.shape
    token_count = shard * kv_count
    tok_blk = token_count // req_count
    query_rows = tok_blk * 3 // 4
    kvh_local = qkv_weight.shape[1]
    head_size = cache_entries.shape[3] // 2
    group_size = qkv_weight.shape[2] // head_size - 2
    per_block = cache_entries.shape[0]
    ny = kv_count // 2
    block_id = lax.axis_index("req")
    kv_id = lax.axis_index("kv")
    ring, ahead_of, behind_of, place_of = ring_of(req_count)
    place_here = chosen_of(block_id, place_of)
    token_of_row, row_of_token, pos_of_row, slot_of_row, offset_row = layout(
        new_lengths, cache_lengths, request_slot, tok_blk
    )
    ring_array = jnp.asarray(ring, jnp.int32)
    ring_places = lax.rem(place_here + jnp.arange(req_count, dtype=jnp.int32), req_count)
    ring_blocks = jnp.sum(
        jnp.where(ring_places[:, None] == jnp.arange(req_count)[None, :], ring_array[None, :], 0),
        axis=1,
    )
    ring_pick = (ring_blocks[:, None] == jnp.arange(req_count)[None, :]).astype(jnp.int32)
    ring_tokens = jnp.sum(
        ring_pick[:, :, None] * token_of_row.reshape(req_count, tok_blk)[None], axis=1
    ).reshape(-1)
    owner = ring_tokens // shard
    dy = lax.rem(kv_id // 2 - owner // 2 + ny, ny)
    dc = lax.rem(kv_id + owner, 2)
    tok = ((2 * dy + dc) * shard + lax.rem(ring_tokens, shard)).reshape(-1, 1)
    first_row = block_id * tok_blk
    my_positions = lax.dynamic_slice_in_dim(pos_of_row, first_row, tok_blk, 0)
    half_size = head_size // 2
    frequency = jnp.exp(
        -(jnp.arange(half_size, dtype=jnp.float32) * (2.0 / head_size)) * math.log(rope_base)
    )
    angles = my_positions.astype(jnp.float32)[:, None] * frequency[None, :]
    cosine = jnp.cos(angles)
    sine = jnp.sin(angles)
    rotated = qkv_call(
        activations,
        input_gain.astype(jnp.float32).reshape(1, -1),
        tok,
        qkv_weight.reshape(width_slice, -1),
        jnp.concatenate([cosine, cosine], axis=1),
        jnp.concatenate([-sine, sine], axis=1),
        group_size,
        head_size,
    )
    rotated_heads = rotated.reshape(tok_blk, kvh_local, group_size + 2, head_size)
    appended = rotated_heads[:, :, group_size:, :].reshape(tok_blk, kvh_local, 2 * head_size)
    attention = attend(
        rotated_heads, cache_entries, new_lengths, cache_lengths, slot_of_row, offset_row, query_rows, group_size
    )
    place_array = jnp.asarray(place_of, jnp.int32)
    block_of_token = row_of_token // tok_blk
    place_of_token = jnp.sum(
        jnp.where(
            block_of_token[:, None] == jnp.arange(req_count)[None, :], place_array[None, :], 0
        ),
        axis=1,
    )
    ring_row = lax.rem(place_of_token - place_here + req_count, req_count) * tok_blk + lax.rem(
        row_of_token, tok_blk
    )
    owners = jnp.stack(
        [partner(kv_id, dy, dc, ny) for dy in range(ny) for dc in range(2)]
    )
    owner_pick = (owners[:, None] == jnp.arange(kv_count)[None, :]).astype(jnp.int32)
    rows = jnp.sum(
        owner_pick[:, :, None] * ring_row.reshape(kv_count, shard)[None], axis=1
    ).reshape(kv_count, shard, 1)
    projected, normed = out_call(
        attention,
        out_weight.reshape(-1, width_slice),
        activations,
        post_gain.astype(jnp.float32).reshape(1, -1),
        rows,
    )
    return (projected, normed, appended)


def attend(rotated_heads, cache_entries, new_lengths, cache_lengths, slot_of_row, offset_row, query_rows, group_size):
    tok_blk, kvh_local, vectors, head_size = rotated_heads.shape
    per_block = cache_entries.shape[0]
    block_id = lax.axis_index("req")
    new_counts = lax.dynamic_index_in_dim(new_lengths, block_id, 0, keepdims=False)
    cached_counts = lax.dynamic_index_in_dim(cache_lengths, block_id, 0, keepdims=False)
    starts = sums_before(new_counts[None])[0]
    picked = jnp.minimum(
        starts[:, None] + jnp.arange(query_rows, dtype=jnp.int32)[None, :], tok_blk - 1
    ).reshape(-1)
    slot_rows = jnp.take(rotated_heads.reshape(tok_blk, -1), picked, axis=0, mode="clip").reshape(
        per_block, query_rows, kvh_local, group_size + 2, head_size
    )
    queries = jnp.transpose(slot_rows[:, :, :, :group_size], (0, 2, 1, 3, 4)).reshape(
        per_block, kvh_local, query_rows * group_size, head_size
    )
    stacked = block_attention(
        queries,
        jnp.transpose(slot_rows[:, :, :, group_size], (0, 2, 1, 3)),
        jnp.transpose(slot_rows[:, :, :, group_size + 1], (0, 2, 1, 3)),
        cache_entries,
        cached_counts,
        new_counts,
        group_size,
    )
    stacked = jnp.transpose(
        stacked.reshape(per_block, kvh_local, query_rows, -1), (0, 2, 1, 3)
    ).reshape(per_block * query_rows, -1)
    first_row = block_id * tok_blk
    local_slot = lax.dynamic_slice_in_dim(slot_of_row, first_row, tok_blk, 0) - block_id * per_block
    local_offset = lax.dynamic_slice_in_dim(offset_row, first_row, tok_blk, 0)
    return jnp.take(stacked, local_slot * query_rows + local_offset, axis=0, mode="clip")


def solution(mesh):
    in_specs = (
        P("kv", "req"),
        P("req"),
        P("req", "kv", None),
        P("kv", None, "req"),
        P("req"),
        P("req", None, "kv", None),
        P(),
        P(),
        P(),
    )
    out_specs = (P("kv", "req"), P("kv", "req"), P("req", "kv", None))
    return jax.shard_map(
        per_device, mesh=mesh, in_specs=in_specs, out_specs=out_specs, check_vma=False
    )
```

```python
import functools
import math

import jax
import jax.numpy as jnp
from jax import lax
from jax.experimental import pallas as pl
from jax.experimental.pallas import tpu as pltpu
from jax.sharding import PartitionSpec as P

epsilon_norm = 1e-05
rope_base = 500000.0


def sums_before(values):
    count = values.shape[1]
    earlier = jnp.arange(count)[:, None] < jnp.arange(count)[None, :]
    return jnp.sum(jnp.where(earlier[None], values[:, :, None], 0), axis=1)


def layout(new_lengths, cache_lengths, request_slot, block_tokens):
    blocks, per_block = new_lengths.shape
    request_total = blocks * per_block
    token_total = blocks * block_tokens
    slot_ids = jnp.arange(request_total, dtype=jnp.int32)
    new_flat = new_lengths.reshape(request_total)
    cache_flat = cache_lengths.reshape(request_total)
    chosen = (request_slot[:, None] == slot_ids[None, :]).astype(jnp.int32)
    arrival_len = jnp.sum(chosen * new_flat[None, :], axis=1)
    arrival_start = sums_before(arrival_len[None])[0]
    inside = sums_before(new_lengths)
    slot_start = (inside + block_tokens * jnp.arange(blocks, dtype=jnp.int32)[:, None]).reshape(
        request_total
    )
    slot_arrival_start = jnp.sum(chosen * arrival_start[:, None], axis=0)
    positions = jnp.arange(token_total, dtype=jnp.int32)
    slot_of_row = jnp.sum((slot_start[None, :] <= positions[:, None]).astype(jnp.int32), axis=1) - 1
    row_pick = (slot_of_row[:, None] == slot_ids[None, :]).astype(jnp.int32)
    offset_row = positions - jnp.sum(row_pick * slot_start[None, :], axis=1)
    token_of_row = jnp.sum(row_pick * slot_arrival_start[None, :], axis=1) + offset_row
    pos_of_row = jnp.sum(row_pick * cache_flat[None, :], axis=1) + offset_row
    arrival_of_token = (
        jnp.sum((arrival_start[None, :] <= positions[:, None]).astype(jnp.int32), axis=1) - 1
    )
    token_pick = (arrival_of_token[:, None] == slot_ids[None, :]).astype(jnp.int32)
    slot_of_token = jnp.sum(token_pick * request_slot[None, :], axis=1)
    offset_token = positions - jnp.sum(token_pick * arrival_start[None, :], axis=1)
    token_slot_pick = (slot_of_token[:, None] == slot_ids[None, :]).astype(jnp.int32)
    row_of_token = jnp.sum(token_slot_pick * slot_start[None, :], axis=1) + offset_token
    return (token_of_row, row_of_token, pos_of_row)


def attention_kernel(
    group_size, key_block, starts_ref, cached_ref, rotated_ref, stored_hbm, out_ref,
    raw, staged, keys, values, scores, copy_sem,
):
    slots = stored_hbm.shape[0]
    heads = keys.shape[0]
    block = rotated_ref.shape[0]
    head_size = keys.shape[2]
    stride = 2 * heads
    tokens = min(32, block)
    rows = tokens * group_size
    small = key_block // 2
    scale = math.log2(math.e) / math.sqrt(head_size)
    span = (group_size + 2) * head_size
    contract_last = (((1,), (1,)), ((), ()))

    def load(slot, index):
        at = pl.ds(pl.multiple_of(index * key_block * stride, key_block * stride), key_block * stride)
        return pltpu.make_async_copy(
            stored_hbm.at[slot, at], raw.at[slot, at], copy_sem.at[slot, index]
        )

    def blocks_of(slot):
        return (cached_ref[slot] + key_block - 1) // key_block

    def begin(slot, carry):
        def one(index, inner):
            load(slot, index).start()
            return inner

        return lax.fori_loop(0, blocks_of(slot), one, carry)

    lax.fori_loop(0, slots, begin, 0)

    def lane_fold(op, value):
        folded = value[:, :head_size]
        for part in range(1, value.shape[1] // head_size):
            folded = op(folded, value[:, part * head_size : (part + 1) * head_size])
        return folded

    def one_slot(slot, carry):
        start, end = starts_ref[slot], starts_ref[slot + 1]
        cached = cached_ref[slot]

        def split(index, inner):
            load(slot, index).wait()
            base = pl.multiple_of(index * key_block, key_block)
            staged[...] = raw[
                slot, pl.ds(pl.multiple_of(base * stride, key_block * stride), key_block * stride), :
            ].astype(jnp.float32)
            for head in range(heads):
                keys[head, pl.ds(base, key_block), :] = staged[
                    pl.ds(head, key_block, stride=stride), :
                ].astype(jnp.bfloat16)
                values[head, pl.ds(base, key_block), :] = staged[
                    pl.ds(heads + head, key_block, stride=stride), :
                ].astype(jnp.bfloat16)
            return inner

        lax.fori_loop(0, blocks_of(slot), split, 0)
        whole = cached // key_block
        first_part = whole * (key_block // small)
        last_part = (cached + small - 1) // small

        def one_chunk(chunk, inner):
            at = pl.ds(pl.multiple_of(chunk * tokens, tokens), tokens)
            token = chunk * tokens + lax.rem(
                lax.broadcasted_iota(jnp.int32, (rows, block), 0), tokens
            )
            other = lax.broadcasted_iota(jnp.int32, (rows, block), 1)
            allowed = (other <= token) & (other >= start)
            queries, owns = [], []
            for head in range(heads):
                query = jnp.concatenate(
                    [
                        rotated_ref[at, head * span + g * head_size : head * span + (g + 1) * head_size]
                        for g in range(group_size)
                    ],
                    axis=0,
                )
                new_key = rotated_ref[:, head * span + group_size * head_size : head * span + (group_size + 1) * head_size]
                own = lax.dot_general(
                    query, new_key, contract_last, preferred_element_type=jnp.float32
                )
                queries.append(query)
                owns.append(jnp.where(allowed, own, -jnp.inf))

            def score(head, first, width):
                return lax.dot_general(
                    queries[head],
                    keys[head, pl.ds(first, width), :],
                    contract_last,
                    preferred_element_type=jnp.float32,
                )

            def fill(index, highest):
                first = pl.multiple_of(index * key_block, key_block)
                found = [score(head, first, key_block) for head in range(heads)]
                for head in range(heads):
                    scores[head, :, pl.ds(first, key_block)] = found[head]
                return tuple(
                    jnp.maximum(highest[head], lane_fold(jnp.maximum, found[head]))
                    for head in range(heads)
                )

            def fill_part(index, highest):
                first = pl.multiple_of(index * small, small)
                places = lax.broadcasted_iota(jnp.int32, (rows, small), 1)
                found = [
                    jnp.where(places < cached - first, score(head, first, small), -jnp.inf)
                    for head in range(heads)
                ]
                for head in range(heads):
                    scores[head, :, pl.ds(first, small)] = found[head]
                return tuple(
                    jnp.maximum(highest[head], lane_fold(jnp.maximum, found[head]))
                    for head in range(heads)
                )

            highest = tuple(lane_fold(jnp.maximum, owns[head]) for head in range(heads))
            highest = lax.fori_loop(0, whole, fill, highest)
            highest = lax.fori_loop(first_part, last_part, fill_part, highest)
            tops = [jnp.max(highest[head], axis=1, keepdims=True) for head in range(heads)]
            state = []
            for head in range(heads):
                weights = jnp.exp2((owns[head] - tops[head]) * scale)
                new_value = rotated_ref[:, head * span + (group_size + 1) * head_size : (head + 1) * span]
                state.append(lane_fold(jnp.add, weights))
                state.append(
                    jnp.dot(
                        weights.astype(jnp.bfloat16), new_value, preferred_element_type=jnp.float32
                    )
                )

            def accumulate(width):
                def body(index, state):
                    first = pl.multiple_of(index * width, width)
                    result = []
                    for head in range(heads):
                        weights = jnp.exp2(
                            (scores[head, :, pl.ds(first, width)] - tops[head]) * scale
                        )
                        added = jnp.dot(
                            weights.astype(jnp.bfloat16),
                            values[head, pl.ds(first, width), :],
                            preferred_element_type=jnp.float32,
                        )
                        result.append(state[2 * head] + lane_fold(jnp.add, weights))
                        result.append(state[2 * head + 1] + added)
                    return tuple(result)

                return body

            state = lax.fori_loop(0, whole, accumulate(key_block), tuple(state))
            state = lax.fori_loop(first_part, last_part, accumulate(small), state)
            member_token = chunk * tokens + lax.broadcasted_iota(jnp.int32, (tokens, head_size), 0)
            member = (member_token >= start) & (member_token < end)
            for head in range(heads):
                total = jnp.sum(state[2 * head], axis=1, keepdims=True)
                made = state[2 * head + 1] / total
                for g in range(group_size):
                    columns = slice(
                        (head * group_size + g) * head_size, (head * group_size + g + 1) * head_size
                    )
                    old = out_ref[at, columns].astype(jnp.float32)
                    out_ref[at, columns] = jnp.where(
                        member, made[g * tokens : (g + 1) * tokens], old
                    ).astype(jnp.bfloat16)
            return inner

        return lax.fori_loop(start // tokens, (end + tokens - 1) // tokens, one_chunk, carry)

    lax.fori_loop(0, slots, one_slot, 0)


def block_attention(rotated, cache_entries, starts, cached_counts, group_size):
    slots, slot_length, heads, both = cache_entries.shape
    head_size = both // 2
    block = rotated.shape[0]
    key_block = min(512, slot_length)
    stored = jnp.transpose(
        cache_entries.reshape(slots, slot_length, heads, 2, head_size), (0, 1, 3, 2, 4)
    ).reshape(slots, slot_length * 2 * heads, head_size)
    rows = min(32, block) * group_size
    grid_spec = pltpu.PrefetchScalarGridSpec(
        num_scalar_prefetch=2,
        grid=(1,),
        in_specs=[
            pl.BlockSpec(rotated.shape, lambda i, s, c: (0, 0)),
            pl.BlockSpec(memory_space=pl.ANY),
        ],
        out_specs=pl.BlockSpec((block, heads * group_size * head_size), lambda i, s, c: (0, 0)),
        scratch_shapes=[
            pltpu.VMEM((slots, slot_length * 2 * heads, head_size), jnp.bfloat16),
            pltpu.VMEM((key_block * 2 * heads, head_size), jnp.float32),
            pltpu.VMEM((heads, slot_length, head_size), jnp.bfloat16),
            pltpu.VMEM((heads, slot_length, head_size), jnp.bfloat16),
            pltpu.VMEM((heads, rows, slot_length), jnp.float32),
            pltpu.SemaphoreType.DMA((slots, slot_length // key_block)),
        ],
    )
    return pl.pallas_call(
        functools.partial(attention_kernel, group_size, key_block),
        grid_spec=grid_spec,
        out_shape=jax.ShapeDtypeStruct((block, heads * group_size * head_size), jnp.bfloat16),
        compiler_params=pltpu.CompilerParams(vmem_limit_bytes=56 << 20),
    )(starts, cached_counts, rotated, stored)


MESH = pl.DeviceIdType.MESH


def chosen_of(index, table):
    found = jnp.int32(table[0])
    for place in range(1, len(table)):
        found = jnp.where(index == place, jnp.int32(table[place]), found)
    return found


def ring_of(count):
    across = 1
    while 4 * across * across <= count:
        across *= 2
    along = count // across
    ring = [place * across for place in range(along)]
    for turn, place in enumerate(reversed(range(along))):
        row = [place * across + step for step in range(1, across)]
        ring += row if turn % 2 == 0 else row[::-1]
    ahead = [0] * count
    behind = [0] * count
    place_of = [0] * count
    for i in range(count):
        ahead[ring[i]] = ring[(i + 1) % count]
        behind[ring[i]] = ring[(i - 1) % count]
        place_of[ring[i]] = i
    return ring, ahead, behind, place_of


def enter(req_count, kv_count):
    req = lax.axis_index("req")
    kv = lax.axis_index("kv")
    barrier = pltpu.get_barrier_semaphore()
    for step in range(1, req_count):
        pl.semaphore_signal(
            barrier, inc=1, device_id=(lax.rem(req + step, req_count), kv), device_id_type=MESH
        )
    for step in range(1, kv_count):
        pl.semaphore_signal(
            barrier, inc=1, device_id=(req, lax.rem(kv + step, kv_count)), device_id_type=MESH
        )
    pl.semaphore_wait(barrier, req_count + kv_count - 2)
    return req, kv


def column_to_row(column):
    count = column.shape[0]
    here = lax.broadcasted_iota(jnp.int32, (count, count), 0)
    there = lax.broadcasted_iota(jnp.int32, (count, count), 1)
    return jnp.sum(jnp.where(here == there, column, 0.0), axis=0, keepdims=True)


def row_to_column(row):
    count = row.shape[1]
    here = lax.broadcasted_iota(jnp.int32, (count, count), 0)
    there = lax.broadcasted_iota(jnp.int32, (count, count), 1)
    return jnp.sum(jnp.where(here == there, row, 0.0), axis=1, keepdims=True)


def partner(kv, dy, dc, ny):
    return lax.rem(kv // 2 + dy, ny) * 2 + lax.rem(kv + dc, 2)


def qkv_kernel(
    sizes,
    x_hbm,
    gain_ref,
    tok_ref,
    w_hbm,
    cos_ref,
    sin_ref,
    out_ref,
    x_all,
    w_all,
    normed,
    squares,
    squares_in,
    totals_in,
    land,
    leave,
    steps_in,
    steps_out,
    local_sem,
    square_sem,
    total_sem,
    gather_sem,
    share_sem,
    ring_sem,
    step_sem,
):
    req_count, kv_count, group_size, head_size, pieces, ahead_of, behind_of = sizes
    ny = kv_count // 2
    shard = x_hbm.shape[0]
    width = x_hbm.shape[1]
    block = out_ref.shape[0]
    w_copy = pltpu.make_async_copy(w_hbm, w_all, local_sem.at[0])
    x_copy = pltpu.make_async_copy(x_hbm, x_all.at[0], local_sem.at[1])
    x_copy.start()
    w_copy.start()
    req, kv = enter(req_count, kv_count)
    x_copy.wait()
    chunk = shard // 2

    def gather_copy(dy, part):
        rows = pl.ds(part * chunk, chunk)
        return pltpu.make_async_remote_copy(
            src_ref=x_all.at[0, rows],
            dst_ref=x_all.at[2 * dy, rows],
            send_sem=gather_sem.at[0, dy, part],
            recv_sem=gather_sem.at[1, dy, part],
            device_id=(req, partner(kv, dy, 0, ny)),
            device_id_type=MESH,
        )

    def share_copy(dy, part):
        rows = pl.ds(part * chunk, chunk)
        return pltpu.make_async_remote_copy(
            src_ref=x_all.at[2 * dy, rows],
            dst_ref=x_all.at[2 * dy + 1, rows],
            send_sem=share_sem.at[0, dy, part],
            recv_sem=share_sem.at[1, dy, part],
            device_id=(req, partner(kv, 0, 1, ny)),
            device_id_type=MESH,
        )

    def square_copy(step):
        return pltpu.make_async_remote_copy(
            src_ref=squares.at[0],
            dst_ref=squares_in.at[step],
            send_sem=square_sem.at[0, step],
            recv_sem=square_sem.at[1, step],
            device_id=(lax.rem(req + step, req_count), kv),
            device_id_type=MESH,
        )

    def total_copy(dy, dc):
        slot = 2 * dy + dc
        return pltpu.make_async_remote_copy(
            src_ref=squares.at[1],
            dst_ref=totals_in.at[slot],
            send_sem=total_sem.at[0, slot],
            recv_sem=total_sem.at[1, slot],
            device_id=(req, partner(kv, dy, dc, ny)),
            device_id_type=MESH,
        )

    for part in range(2):
        for dy in range(1, ny):
            gather_copy(dy, part).start()
    x_own = x_all[0].astype(jnp.float32)
    own = column_to_row(jnp.sum(x_own * x_own, axis=1, keepdims=True))
    squares[0] = jnp.broadcast_to(own, squares.shape[1:])
    for step in range(1, req_count):
        square_copy(step).start()
    for part in range(2):
        share_copy(0, part).start()
    total = squares[0]
    for step in range(1, req_count):
        square_copy(step).wait_recv()
        total = total + squares_in[step]
    squares[1] = total
    others = [(dy, dc) for dy in range(ny) for dc in range(2) if dy or dc]
    for dy, dc in others:
        total_copy(dy, dc).start()
    rate_rows = [None] * kv_count
    rate_rows[0] = lax.rsqrt(total[0:1] / (width * req_count) + epsilon_norm)
    for dy, dc in others:
        total_copy(dy, dc).wait_recv()
        rate_rows[2 * dy + dc] = lax.rsqrt(
            totals_in[2 * dy + dc, 0:1] / (width * req_count) + epsilon_norm
        )
    for part in range(2):
        for dy in range(1, ny):
            gather_copy(dy, part).wait_recv()
            share_copy(dy, part).start()
    for dy in range(ny):
        for part in range(2):
            share_copy(dy, part).wait_recv()
    w_copy.wait()
    rows_of_all = x_all[...].reshape(kv_count * shard, width)

    def normalise(k):
        at = pl.ds(pl.multiple_of(k * block, block), block)
        wanted = tok_ref[at, :]
        picks = []
        rate = jnp.zeros((block, 1), jnp.float32)
        for slot in range(kv_count):
            places = lax.broadcasted_iota(jnp.int32, (block, shard), 1) + slot * shard
            pick = wanted == places
            rate = rate + jnp.sum(jnp.where(pick, rate_rows[slot], 0.0), axis=1, keepdims=True)
            picks.append(jnp.where(pick, 1.0, 0.0).astype(jnp.bfloat16))
        rows = jnp.dot(
            jnp.concatenate(picks, axis=1), rows_of_all, preferred_element_type=jnp.float32
        )
        normed[at, :] = (rows * rate * gain_ref[...]).astype(jnp.bfloat16)

    def product(k, first, last):
        at = pl.ds(pl.multiple_of(k * block, block), block)
        return jnp.dot(normed[at, :], w_all[:, first:last], preferred_element_type=jnp.float32)

    targets = (chosen_of(req, ahead_of), chosen_of(req, behind_of))

    def ring_copy(step, piece):
        way, first, last = pieces[piece]
        columns = pl.ds(first, last - first)
        return pltpu.make_async_remote_copy(
            src_ref=leave.at[step, :, columns],
            dst_ref=land.at[step, :, columns],
            send_sem=ring_sem.at[0, step, piece],
            recv_sem=ring_sem.at[1, step, piece],
            device_id=(targets[way], kv),
            device_id_type=MESH,
        )

    def step_copy(step, piece):
        return pltpu.make_async_remote_copy(
            src_ref=steps_out.at[step, piece],
            dst_ref=steps_in.at[step, piece],
            send_sem=step_sem.at[0, step, piece],
            recv_sem=step_sem.at[1, step, piece],
            device_id=(targets[pieces[piece][0]], kv),
            device_id_type=MESH,
        )

    def pass_on(step, piece, value):
        way, first, last = pieces[piece]
        top = jnp.maximum(jnp.max(jnp.abs(value), axis=1, keepdims=True), 1e-30)
        steps_out[step, piece] = jnp.broadcast_to(
            column_to_row(top * (1.0 / 32767.0)), steps_out.shape[2:]
        )
        step_copy(step, piece).start()
        codes = jnp.floor(value * (32767.0 / top) + 0.5).astype(jnp.int32)
        leave[step, :, first:last] = codes.astype(jnp.int16)
        ring_copy(step, piece).start()

    def arrived(step, piece):
        way, first, last = pieces[piece]
        step_copy(step, piece).wait_recv()
        unit = row_to_column(steps_in[step, piece, 0:1])
        ring_copy(step, piece).wait_recv()
        codes = land[step, :, first:last].astype(jnp.int32)
        return codes.astype(jnp.float32) * unit

    order = sorted(range(len(pieces)), key=lambda p: p % 2)
    normalise(req_count - 1)
    normalise(1)
    for piece in range(len(pieces)):
        way, first, last = pieces[piece]
        pass_on(0, piece, product(1 if way else req_count - 1, first, last))

    def rest(k, carry):
        normalise(lax.rem(k, req_count))
        return carry

    lax.fori_loop(2, req_count - 1, rest, 0)
    normalise(0)

    def one_step(step, carry):
        for piece in order:
            way, first, last = pieces[piece]
            k = 2 + step if way else req_count - 2 - step
            added = product(k, first, last)
            pass_on(step + 1, piece, arrived(step, piece) + added)
        return carry

    lax.fori_loop(0, req_count - 2, one_step, 0)
    half = head_size // 2
    for piece in order:
        way, first, last = pieces[piece]
        added = product(0, first, last)
        summed = arrived(req_count - 2, piece) + added
        for place in range((last - first) // head_size):
            vector = summed[:, place * head_size : (place + 1) * head_size]
            start = first + place * head_size
            if (start // head_size) % (group_size + 2) <= group_size:
                vector = vector * cos_ref[...] + pltpu.roll(vector, half, 1) * sin_ref[...]
            out_ref[:, start : start + head_size] = vector.astype(jnp.bfloat16)

    for dy in range(1, ny):
        for part in range(2):
            gather_copy(dy, part).wait_send()
    for dy in range(ny):
        for part in range(2):
            share_copy(dy, part).wait_send()
    for step in range(1, req_count):
        square_copy(step).wait_send()
    for dy, dc in others:
        total_copy(dy, dc).wait_send()

    def sent(step, carry):
        for piece in range(len(pieces)):
            ring_copy(step, piece).wait_send()
            step_copy(step, piece).wait_send()
        return carry

    lax.fori_loop(0, req_count - 1, sent, 0)


def qkv_call(x, gain, tok, weight, cosine, sine, group_size, head_size):
    req_count = lax.axis_size("req")
    kv_count = lax.axis_size("kv")
    ring, ahead_of, behind_of, place_of = ring_of(req_count)
    shard, width = x.shape
    columns = weight.shape[1]
    block = shard * kv_count // req_count
    vectors = columns // head_size
    half = vectors // 2
    pieces = []
    for way in range(2):
        middle = way * half + (half + 1) // 2
        pieces.append((way, way * half * head_size, middle * head_size))
        pieces.append((way, middle * head_size, (way + 1) * half * head_size))
    sizes = (req_count, kv_count, group_size, head_size, pieces, ahead_of, behind_of)
    vmem = pl.BlockSpec(memory_space=pltpu.VMEM)
    anywhere = pl.BlockSpec(memory_space=pl.ANY)
    dma = pltpu.SemaphoreType.DMA
    return pl.pallas_call(
        functools.partial(qkv_kernel, sizes),
        out_shape=jax.ShapeDtypeStruct((block, columns), jnp.bfloat16),
        in_specs=[anywhere, vmem, vmem, anywhere, vmem, vmem],
        out_specs=vmem,
        scratch_shapes=[
            pltpu.VMEM((kv_count, shard, width), jnp.bfloat16),
            pltpu.VMEM((width, columns), jnp.bfloat16),
            pltpu.VMEM((kv_count * shard, width), jnp.bfloat16),
            pltpu.VMEM((2, 8, shard), jnp.float32),
            pltpu.VMEM((req_count, 8, shard), jnp.float32),
            pltpu.VMEM((kv_count, 8, shard), jnp.float32),
            pltpu.VMEM((req_count - 1, block, columns), jnp.int16),
            pltpu.VMEM((req_count - 1, block, columns), jnp.int16),
            pltpu.VMEM((req_count - 1, len(pieces), 8, block), jnp.float32),
            pltpu.VMEM((req_count - 1, len(pieces), 8, block), jnp.float32),
            dma((2,)),
            dma((2, req_count)),
            dma((2, kv_count)),
            dma((2, kv_count // 2, 2)),
            dma((2, kv_count // 2, 2)),
            dma((2, req_count - 1, len(pieces))),
            dma((2, req_count - 1, len(pieces))),
        ],
        compiler_params=pltpu.CompilerParams(
            collective_id=0, has_side_effects=True, vmem_limit_bytes=56 << 20
        ),
    )(x, gain, tok, weight, cosine, sine)


def out_kernel(
    sizes,
    att_hbm,
    w_hbm,
    x_ref,
    gain_ref,
    row_ref,
    projected_ref,
    normed_ref,
    att,
    w_all,
    products,
    mine,
    lent,
    borrowed,
    crossing,
    crossed,
    squares,
    squares_in,
    local_sem,
    ring_sem,
    lend_sem,
    cross_sem,
    square_sem,
):
    req_count, kv_count, ahead_of, behind_of = sizes
    ny = kv_count // 2
    block = att_hbm.shape[0]
    inner = att_hbm.shape[1]
    shard, width = x_ref.shape
    att_copy = pltpu.make_async_copy(att_hbm, att.at[0], local_sem.at[0])
    w_copy = pltpu.make_async_copy(w_hbm, w_all, local_sem.at[1])
    att_copy.start()
    w_copy.start()
    req, kv = enter(req_count, kv_count)
    att_copy.wait()
    targets = (chosen_of(req, ahead_of), chosen_of(req, behind_of))
    half_way = req_count // 2
    wide = inner // 2

    def ring_copy(step, way, part):
        source = (lax.rem(req_count - step + 1, req_count), step - 1)[way]
        target = (req_count - step, step)[way]
        columns = pl.ds(part * wide, wide)
        return pltpu.make_async_remote_copy(
            src_ref=att.at[source, :, columns],
            dst_ref=att.at[target, :, columns],
            send_sem=ring_sem.at[0, step, way, part],
            recv_sem=ring_sem.at[1, step, way, part],
            device_id=(targets[way], kv),
            device_id_type=MESH,
        )

    def multiply(k):
        at = pl.ds(k * block, block)
        products[at, :] = jnp.dot(
            att[k], w_all[...], preferred_element_type=jnp.float32
        ).astype(jnp.bfloat16)

    for part in range(2):
        for way in range(2):
            if half_way > 1 or part == way:
                ring_copy(1, way, part).start()
    w_copy.wait()
    multiply(0)
    for step in range(1, half_way):
        for part in range(2):
            for way in range(2):
                ring_copy(step, way, part).wait_recv()
                if step + 1 < half_way or part == way:
                    ring_copy(step + 1, way, part).start()
        multiply(req_count - step)
        multiply(step)
    for way in range(2):
        ring_copy(half_way, way, way).wait_recv()
    multiply(half_way)

    rows_total = req_count * block

    def gathered(dy, dc, part):
        count = shard // 2
        wanted = row_ref[2 * dy + dc, part * count : (part + 1) * count, :]
        places = lax.broadcasted_iota(jnp.int32, (count, rows_total), 1)
        pick = jnp.where(wanted == places, 1.0, 0.0).astype(jnp.bfloat16)
        return jnp.dot(pick, products[...], preferred_element_type=jnp.float32)

    def lend_copy(dy, part):
        count = shard // 2
        rows = pl.ds(part * count, count)
        return pltpu.make_async_remote_copy(
            src_ref=lent.at[dy, rows],
            dst_ref=borrowed.at[dy, rows],
            send_sem=lend_sem.at[0, dy, part],
            recv_sem=lend_sem.at[1, dy, part],
            device_id=(req, partner(kv, 0, 1, ny)),
            device_id_type=MESH,
        )

    def cross_copy(dy, part):
        count = shard // 2
        rows = pl.ds(part * count, count)
        return pltpu.make_async_remote_copy(
            src_ref=crossing.at[dy, rows],
            dst_ref=crossed.at[dy, rows],
            send_sem=cross_sem.at[0, dy, part],
            recv_sem=cross_sem.at[1, dy, part],
            device_id=(req, partner(kv, dy, 0, ny)),
            device_id_type=MESH,
        )

    def part_rows(part):
        return slice(part * (shard // 2), (part + 1) * (shard // 2))

    turns = [(dy, part) for dy in list(range(1, ny)) + [0] for part in range(2)]
    for dy, part in turns:
        lent[dy, part_rows(part)] = gathered(dy, 1, part).astype(jnp.bfloat16)
        lend_copy(dy, part).start()
        if dy:
            own = gathered(dy, 0, part)
            lend_copy(dy, part).wait_recv()
            crossing[dy, part_rows(part)] = (
                own + borrowed[dy, part_rows(part)].astype(jnp.float32)
            ).astype(jnp.bfloat16)
            cross_copy(dy, part).start()
    for part in range(2):
        mine[part_rows(part)] = gathered(0, 0, part)
    sums = []
    for part in range(2):
        lend_copy(0, part).wait_recv()
        projection = mine[part_rows(part)] + borrowed[0, part_rows(part)].astype(jnp.float32)
        for dy in range(1, ny):
            cross_copy(dy, part).wait_recv()
            projection = projection + crossed[dy, part_rows(part)].astype(jnp.float32)
        projected_ref[part_rows(part)] = projection.astype(jnp.bfloat16)
        residual = x_ref[part_rows(part)].astype(jnp.float32) + projection
        mine[part_rows(part)] = residual
        sums.append(column_to_row(jnp.sum(residual * residual, axis=1, keepdims=True)))
    squares[...] = jnp.broadcast_to(jnp.concatenate(sums, axis=1), squares.shape)

    def square_copy(step):
        return pltpu.make_async_remote_copy(
            src_ref=squares,
            dst_ref=squares_in.at[step],
            send_sem=square_sem.at[0, step],
            recv_sem=square_sem.at[1, step],
            device_id=(lax.rem(req + step, req_count), kv),
            device_id_type=MESH,
        )

    for step in range(1, req_count):
        square_copy(step).start()
    total = squares[...]
    for step in range(1, req_count):
        square_copy(step).wait_recv()
        total = total + squares_in[step]
    rate = row_to_column(lax.rsqrt(total[0:1] / (width * req_count) + epsilon_norm))
    normed_ref[...] = (mine[...] * rate * gain_ref[...]).astype(jnp.bfloat16)

    for step in range(1, half_way + 1):
        for part in range(2):
            for way in range(2):
                if step < half_way or part == way:
                    ring_copy(step, way, part).wait_send()
    for dy, part in turns:
        lend_copy(dy, part).wait_send()
        if dy:
            cross_copy(dy, part).wait_send()
    for step in range(1, req_count):
        square_copy(step).wait_send()


def out_call(attention, weight, x, gain, rows):
    req_count = lax.axis_size("req")
    kv_count = lax.axis_size("kv")
    ring, ahead_of, behind_of, place_of = ring_of(req_count)
    block, inner = attention.shape
    shard, width = x.shape
    ny = kv_count // 2
    vmem = pl.BlockSpec(memory_space=pltpu.VMEM)
    anywhere = pl.BlockSpec(memory_space=pl.ANY)
    dma = pltpu.SemaphoreType.DMA
    made = jax.ShapeDtypeStruct((shard, width), jnp.bfloat16)
    return pl.pallas_call(
        functools.partial(out_kernel, (req_count, kv_count, ahead_of, behind_of)),
        out_shape=(made, made),
        in_specs=[anywhere, anywhere, vmem, vmem, vmem],
        out_specs=(vmem, vmem),
        scratch_shapes=[
            pltpu.VMEM((req_count, block, inner), jnp.bfloat16),
            pltpu.VMEM((inner, width), jnp.bfloat16),
            pltpu.VMEM((req_count * block, width), jnp.bfloat16),
            pltpu.VMEM((shard, width), jnp.float32),
            pltpu.VMEM((ny, shard, width), jnp.bfloat16),
            pltpu.VMEM((ny, shard, width), jnp.bfloat16),
            pltpu.VMEM((ny, shard, width), jnp.bfloat16),
            pltpu.VMEM((ny, shard, width), jnp.bfloat16),
            pltpu.VMEM((8, shard), jnp.float32),
            pltpu.VMEM((req_count, 8, shard), jnp.float32),
            dma((2,)),
            dma((2, req_count // 2 + 1, 2, 2)),
            dma((2, ny, 2)),
            dma((2, ny, 2)),
            dma((2, req_count)),
        ],
        compiler_params=pltpu.CompilerParams(
            collective_id=1, has_side_effects=True, vmem_limit_bytes=56 << 20
        ),
    )(attention, weight, x, gain, rows)


def per_device(
    activations,
    input_gain,
    qkv_weight,
    out_weight,
    post_gain,
    cache_entries,
    new_lengths,
    cache_lengths,
    request_slot,
):
    req_count = lax.axis_size("req")
    kv_count = lax.axis_size("kv")
    shard, width_slice = activations.shape
    token_count = shard * kv_count
    tok_blk = token_count // req_count
    kvh_local = qkv_weight.shape[1]
    head_size = cache_entries.shape[3] // 2
    group_size = qkv_weight.shape[2] // head_size - 2
    ny = kv_count // 2
    block_id = lax.axis_index("req")
    kv_id = lax.axis_index("kv")
    ring, ahead_of, behind_of, place_of = ring_of(req_count)
    place_here = chosen_of(block_id, place_of)
    token_of_row, row_of_token, pos_of_row = layout(
        new_lengths, cache_lengths, request_slot, tok_blk
    )
    ring_array = jnp.asarray(ring, jnp.int32)
    ring_places = lax.rem(place_here + jnp.arange(req_count, dtype=jnp.int32), req_count)
    ring_blocks = jnp.sum(
        jnp.where(ring_places[:, None] == jnp.arange(req_count)[None, :], ring_array[None, :], 0),
        axis=1,
    )
    ring_pick = (ring_blocks[:, None] == jnp.arange(req_count)[None, :]).astype(jnp.int32)
    ring_tokens = jnp.sum(
        ring_pick[:, :, None] * token_of_row.reshape(req_count, tok_blk)[None], axis=1
    ).reshape(-1)
    owner = ring_tokens // shard
    dy = lax.rem(kv_id // 2 - owner // 2 + ny, ny)
    dc = lax.rem(kv_id + owner, 2)
    tok = ((2 * dy + dc) * shard + lax.rem(ring_tokens, shard)).reshape(-1, 1)
    first_row = block_id * tok_blk
    my_positions = lax.dynamic_slice_in_dim(pos_of_row, first_row, tok_blk, 0)
    half_size = head_size // 2
    frequency = jnp.exp(
        -(jnp.arange(half_size, dtype=jnp.float32) * (2.0 / head_size)) * math.log(rope_base)
    )
    angles = my_positions.astype(jnp.float32)[:, None] * frequency[None, :]
    cosine = jnp.cos(angles)
    sine = jnp.sin(angles)
    rotated = qkv_call(
        activations,
        input_gain.astype(jnp.float32).reshape(1, -1),
        tok,
        qkv_weight.reshape(width_slice, -1),
        jnp.concatenate([cosine, cosine], axis=1),
        jnp.concatenate([-sine, sine], axis=1),
        group_size,
        head_size,
    )
    appended = rotated.reshape(tok_blk, kvh_local, group_size + 2, head_size)[
        :, :, group_size:, :
    ].reshape(tok_blk, kvh_local, 2 * head_size)
    new_counts = lax.dynamic_index_in_dim(new_lengths, block_id, 0, keepdims=False)
    cached_counts = lax.dynamic_index_in_dim(cache_lengths, block_id, 0, keepdims=False)
    starts = jnp.concatenate(
        [sums_before(new_counts[None])[0], jnp.full((1,), tok_blk, jnp.int32)]
    )
    attention = block_attention(rotated, cache_entries, starts, cached_counts, group_size)
    place_array = jnp.asarray(place_of, jnp.int32)
    block_of_token = row_of_token // tok_blk
    place_of_token = jnp.sum(
        jnp.where(
            block_of_token[:, None] == jnp.arange(req_count)[None, :], place_array[None, :], 0
        ),
        axis=1,
    )
    ring_row = lax.rem(place_of_token - place_here + req_count, req_count) * tok_blk + lax.rem(
        row_of_token, tok_blk
    )
    owners = jnp.stack(
        [partner(kv_id, dy, dc, ny) for dy in range(ny) for dc in range(2)]
    )
    owner_pick = (owners[:, None] == jnp.arange(kv_count)[None, :]).astype(jnp.int32)
    rows = jnp.sum(
        owner_pick[:, :, None] * ring_row.reshape(kv_count, shard)[None], axis=1
    ).reshape(kv_count, shard, 1)
    projected, normed = out_call(
        attention,
        out_weight.reshape(-1, width_slice),
        activations,
        post_gain.astype(jnp.float32).reshape(1, -1),
        rows,
    )
    return (projected, normed, appended)


def solution(mesh):
    in_specs = (
        P("kv", "req"),
        P("req"),
        P("req", "kv", None),
        P("kv", None, "req"),
        P("req"),
        P("req", None, "kv", None),
        P(),
        P(),
        P(),
    )
    out_specs = (P("kv", "req"), P("kv", "req"), P("req", "kv", None))
    return jax.shard_map(
        per_device, mesh=mesh, in_specs=in_specs, out_specs=out_specs, check_vma=False
    )
```

```python
import functools
import math

import jax
import jax.numpy as jnp
from jax import lax
from jax.experimental import pallas as pl
from jax.experimental.pallas import tpu as pltpu
from jax.sharding import PartitionSpec as P

epsilon_norm = 1e-05
rope_base = 500000.0


def plan_kernel(
    sizes, lengths_ref, filled_ref, slot_ref, tok_ref, row_ref, cos_ref, sin_ref, begin_ref, arrival_ref, ring_ref
):
    req_count, kv_count, ring, place_of = sizes
    per_block = lengths_ref.shape[1]
    requests = req_count * per_block
    block = cos_ref.shape[0]
    head_size = cos_ref.shape[1]
    shard = row_ref.shape[0] // kv_count
    ny = kv_count // 2
    req = lax.axis_index("req")
    kv = lax.axis_index("kv")
    place = chosen_of(req, place_of)
    for k in range(req_count):
        ring_ref[k] = jnp.int32(ring[k])

    def inside(b, carry):
        start = jnp.int32(0)
        for j in range(per_block):
            begin_ref[b * per_block + j] = start
            start = start + lengths_ref[b, j]
        return carry

    lax.fori_loop(0, req_count, inside, 0)
    lanes = lax.broadcasted_iota(jnp.int32, (1, block), 1)
    count = req_count * block
    rows_of = lax.broadcasted_iota(jnp.int32, (count // block, block), 0)
    token = rows_of * block + lax.broadcasted_iota(jnp.int32, (count // block, block), 1)

    def arrive(q, carry):
        start, found = carry
        slot = slot_ref[q]
        b = slot // per_block
        arrival_ref[slot] = start
        turn = lax.rem(chosen_of(b, place_of) - place + req_count, req_count)
        first = turn * block + begin_ref[slot]
        found = jnp.where(token >= start, first + token - start, found)
        return start + lengths_ref[b, slot - b * per_block], found

    _, ring_row = lax.fori_loop(0, requests, arrive, (jnp.int32(0), jnp.zeros_like(token)))

    def to_column(row):
        size = row.shape[1]
        here = lax.broadcasted_iota(jnp.int32, (size, size), 0)
        there = lax.broadcasted_iota(jnp.int32, (size, size), 1)
        return jnp.sum(jnp.where(here == there, row.astype(jnp.float32), 0.0), axis=1, keepdims=True).astype(jnp.int32)

    columns = [to_column(ring_row[r : r + 1]) for r in range(count // block)]
    each = shard // block
    for dy in range(ny):
        for dc in range(2):
            owner = partner(kv, dy, dc, ny)
            for part in range(each):
                column = columns[part]
                for other in range(1, kv_count):
                    column = jnp.where(owner == other, columns[other * each + part], column)
                row_ref[pl.ds((2 * dy + dc) * shard + part * block, block), :] = column

    def tokens_of(b):
        wanted = jnp.zeros_like(lanes)
        for j in range(per_block):
            at = b * per_block + j
            start = begin_ref[at]
            wanted = jnp.where(lanes >= start, arrival_ref[at] + lanes - start, wanted)
        return wanted

    for k in range(req_count):
        wanted = tokens_of(ring_ref[lax.rem(place + k, req_count)])
        owner = jnp.zeros_like(wanted)
        for other in range(1, kv_count):
            owner = owner + (wanted >= other * shard).astype(jnp.int32)
        turn = kv // 2 - owner // 2
        turn = jnp.where(turn < 0, turn + ny, turn)
        slot = 2 * turn + lax.rem(kv + owner, 2)
        tok_ref[k * block : (k + 1) * block, :] = to_column(wanted + (slot - owner) * shard)
    position = jnp.zeros_like(lanes)
    for j in range(per_block):
        start = begin_ref[req * per_block + j]
        position = jnp.where(lanes >= start, filled_ref[req, j] + lanes - start, position)
    index = lax.broadcasted_iota(jnp.int32, (1, head_size), 1)
    half = head_size // 2
    pair = jnp.where(index >= half, index - half, index).astype(jnp.float32)
    frequency = jnp.exp(-(pair * (2.0 / head_size)) * math.log(rope_base))
    angles = to_column(position).astype(jnp.float32) * frequency
    cos_ref[...] = jnp.cos(angles)
    sine = jnp.sin(angles)
    sin_ref[...] = jnp.where(index >= half, sine, -sine)


def plan_call(new_lengths, cache_lengths, request_slot, shard, head_size):
    req_count = lax.axis_size("req")
    kv_count = lax.axis_size("kv")
    ring, _, _, place_of = ring_of(req_count)
    block = shard * kv_count // req_count
    smem = pl.BlockSpec(memory_space=pltpu.SMEM)
    vmem = pl.BlockSpec(memory_space=pltpu.VMEM)
    requests = request_slot.shape[0]
    angles = jax.ShapeDtypeStruct((block, head_size), jnp.float32)
    return pl.pallas_call(
        functools.partial(plan_kernel, (req_count, kv_count, ring, place_of)),
        out_shape=(
            jax.ShapeDtypeStruct((req_count * block, 1), jnp.int32),
            jax.ShapeDtypeStruct((kv_count * shard, 1), jnp.int32),
            angles,
            angles,
        ),
        in_specs=[smem, smem, smem],
        out_specs=(vmem, vmem, vmem, vmem),
        scratch_shapes=[
            pltpu.SMEM((requests,), jnp.int32),
            pltpu.SMEM((requests,), jnp.int32),
            pltpu.SMEM((req_count,), jnp.int32),
        ],
    )(new_lengths, cache_lengths, request_slot)


def attention_kernel(
    group_size, key_block, lengths_ref, filled_ref, rotated_ref, stored_hbm, out_ref,
    raw, staged, keys, values, scores, copy_sem,
):
    slots = stored_hbm.shape[0]
    heads = keys.shape[0]
    block = rotated_ref.shape[0]
    head_size = keys.shape[2]
    stride = 2 * heads
    tokens = min(32, block)
    rows = tokens * group_size
    small = key_block // 2
    here = lax.axis_index("req")
    scale = math.log2(math.e) / math.sqrt(head_size)
    span = (group_size + 2) * head_size
    contract_last = (((1,), (1,)), ((), ()))

    def load(slot, index):
        at = pl.ds(pl.multiple_of(index * key_block * stride, key_block * stride), key_block * stride)
        return pltpu.make_async_copy(
            stored_hbm.at[slot, at], raw.at[slot, at], copy_sem.at[slot, index]
        )

    def blocks_of(slot):
        return (filled_ref[here, slot] + key_block - 1) // key_block

    def begin(slot, carry):
        def one(index, inner):
            load(slot, index).start()
            return inner

        return lax.fori_loop(0, blocks_of(slot), one, carry)

    lax.fori_loop(0, slots, begin, 0)

    def lane_fold(op, value):
        folded = value[:, :head_size]
        for part in range(1, value.shape[1] // head_size):
            folded = op(folded, value[:, part * head_size : (part + 1) * head_size])
        return folded

    def one_slot(slot, start):
        end = start + lengths_ref[here, slot]
        cached = filled_ref[here, slot]

        def split(index, inner):
            load(slot, index).wait()
            base = pl.multiple_of(index * key_block, key_block)
            staged[...] = raw[
                slot, pl.ds(pl.multiple_of(base * stride, key_block * stride), key_block * stride), :
            ].astype(jnp.float32)
            for head in range(heads):
                keys[head, pl.ds(base, key_block), :] = staged[
                    pl.ds(head, key_block, stride=stride), :
                ].astype(jnp.bfloat16)
                values[head, pl.ds(base, key_block), :] = staged[
                    pl.ds(heads + head, key_block, stride=stride), :
                ].astype(jnp.bfloat16)
            return inner

        lax.fori_loop(0, blocks_of(slot), split, 0)
        whole = cached // key_block
        first_part = whole * (key_block // small)
        last_part = (cached + small - 1) // small

        def one_chunk(chunk, inner):
            at = pl.ds(pl.multiple_of(chunk * tokens, tokens), tokens)
            token = chunk * tokens + lax.rem(
                lax.broadcasted_iota(jnp.int32, (rows, block), 0), tokens
            )
            other = lax.broadcasted_iota(jnp.int32, (rows, block), 1)
            allowed = (other <= token) & (other >= start)
            queries, owns = [], []
            for head in range(heads):
                query = jnp.concatenate(
                    [
                        rotated_ref[at, head * span + g * head_size : head * span + (g + 1) * head_size]
                        for g in range(group_size)
                    ],
                    axis=0,
                )
                new_key = rotated_ref[:, head * span + group_size * head_size : head * span + (group_size + 1) * head_size]
                own = lax.dot_general(
                    query, new_key, contract_last, preferred_element_type=jnp.float32
                )
                queries.append(query)
                owns.append(jnp.where(allowed, own, -jnp.inf))

            def score(head, first, width):
                return lax.dot_general(
                    queries[head],
                    keys[head, pl.ds(first, width), :],
                    contract_last,
                    preferred_element_type=jnp.float32,
                )

            def fill(index, highest):
                first = pl.multiple_of(index * key_block, key_block)
                found = [score(head, first, key_block) for head in range(heads)]
                for head in range(heads):
                    scores[head, :, pl.ds(first, key_block)] = found[head]
                return tuple(
                    jnp.maximum(highest[head], lane_fold(jnp.maximum, found[head]))
                    for head in range(heads)
                )

            def fill_part(index, highest):
                first = pl.multiple_of(index * small, small)
                places = lax.broadcasted_iota(jnp.int32, (rows, small), 1)
                found = [
                    jnp.where(places < cached - first, score(head, first, small), -jnp.inf)
                    for head in range(heads)
                ]
                for head in range(heads):
                    scores[head, :, pl.ds(first, small)] = found[head]
                return tuple(
                    jnp.maximum(highest[head], lane_fold(jnp.maximum, found[head]))
                    for head in range(heads)
                )

            highest = tuple(lane_fold(jnp.maximum, owns[head]) for head in range(heads))
            highest = lax.fori_loop(0, whole, fill, highest)
            highest = lax.fori_loop(first_part, last_part, fill_part, highest)
            tops = [jnp.max(highest[head], axis=1, keepdims=True) for head in range(heads)]
            state = []
            for head in range(heads):
                weights = jnp.exp2((owns[head] - tops[head]) * scale)
                new_value = rotated_ref[:, head * span + (group_size + 1) * head_size : (head + 1) * span]
                state.append(lane_fold(jnp.add, weights))
                state.append(
                    jnp.dot(
                        weights.astype(jnp.bfloat16), new_value, preferred_element_type=jnp.float32
                    )
                )

            def accumulate(width):
                def body(index, state):
                    first = pl.multiple_of(index * width, width)
                    result = []
                    for head in range(heads):
                        weights = jnp.exp2(
                            (scores[head, :, pl.ds(first, width)] - tops[head]) * scale
                        )
                        added = jnp.dot(
                            weights.astype(jnp.bfloat16),
                            values[head, pl.ds(first, width), :],
                            preferred_element_type=jnp.float32,
                        )
                        result.append(state[2 * head] + lane_fold(jnp.add, weights))
                        result.append(state[2 * head + 1] + added)
                    return tuple(result)

                return body

            state = lax.fori_loop(0, whole, accumulate(key_block), tuple(state))
            state = lax.fori_loop(first_part, last_part, accumulate(small), state)
            member_token = chunk * tokens + lax.broadcasted_iota(jnp.int32, (tokens, head_size), 0)
            member = (member_token >= start) & (member_token < end)
            for head in range(heads):
                total = jnp.sum(state[2 * head], axis=1, keepdims=True)
                made = state[2 * head + 1] / total
                for g in range(group_size):
                    columns = slice(
                        (head * group_size + g) * head_size, (head * group_size + g + 1) * head_size
                    )
                    old = out_ref[at, columns].astype(jnp.float32)
                    out_ref[at, columns] = jnp.where(
                        member, made[g * tokens : (g + 1) * tokens], old
                    ).astype(jnp.bfloat16)
            return inner

        lax.fori_loop(start // tokens, (end + tokens - 1) // tokens, one_chunk, 0)
        return end

    lax.fori_loop(0, slots, one_slot, 0)


def block_attention(rotated, cache_entries, new_lengths, cache_lengths, group_size):
    slots, slot_length, heads, both = cache_entries.shape
    head_size = both // 2
    block = rotated.shape[0]
    key_block = min(512, slot_length)
    stored = jnp.transpose(
        cache_entries.reshape(slots, slot_length, heads, 2, head_size), (0, 1, 3, 2, 4)
    ).reshape(slots, slot_length * 2 * heads, head_size)
    rows = min(32, block) * group_size
    grid_spec = pltpu.PrefetchScalarGridSpec(
        num_scalar_prefetch=2,
        grid=(1,),
        in_specs=[
            pl.BlockSpec(rotated.shape, lambda i, s, c: (0, 0)),
            pl.BlockSpec(memory_space=pl.ANY),
        ],
        out_specs=pl.BlockSpec((block, heads * group_size * head_size), lambda i, s, c: (0, 0)),
        scratch_shapes=[
            pltpu.VMEM((slots, slot_length * 2 * heads, head_size), jnp.bfloat16),
            pltpu.VMEM((key_block * 2 * heads, head_size), jnp.float32),
            pltpu.VMEM((heads, slot_length, head_size), jnp.bfloat16),
            pltpu.VMEM((heads, slot_length, head_size), jnp.bfloat16),
            pltpu.VMEM((heads, rows, slot_length), jnp.float32),
            pltpu.SemaphoreType.DMA((slots, slot_length // key_block)),
        ],
    )
    return pl.pallas_call(
        functools.partial(attention_kernel, group_size, key_block),
        grid_spec=grid_spec,
        out_shape=jax.ShapeDtypeStruct((block, heads * group_size * head_size), jnp.bfloat16),
        compiler_params=pltpu.CompilerParams(vmem_limit_bytes=56 << 20),
    )(new_lengths, cache_lengths, rotated, stored)


MESH = pl.DeviceIdType.MESH


def chosen_of(index, table):
    found = jnp.int32(table[0])
    for place in range(1, len(table)):
        found = jnp.where(index == place, jnp.int32(table[place]), found)
    return found


def ring_of(count):
    across = 1
    while 4 * across * across <= count:
        across *= 2
    along = count // across
    ring = [place * across for place in range(along)]
    for turn, place in enumerate(reversed(range(along))):
        row = [place * across + step for step in range(1, across)]
        ring += row if turn % 2 == 0 else row[::-1]
    ahead = [0] * count
    behind = [0] * count
    place_of = [0] * count
    for i in range(count):
        ahead[ring[i]] = ring[(i + 1) % count]
        behind[ring[i]] = ring[(i - 1) % count]
        place_of[ring[i]] = i
    return ring, ahead, behind, place_of


def enter(req_count, kv_count):
    req = lax.axis_index("req")
    kv = lax.axis_index("kv")
    barrier = pltpu.get_barrier_semaphore()
    for step in range(1, req_count):
        pl.semaphore_signal(
            barrier, inc=1, device_id=(lax.rem(req + step, req_count), kv), device_id_type=MESH
        )
    for step in range(1, kv_count):
        pl.semaphore_signal(
            barrier, inc=1, device_id=(req, lax.rem(kv + step, kv_count)), device_id_type=MESH
        )
    pl.semaphore_wait(barrier, req_count + kv_count - 2)
    return req, kv


def column_to_row(column):
    count = column.shape[0]
    here = lax.broadcasted_iota(jnp.int32, (count, count), 0)
    there = lax.broadcasted_iota(jnp.int32, (count, count), 1)
    return jnp.sum(jnp.where(here == there, column, 0.0), axis=0, keepdims=True)


def row_to_column(row):
    count = row.shape[1]
    here = lax.broadcasted_iota(jnp.int32, (count, count), 0)
    there = lax.broadcasted_iota(jnp.int32, (count, count), 1)
    return jnp.sum(jnp.where(here == there, row, 0.0), axis=1, keepdims=True)


def partner(kv, dy, dc, ny):
    return lax.rem(kv // 2 + dy, ny) * 2 + lax.rem(kv + dc, 2)


def qkv_kernel(
    sizes,
    x_hbm,
    gain_ref,
    tok_ref,
    w_hbm,
    cos_ref,
    sin_ref,
    out_ref,
    x_all,
    w_all,
    picks,
    rates,
    normed,
    squares,
    squares_in,
    totals_in,
    land,
    leave,
    steps_in,
    steps_out,
    local_sem,
    square_sem,
    total_sem,
    gather_sem,
    share_sem,
    ring_sem,
    step_sem,
):
    req_count, kv_count, group_size, head_size, pieces, ahead_of, behind_of = sizes
    ny = kv_count // 2
    shard = x_hbm.shape[0]
    width = x_hbm.shape[1]
    block = out_ref.shape[0]
    w_copy = pltpu.make_async_copy(w_hbm, w_all, local_sem.at[0])
    x_copy = pltpu.make_async_copy(x_hbm, x_all.at[0], local_sem.at[1])
    x_copy.start()
    w_copy.start()
    req, kv = enter(req_count, kv_count)
    x_copy.wait()
    chunk = shard // 2

    def gather_copy(dy, part):
        rows = pl.ds(part * chunk, chunk)
        return pltpu.make_async_remote_copy(
            src_ref=x_all.at[0, rows],
            dst_ref=x_all.at[2 * dy, rows],
            send_sem=gather_sem.at[0, dy, part],
            recv_sem=gather_sem.at[1, dy, part],
            device_id=(req, partner(kv, dy, 0, ny)),
            device_id_type=MESH,
        )

    def share_copy(dy, part):
        rows = pl.ds(part * chunk, chunk)
        return pltpu.make_async_remote_copy(
            src_ref=x_all.at[2 * dy, rows],
            dst_ref=x_all.at[2 * dy + 1, rows],
            send_sem=share_sem.at[0, dy, part],
            recv_sem=share_sem.at[1, dy, part],
            device_id=(req, partner(kv, 0, 1, ny)),
            device_id_type=MESH,
        )

    def square_copy(step):
        return pltpu.make_async_remote_copy(
            src_ref=squares.at[0],
            dst_ref=squares_in.at[step],
            send_sem=square_sem.at[0, step],
            recv_sem=square_sem.at[1, step],
            device_id=(lax.rem(req + step, req_count), kv),
            device_id_type=MESH,
        )

    def total_copy(dy, dc):
        slot = 2 * dy + dc
        return pltpu.make_async_remote_copy(
            src_ref=squares.at[1],
            dst_ref=totals_in.at[slot],
            send_sem=total_sem.at[0, slot],
            recv_sem=total_sem.at[1, slot],
            device_id=(req, partner(kv, dy, dc, ny)),
            device_id_type=MESH,
        )

    for part in range(2):
        for dy in range(1, ny):
            gather_copy(dy, part).start()
    x_own = x_all[0].astype(jnp.float32)
    own = column_to_row(jnp.sum(x_own * x_own, axis=1, keepdims=True))
    squares[0] = jnp.broadcast_to(own, squares.shape[1:])
    for step in range(1, req_count):
        square_copy(step).start()
    for part in range(2):
        share_copy(0, part).start()
    total = squares[0]
    for step in range(1, req_count):
        square_copy(step).wait_recv()
        total = total + squares_in[step]
    squares[1] = total
    others = [(dy, dc) for dy in range(ny) for dc in range(2) if dy or dc]
    for dy, dc in others:
        total_copy(dy, dc).start()
    rate_rows = [None] * kv_count
    rate_rows[0] = lax.rsqrt(total[0:1] / (width * req_count) + epsilon_norm)
    for dy, dc in others:
        total_copy(dy, dc).wait_recv()
        rate_rows[2 * dy + dc] = lax.rsqrt(
            totals_in[2 * dy + dc, 0:1] / (width * req_count) + epsilon_norm
        )
    def pick_rows(k, carry):
        at = pl.ds(pl.multiple_of(k * block, block), block)
        wanted = tok_ref[at, :]
        rate = jnp.zeros((block, 1), jnp.float32)
        for slot in range(kv_count):
            places = lax.broadcasted_iota(jnp.int32, (block, shard), 1) + slot * shard
            pick = wanted == places
            rate = rate + jnp.sum(jnp.where(pick, rate_rows[slot], 0.0), axis=1, keepdims=True)
            picks[at, slot * shard : (slot + 1) * shard] = jnp.where(pick, 1.0, 0.0).astype(
                jnp.bfloat16
            )
        rates[at, :] = rate
        return carry

    lax.fori_loop(0, req_count, pick_rows, 0)
    for part in range(2):
        for dy in range(1, ny):
            gather_copy(dy, part).wait_recv()
            share_copy(dy, part).start()
    for dy in range(ny):
        for part in range(2):
            share_copy(dy, part).wait_recv()
    w_copy.wait()
    rows_of_all = x_all[...].reshape(kv_count * shard, width)

    def normalise(k):
        at = pl.ds(pl.multiple_of(k * block, block), block)
        rows = jnp.dot(picks[at, :], rows_of_all, preferred_element_type=jnp.float32)
        normed[at, :] = (rows * rates[at, :] * gain_ref[...]).astype(jnp.bfloat16)

    def product(k, first, last):
        at = pl.ds(pl.multiple_of(k * block, block), block)
        return jnp.dot(normed[at, :], w_all[:, first:last], preferred_element_type=jnp.float32)

    targets = (chosen_of(req, ahead_of), chosen_of(req, behind_of))

    def ring_copy(step, piece):
        way, first, last = pieces[piece]
        columns = pl.ds(first, last - first)
        return pltpu.make_async_remote_copy(
            src_ref=leave.at[step, :, columns],
            dst_ref=land.at[step, :, columns],
            send_sem=ring_sem.at[0, step, piece],
            recv_sem=ring_sem.at[1, step, piece],
            device_id=(targets[way], kv),
            device_id_type=MESH,
        )

    def step_copy(step, piece):
        return pltpu.make_async_remote_copy(
            src_ref=steps_out.at[step, piece],
            dst_ref=steps_in.at[step, piece],
            send_sem=step_sem.at[0, step, piece],
            recv_sem=step_sem.at[1, step, piece],
            device_id=(targets[pieces[piece][0]], kv),
            device_id_type=MESH,
        )

    def pass_on(step, piece, value):
        way, first, last = pieces[piece]
        top = jnp.maximum(jnp.max(jnp.abs(value), axis=1, keepdims=True), 1e-30)
        steps_out[step, piece] = jnp.broadcast_to(
            column_to_row(top * (1.0 / 32767.0)), steps_out.shape[2:]
        )
        step_copy(step, piece).start()
        codes = jnp.floor(value * (32767.0 / top) + 0.5).astype(jnp.int32)
        leave[step, :, first:last] = codes.astype(jnp.int16)
        ring_copy(step, piece).start()

    def arrived(step, piece):
        way, first, last = pieces[piece]
        step_copy(step, piece).wait_recv()
        unit = row_to_column(steps_in[step, piece, 0:1])
        ring_copy(step, piece).wait_recv()
        codes = land[step, :, first:last].astype(jnp.int32)
        return codes.astype(jnp.float32) * unit

    order = sorted(range(len(pieces)), key=lambda p: p % 2)
    normalise(req_count - 1)
    normalise(1)
    for piece in range(len(pieces)):
        way, first, last = pieces[piece]
        pass_on(0, piece, product(1 if way else req_count - 1, first, last))

    def rest(k, carry):
        normalise(lax.rem(k, req_count))
        return carry

    lax.fori_loop(2, req_count - 1, rest, 0)
    normalise(0)

    def one_step(step, carry):
        for piece in order:
            way, first, last = pieces[piece]
            k = 2 + step if way else req_count - 2 - step
            added = product(k, first, last)
            pass_on(step + 1, piece, arrived(step, piece) + added)
        return carry

    lax.fori_loop(0, req_count - 2, one_step, 0)
    half = head_size // 2
    for piece in order:
        way, first, last = pieces[piece]
        added = product(0, first, last)
        summed = arrived(req_count - 2, piece) + added
        for place in range((last - first) // head_size):
            vector = summed[:, place * head_size : (place + 1) * head_size]
            start = first + place * head_size
            if (start // head_size) % (group_size + 2) <= group_size:
                vector = vector * cos_ref[...] + pltpu.roll(vector, half, 1) * sin_ref[...]
            out_ref[:, start : start + head_size] = vector.astype(jnp.bfloat16)

    for dy in range(1, ny):
        for part in range(2):
            gather_copy(dy, part).wait_send()
    for dy in range(ny):
        for part in range(2):
            share_copy(dy, part).wait_send()
    for step in range(1, req_count):
        square_copy(step).wait_send()
    for dy, dc in others:
        total_copy(dy, dc).wait_send()

    def sent(step, carry):
        for piece in range(len(pieces)):
            ring_copy(step, piece).wait_send()
            step_copy(step, piece).wait_send()
        return carry

    lax.fori_loop(0, req_count - 1, sent, 0)


def qkv_call(x, gain, tok, weight, head_size, cosine, sine, heads, group_size):
    req_count = lax.axis_size("req")
    kv_count = lax.axis_size("kv")
    ring, ahead_of, behind_of, place_of = ring_of(req_count)
    shard, width = x.shape
    columns = heads * (group_size + 2) * head_size
    block = shard * kv_count // req_count
    vectors = columns // head_size
    half = vectors // 2
    pieces = []
    for way in range(2):
        middle = way * half + (half + 1) // 2
        pieces.append((way, way * half * head_size, middle * head_size))
        pieces.append((way, middle * head_size, (way + 1) * half * head_size))
    sizes = (req_count, kv_count, group_size, head_size, pieces, ahead_of, behind_of)
    vmem = pl.BlockSpec(memory_space=pltpu.VMEM)
    anywhere = pl.BlockSpec(memory_space=pl.ANY)
    dma = pltpu.SemaphoreType.DMA
    return pl.pallas_call(
        functools.partial(qkv_kernel, sizes),
        out_shape=jax.ShapeDtypeStruct((block, columns), jnp.bfloat16),
        in_specs=[anywhere, vmem, vmem, anywhere, vmem, vmem],
        out_specs=vmem,
        scratch_shapes=[
            pltpu.VMEM((kv_count, shard, width), jnp.bfloat16),
            pltpu.VMEM((width, columns), jnp.bfloat16),
            pltpu.VMEM((kv_count * shard, kv_count * shard), jnp.bfloat16),
            pltpu.VMEM((kv_count * shard, 1), jnp.float32),
            pltpu.VMEM((kv_count * shard, width), jnp.bfloat16),
            pltpu.VMEM((2, 8, shard), jnp.float32),
            pltpu.VMEM((req_count, 8, shard), jnp.float32),
            pltpu.VMEM((kv_count, 8, shard), jnp.float32),
            pltpu.VMEM((req_count - 1, block, columns), jnp.int16),
            pltpu.VMEM((req_count - 1, block, columns), jnp.int16),
            pltpu.VMEM((req_count - 1, len(pieces), 8, block), jnp.float32),
            pltpu.VMEM((req_count - 1, len(pieces), 8, block), jnp.float32),
            dma((2,)),
            dma((2, req_count)),
            dma((2, kv_count)),
            dma((2, kv_count // 2, 2)),
            dma((2, kv_count // 2, 2)),
            dma((2, req_count - 1, len(pieces))),
            dma((2, req_count - 1, len(pieces))),
        ],
        compiler_params=pltpu.CompilerParams(
            collective_id=0, has_side_effects=True, vmem_limit_bytes=56 << 20
        ),
    )(x, gain, tok, weight, cosine, sine)


def out_kernel(
    sizes,
    att_hbm,
    w_hbm,
    x_ref,
    gain_ref,
    row_ref,
    projected_ref,
    normed_ref,
    att,
    w_all,
    products,
    picks,
    taken,
    mine,
    lent,
    borrowed,
    crossing,
    crossed,
    squares,
    squares_in,
    local_sem,
    ring_sem,
    lend_sem,
    cross_sem,
    square_sem,
):
    req_count, kv_count, ahead_of, behind_of = sizes
    ny = kv_count // 2
    block = att_hbm.shape[0]
    inner = att_hbm.shape[1]
    shard, width = x_ref.shape
    att_copy = pltpu.make_async_copy(att_hbm, att.at[0], local_sem.at[0])
    w_copy = pltpu.make_async_copy(w_hbm, w_all, local_sem.at[1])
    att_copy.start()
    w_copy.start()
    req, kv = enter(req_count, kv_count)
    att_copy.wait()
    targets = (chosen_of(req, ahead_of), chosen_of(req, behind_of))
    half_way = req_count // 2
    wide = inner // 2

    def ring_copy(step, way, part):
        source = (lax.rem(req_count - step + 1, req_count), step - 1)[way]
        target = (req_count - step, step)[way]
        columns = pl.ds(part * wide, wide)
        return pltpu.make_async_remote_copy(
            src_ref=att.at[source, :, columns],
            dst_ref=att.at[target, :, columns],
            send_sem=ring_sem.at[0, step, way, part],
            recv_sem=ring_sem.at[1, step, way, part],
            device_id=(targets[way], kv),
            device_id_type=MESH,
        )

    def multiply(k):
        at = pl.ds(k * block, block)
        products[at, :] = jnp.dot(
            att[k], w_all[...], preferred_element_type=jnp.float32
        ).astype(jnp.bfloat16)

    for part in range(2):
        for way in range(2):
            if half_way > 1 or part == way:
                ring_copy(1, way, part).start()
    w_copy.wait()
    multiply(0)
    rows_total = req_count * block
    groups = [(dy, dc, part) for dy in range(ny) for dc in range(2) for part in range(2)]
    count = shard // 2

    def pick_rows(index, carry):
        wanted = row_ref[pl.ds(pl.multiple_of(index * count, count), count), :]
        places = lax.broadcasted_iota(jnp.int32, (count, rows_total), 1)
        picks[pl.ds(pl.multiple_of(index * count, count), count), :] = jnp.where(
            wanted == places, 1.0, 0.0
        ).astype(jnp.bfloat16)
        return carry

    lax.fori_loop(0, len(groups), pick_rows, 0)
    for step in range(1, half_way):
        for part in range(2):
            for way in range(2):
                ring_copy(step, way, part).wait_recv()
                if step + 1 < half_way or part == way:
                    ring_copy(step + 1, way, part).start()
        multiply(req_count - step)
        multiply(step)
    products[half_way * block : (half_way + 1) * block, :] = jnp.zeros((block, width), jnp.bfloat16)

    def take(index, carry):
        at = pl.ds(pl.multiple_of(index * count, count), count)
        taken[at, :] = jnp.dot(
            picks[at, :], products[...], preferred_element_type=jnp.float32
        )
        return carry

    lax.fori_loop(0, len(groups), take, 0)
    for way in range(2):
        ring_copy(half_way, way, way).wait_recv()
    multiply(half_way)

    def gathered(dy, dc, part):
        at = groups.index((dy, dc, part)) * count
        return taken[at : at + count, :] + jnp.dot(
            picks[at : at + count, half_way * block : (half_way + 1) * block],
            products[half_way * block : (half_way + 1) * block, :],
            preferred_element_type=jnp.float32,
        )

    def lend_copy(dy, part):
        rows = pl.ds(part * count, count)
        return pltpu.make_async_remote_copy(
            src_ref=lent.at[dy, rows],
            dst_ref=borrowed.at[dy, rows],
            send_sem=lend_sem.at[0, dy, part],
            recv_sem=lend_sem.at[1, dy, part],
            device_id=(req, partner(kv, 0, 1, ny)),
            device_id_type=MESH,
        )

    def cross_copy(dy, part):
        rows = pl.ds(part * count, count)
        return pltpu.make_async_remote_copy(
            src_ref=crossing.at[dy, rows],
            dst_ref=crossed.at[dy, rows],
            send_sem=cross_sem.at[0, dy, part],
            recv_sem=cross_sem.at[1, dy, part],
            device_id=(req, partner(kv, dy, 0, ny)),
            device_id_type=MESH,
        )

    def part_rows(part):
        return slice(part * (shard // 2), (part + 1) * (shard // 2))

    turns = [(dy, part) for dy in list(range(1, ny)) + [0] for part in range(2)]
    for dy, part in turns:
        lent[dy, part_rows(part)] = gathered(dy, 1, part).astype(jnp.bfloat16)
        lend_copy(dy, part).start()
        if dy:
            own = gathered(dy, 0, part)
            lend_copy(dy, part).wait_recv()
            crossing[dy, part_rows(part)] = (
                own + borrowed[dy, part_rows(part)].astype(jnp.float32)
            ).astype(jnp.bfloat16)
            cross_copy(dy, part).start()
    for part in range(2):
        mine[part_rows(part)] = gathered(0, 0, part)
    sums = []
    for part in range(2):
        lend_copy(0, part).wait_recv()
        projection = mine[part_rows(part)] + borrowed[0, part_rows(part)].astype(jnp.float32)
        for dy in range(1, ny):
            cross_copy(dy, part).wait_recv()
            projection = projection + crossed[dy, part_rows(part)].astype(jnp.float32)
        projected_ref[part_rows(part)] = projection.astype(jnp.bfloat16)
        residual = x_ref[part_rows(part)].astype(jnp.float32) + projection
        mine[part_rows(part)] = residual
        sums.append(column_to_row(jnp.sum(residual * residual, axis=1, keepdims=True)))
    squares[...] = jnp.broadcast_to(jnp.concatenate(sums, axis=1), squares.shape)

    def square_copy(step):
        return pltpu.make_async_remote_copy(
            src_ref=squares,
            dst_ref=squares_in.at[step],
            send_sem=square_sem.at[0, step],
            recv_sem=square_sem.at[1, step],
            device_id=(lax.rem(req + step, req_count), kv),
            device_id_type=MESH,
        )

    for step in range(1, req_count):
        square_copy(step).start()
    total = squares[...]
    for step in range(1, req_count):
        square_copy(step).wait_recv()
        total = total + squares_in[step]
    rate = row_to_column(lax.rsqrt(total[0:1] / (width * req_count) + epsilon_norm))
    normed_ref[...] = (mine[...] * rate * gain_ref[...]).astype(jnp.bfloat16)

    for step in range(1, half_way + 1):
        for part in range(2):
            for way in range(2):
                if step < half_way or part == way:
                    ring_copy(step, way, part).wait_send()
    for dy, part in turns:
        lend_copy(dy, part).wait_send()
        if dy:
            cross_copy(dy, part).wait_send()
    for step in range(1, req_count):
        square_copy(step).wait_send()


def out_call(attention, weight, x, gain, rows):
    req_count = lax.axis_size("req")
    kv_count = lax.axis_size("kv")
    ring, ahead_of, behind_of, place_of = ring_of(req_count)
    block, inner = attention.shape
    shard, width = x.shape
    ny = kv_count // 2
    vmem = pl.BlockSpec(memory_space=pltpu.VMEM)
    anywhere = pl.BlockSpec(memory_space=pl.ANY)
    dma = pltpu.SemaphoreType.DMA
    made = jax.ShapeDtypeStruct((shard, width), jnp.bfloat16)
    return pl.pallas_call(
        functools.partial(out_kernel, (req_count, kv_count, ahead_of, behind_of)),
        out_shape=(made, made),
        in_specs=[anywhere, anywhere, vmem, vmem, vmem],
        out_specs=(vmem, vmem),
        scratch_shapes=[
            pltpu.VMEM((req_count, block, inner), jnp.bfloat16),
            pltpu.VMEM((inner, width), jnp.bfloat16),
            pltpu.VMEM((req_count * block, width), jnp.bfloat16),
            pltpu.VMEM((kv_count * shard, req_count * block), jnp.bfloat16),
            pltpu.VMEM((kv_count * shard, width), jnp.float32),
            pltpu.VMEM((shard, width), jnp.float32),
            pltpu.VMEM((ny, shard, width), jnp.bfloat16),
            pltpu.VMEM((ny, shard, width), jnp.bfloat16),
            pltpu.VMEM((ny, shard, width), jnp.bfloat16),
            pltpu.VMEM((ny, shard, width), jnp.bfloat16),
            pltpu.VMEM((8, shard), jnp.float32),
            pltpu.VMEM((req_count, 8, shard), jnp.float32),
            dma((2,)),
            dma((2, req_count // 2 + 1, 2, 2)),
            dma((2, ny, 2)),
            dma((2, ny, 2)),
            dma((2, req_count)),
        ],
        compiler_params=pltpu.CompilerParams(
            collective_id=1, has_side_effects=True, vmem_limit_bytes=56 << 20
        ),
    )(attention, weight, x, gain, rows)


def per_device(
    activations,
    input_gain,
    qkv_weight,
    out_weight,
    post_gain,
    cache_entries,
    new_lengths,
    cache_lengths,
    request_slot,
):
    req_count = lax.axis_size("req")
    kv_count = lax.axis_size("kv")
    shard, width_slice = activations.shape
    kvh_local = qkv_weight.shape[1]
    head_size = cache_entries.shape[3] // 2
    vectors = qkv_weight.shape[2] // head_size
    group_size = vectors - 2
    tok_blk = shard * kv_count // req_count
    tok, rows, cosine, sine = plan_call(
        new_lengths, cache_lengths, request_slot, shard, head_size
    )
    rotated = qkv_call(
        activations,
        input_gain.astype(jnp.float32).reshape(1, -1),
        tok,
        qkv_weight.reshape(width_slice, -1),
        head_size,
        cosine,
        sine,
        kvh_local,
        group_size,
    )
    appended = rotated.reshape(tok_blk, kvh_local, vectors, head_size)[
        :, :, group_size:, :
    ].reshape(tok_blk, kvh_local, 2 * head_size)
    attention = block_attention(rotated, cache_entries, new_lengths, cache_lengths, group_size)
    projected, normed = out_call(
        attention,
        out_weight.reshape(-1, width_slice),
        activations,
        post_gain.astype(jnp.float32).reshape(1, -1),
        rows,
    )
    return (projected, normed, appended)


def solution(mesh):
    in_specs = (
        P("kv", "req"),
        P("req"),
        P("req", "kv", None),
        P("kv", None, "req"),
        P("req"),
        P("req", None, "kv", None),
        P(),
        P(),
        P(),
    )
    out_specs = (P("kv", "req"), P("kv", "req"), P("req", "kv", None))
    return jax.shard_map(
        per_device, mesh=mesh, in_specs=in_specs, out_specs=out_specs, check_vma=False
    )
```

```python
import functools
import math

import jax
import jax.numpy as jnp
from jax import lax
from jax.experimental import pallas as pl
from jax.experimental.pallas import tpu as pltpu
from jax.sharding import PartitionSpec as P

epsilon_norm = 1e-05
rope_base = 500000.0


def plan_kernel(
    sizes, lengths_ref, filled_ref, slot_ref, tok_ref, row_ref, cos_ref, sin_ref, begin_ref, arrival_ref, ring_ref
):
    req_count, kv_count, ring, place_of = sizes
    per_block = lengths_ref.shape[1]
    requests = req_count * per_block
    block = cos_ref.shape[0]
    head_size = cos_ref.shape[1]
    shard = row_ref.shape[0] // kv_count
    ny = kv_count // 2
    req = lax.axis_index("req")
    kv = lax.axis_index("kv")
    place = chosen_of(req, place_of)
    for k in range(req_count):
        ring_ref[k] = jnp.int32(ring[k])

    def inside(b, carry):
        start = jnp.int32(0)
        for j in range(per_block):
            begin_ref[b * per_block + j] = start
            start = start + lengths_ref[b, j]
        return carry

    lax.fori_loop(0, req_count, inside, 0)
    lanes = lax.broadcasted_iota(jnp.int32, (1, block), 1)
    count = req_count * block
    rows_of = lax.broadcasted_iota(jnp.int32, (count // block, block), 0)
    token = rows_of * block + lax.broadcasted_iota(jnp.int32, (count // block, block), 1)

    def arrive(q, carry):
        start, found = carry
        slot = slot_ref[q]
        b = slot // per_block
        arrival_ref[slot] = start
        turn = lax.rem(chosen_of(b, place_of) - place + req_count, req_count)
        first = turn * block + begin_ref[slot]
        found = jnp.where(token >= start, first + token - start, found)
        return start + lengths_ref[b, slot - b * per_block], found

    _, ring_row = lax.fori_loop(0, requests, arrive, (jnp.int32(0), jnp.zeros_like(token)))

    def to_column(row):
        size = row.shape[1]
        here = lax.broadcasted_iota(jnp.int32, (size, size), 0)
        there = lax.broadcasted_iota(jnp.int32, (size, size), 1)
        return jnp.sum(jnp.where(here == there, row.astype(jnp.float32), 0.0), axis=1, keepdims=True).astype(jnp.int32)

    columns = [to_column(ring_row[r : r + 1]) for r in range(count // block)]
    each = shard // block
    for dy in range(ny):
        for dc in range(2):
            owner = partner(kv, dy, dc, ny)
            for part in range(each):
                column = columns[part]
                for other in range(1, kv_count):
                    column = jnp.where(owner == other, columns[other * each + part], column)
                row_ref[pl.ds((2 * dy + dc) * shard + part * block, block), :] = column

    def tokens_of(b):
        wanted = jnp.zeros_like(lanes)
        for j in range(per_block):
            at = b * per_block + j
            start = begin_ref[at]
            wanted = jnp.where(lanes >= start, arrival_ref[at] + lanes - start, wanted)
        return wanted

    for k in range(req_count):
        wanted = tokens_of(ring_ref[lax.rem(place + k, req_count)])
        owner = jnp.zeros_like(wanted)
        for other in range(1, kv_count):
            owner = owner + (wanted >= other * shard).astype(jnp.int32)
        turn = kv // 2 - owner // 2
        turn = jnp.where(turn < 0, turn + ny, turn)
        slot = 2 * turn + lax.rem(kv + owner, 2)
        tok_ref[k * block : (k + 1) * block, :] = to_column(wanted + (slot - owner) * shard)
    position = jnp.zeros_like(lanes)
    for j in range(per_block):
        start = begin_ref[req * per_block + j]
        position = jnp.where(lanes >= start, filled_ref[req, j] + lanes - start, position)
    index = lax.broadcasted_iota(jnp.int32, (1, head_size), 1)
    half = head_size // 2
    pair = jnp.where(index >= half, index - half, index).astype(jnp.float32)
    frequency = jnp.exp(-(pair * (2.0 / head_size)) * math.log(rope_base))
    angles = to_column(position).astype(jnp.float32) * frequency
    cos_ref[...] = jnp.cos(angles)
    sine = jnp.sin(angles)
    sin_ref[...] = jnp.where(index >= half, sine, -sine)


def plan_call(new_lengths, cache_lengths, request_slot, shard, head_size):
    req_count = lax.axis_size("req")
    kv_count = lax.axis_size("kv")
    ring, _, _, place_of = ring_of(req_count)
    block = shard * kv_count // req_count
    smem = pl.BlockSpec(memory_space=pltpu.SMEM)
    vmem = pl.BlockSpec(memory_space=pltpu.VMEM)
    requests = request_slot.shape[0]
    angles = jax.ShapeDtypeStruct((block, head_size), jnp.float32)
    return pl.pallas_call(
        functools.partial(plan_kernel, (req_count, kv_count, ring, place_of)),
        out_shape=(
            jax.ShapeDtypeStruct((req_count * block, 1), jnp.int32),
            jax.ShapeDtypeStruct((kv_count * shard, 1), jnp.int32),
            angles,
            angles,
        ),
        in_specs=[smem, smem, smem],
        out_specs=(vmem, vmem, vmem, vmem),
        scratch_shapes=[
            pltpu.SMEM((requests,), jnp.int32),
            pltpu.SMEM((requests,), jnp.int32),
            pltpu.SMEM((req_count,), jnp.int32),
        ],
    )(new_lengths, cache_lengths, request_slot)


def attention_kernel(
    group_size, key_block, small, lengths_ref, filled_ref, rotated_ref, stored_hbm, out_ref,
    raw, staged, keys, values, scores, copy_sem,
):
    slots = stored_hbm.shape[0]
    heads = keys.shape[0]
    block = rotated_ref.shape[0]
    head_size = keys.shape[2]
    stride = 2 * heads
    tokens = min(32, block)
    rows = tokens * group_size
    copied = staged.shape[0] // stride
    here = lax.axis_index("req")
    scale = math.log2(math.e) / math.sqrt(head_size)
    span = (group_size + 2) * head_size
    contract_last = (((1,), (1,)), ((), ()))

    def load(slot, index):
        at = pl.ds(pl.multiple_of(index * copied * stride, copied * stride), copied * stride)
        return pltpu.make_async_copy(
            stored_hbm.at[slot, at], raw.at[slot, at], copy_sem.at[slot, index]
        )

    def blocks_of(slot):
        return (filled_ref[here, slot] + copied - 1) // copied

    def begin(slot, carry):
        def one(index, inner):
            load(slot, index).start()
            return inner

        return lax.fori_loop(0, blocks_of(slot), one, carry)

    lax.fori_loop(0, slots, begin, 0)

    def lane_fold(op, value):
        folded = value[:, :head_size]
        for part in range(1, value.shape[1] // head_size):
            folded = op(folded, value[:, part * head_size : (part + 1) * head_size])
        return folded

    def one_slot(slot, start):
        end = start + lengths_ref[here, slot]
        cached = filled_ref[here, slot]

        def split(index, inner):
            load(slot, index).wait()
            base = pl.multiple_of(index * copied, copied)
            staged[...] = raw[
                slot, pl.ds(pl.multiple_of(base * stride, copied * stride), copied * stride), :
            ].astype(jnp.float32)
            for head in range(heads):
                keys[head, pl.ds(base, copied), :] = staged[
                    pl.ds(head, copied, stride=stride), :
                ].astype(jnp.bfloat16)
                values[head, pl.ds(base, copied), :] = staged[
                    pl.ds(heads + head, copied, stride=stride), :
                ].astype(jnp.bfloat16)
            return inner

        lax.fori_loop(0, blocks_of(slot), split, 0)
        whole = cached // key_block
        first_part = whole * (key_block // small)
        last_part = (cached + small - 1) // small

        def one_chunk(chunk, inner):
            at = pl.ds(pl.multiple_of(chunk * tokens, tokens), tokens)
            token = chunk * tokens + lax.rem(
                lax.broadcasted_iota(jnp.int32, (rows, block), 0), tokens
            )
            other = lax.broadcasted_iota(jnp.int32, (rows, block), 1)
            allowed = (other <= token) & (other >= start)
            queries, owns = [], []
            for head in range(heads):
                query = jnp.concatenate(
                    [
                        rotated_ref[at, head * span + g * head_size : head * span + (g + 1) * head_size]
                        for g in range(group_size)
                    ],
                    axis=0,
                )
                new_key = rotated_ref[:, head * span + group_size * head_size : head * span + (group_size + 1) * head_size]
                own = lax.dot_general(
                    query, new_key, contract_last, preferred_element_type=jnp.float32
                )
                queries.append(query)
                owns.append(jnp.where(allowed, own, -jnp.inf))

            def score(head, first, width):
                return lax.dot_general(
                    queries[head],
                    keys[head, pl.ds(first, width), :],
                    contract_last,
                    preferred_element_type=jnp.float32,
                )

            def fill(index, highest):
                first = pl.multiple_of(index * key_block, key_block)
                found = [score(head, first, key_block) for head in range(heads)]
                for head in range(heads):
                    scores[head, :, pl.ds(first, key_block)] = found[head]
                return tuple(
                    jnp.maximum(highest[head], lane_fold(jnp.maximum, found[head]))
                    for head in range(heads)
                )

            def fill_part(index, highest):
                first = pl.multiple_of(index * small, small)
                places = lax.broadcasted_iota(jnp.int32, (rows, small), 1)
                found = [
                    jnp.where(places < cached - first, score(head, first, small), -jnp.inf)
                    for head in range(heads)
                ]
                for head in range(heads):
                    scores[head, :, pl.ds(first, small)] = found[head]
                return tuple(
                    jnp.maximum(highest[head], lane_fold(jnp.maximum, found[head]))
                    for head in range(heads)
                )

            highest = tuple(lane_fold(jnp.maximum, owns[head]) for head in range(heads))
            highest = lax.fori_loop(0, whole, fill, highest)
            highest = lax.fori_loop(first_part, last_part, fill_part, highest)
            tops = [jnp.max(highest[head], axis=1, keepdims=True) for head in range(heads)]
            state = []
            for head in range(heads):
                weights = jnp.exp2((owns[head] - tops[head]) * scale)
                new_value = rotated_ref[:, head * span + (group_size + 1) * head_size : (head + 1) * span]
                state.append(lane_fold(jnp.add, weights))
                state.append(
                    jnp.dot(
                        weights.astype(jnp.bfloat16), new_value, preferred_element_type=jnp.float32
                    )
                )

            def accumulate(width):
                def body(index, state):
                    first = pl.multiple_of(index * width, width)
                    result = []
                    for head in range(heads):
                        weights = jnp.exp2(
                            (scores[head, :, pl.ds(first, width)] - tops[head]) * scale
                        )
                        added = jnp.dot(
                            weights.astype(jnp.bfloat16),
                            values[head, pl.ds(first, width), :],
                            preferred_element_type=jnp.float32,
                        )
                        result.append(state[2 * head] + lane_fold(jnp.add, weights))
                        result.append(state[2 * head + 1] + added)
                    return tuple(result)

                return body

            state = lax.fori_loop(0, whole, accumulate(key_block), tuple(state))
            state = lax.fori_loop(first_part, last_part, accumulate(small), state)
            member_token = chunk * tokens + lax.broadcasted_iota(jnp.int32, (tokens, head_size), 0)
            member = (member_token >= start) & (member_token < end)
            for head in range(heads):
                total = jnp.sum(state[2 * head], axis=1, keepdims=True)
                made = state[2 * head + 1] / total
                for g in range(group_size):
                    columns = slice(
                        (head * group_size + g) * head_size, (head * group_size + g + 1) * head_size
                    )
                    old = out_ref[at, columns].astype(jnp.float32)
                    out_ref[at, columns] = jnp.where(
                        member, made[g * tokens : (g + 1) * tokens], old
                    ).astype(jnp.bfloat16)
            return inner

        lax.fori_loop(start // tokens, (end + tokens - 1) // tokens, one_chunk, 0)
        return end

    lax.fori_loop(0, slots, one_slot, 0)


def block_attention(rotated, cache_entries, new_lengths, cache_lengths, group_size):
    slots, slot_length, heads, both = cache_entries.shape
    head_size = both // 2
    block = rotated.shape[0]
    key_block = min(4096, slot_length)
    small = min(256, key_block)
    copied = min(512, slot_length)
    stored = jnp.transpose(
        cache_entries.reshape(slots, slot_length, heads, 2, head_size), (0, 1, 3, 2, 4)
    ).reshape(slots, slot_length * 2 * heads, head_size)
    rows = min(32, block) * group_size
    grid_spec = pltpu.PrefetchScalarGridSpec(
        num_scalar_prefetch=2,
        grid=(1,),
        in_specs=[
            pl.BlockSpec(rotated.shape, lambda i, s, c: (0, 0)),
            pl.BlockSpec(memory_space=pl.ANY),
        ],
        out_specs=pl.BlockSpec((block, heads * group_size * head_size), lambda i, s, c: (0, 0)),
        scratch_shapes=[
            pltpu.VMEM((slots, slot_length * 2 * heads, head_size), jnp.bfloat16),
            pltpu.VMEM((copied * 2 * heads, head_size), jnp.float32),
            pltpu.VMEM((heads, slot_length, head_size), jnp.bfloat16),
            pltpu.VMEM((heads, slot_length, head_size), jnp.bfloat16),
            pltpu.VMEM((heads, rows, slot_length), jnp.float32),
            pltpu.SemaphoreType.DMA((slots, slot_length // copied)),
        ],
    )
    return pl.pallas_call(
        functools.partial(attention_kernel, group_size, key_block, small),
        grid_spec=grid_spec,
        out_shape=jax.ShapeDtypeStruct((block, heads * group_size * head_size), jnp.bfloat16),
        compiler_params=pltpu.CompilerParams(vmem_limit_bytes=56 << 20),
    )(new_lengths, cache_lengths, rotated, stored)


MESH = pl.DeviceIdType.MESH


def chosen_of(index, table):
    found = jnp.int32(table[0])
    for place in range(1, len(table)):
        found = jnp.where(index == place, jnp.int32(table[place]), found)
    return found


def ring_of(count):
    across = 1
    while 4 * across * across <= count:
        across *= 2
    along = count // across
    ring = [place * across for place in range(along)]
    for turn, place in enumerate(reversed(range(along))):
        row = [place * across + step for step in range(1, across)]
        ring += row if turn % 2 == 0 else row[::-1]
    ahead = [0] * count
    behind = [0] * count
    place_of = [0] * count
    for i in range(count):
        ahead[ring[i]] = ring[(i + 1) % count]
        behind[ring[i]] = ring[(i - 1) % count]
        place_of[ring[i]] = i
    return ring, ahead, behind, place_of


def enter(req_count, kv_count):
    req = lax.axis_index("req")
    kv = lax.axis_index("kv")
    barrier = pltpu.get_barrier_semaphore()
    for step in range(1, req_count):
        pl.semaphore_signal(
            barrier, inc=1, device_id=(lax.rem(req + step, req_count), kv), device_id_type=MESH
        )
    for step in range(1, kv_count):
        pl.semaphore_signal(
            barrier, inc=1, device_id=(req, lax.rem(kv + step, kv_count)), device_id_type=MESH
        )
    pl.semaphore_wait(barrier, req_count + kv_count - 2)
    return req, kv


def column_to_row(column):
    count = column.shape[0]
    here = lax.broadcasted_iota(jnp.int32, (count, count), 0)
    there = lax.broadcasted_iota(jnp.int32, (count, count), 1)
    return jnp.sum(jnp.where(here == there, column, 0.0), axis=0, keepdims=True)


def row_to_column(row):
    count = row.shape[1]
    here = lax.broadcasted_iota(jnp.int32, (count, count), 0)
    there = lax.broadcasted_iota(jnp.int32, (count, count), 1)
    return jnp.sum(jnp.where(here == there, row, 0.0), axis=1, keepdims=True)


def partner(kv, dy, dc, ny):
    return lax.rem(kv // 2 + dy, ny) * 2 + lax.rem(kv + dc, 2)


def qkv_kernel(
    sizes,
    x_hbm,
    gain_ref,
    tok_ref,
    w_hbm,
    cos_ref,
    sin_ref,
    out_ref,
    x_all,
    w_all,
    picks,
    rates,
    normed,
    squares,
    squares_in,
    totals_in,
    land,
    leave,
    steps_in,
    steps_out,
    local_sem,
    square_sem,
    total_sem,
    gather_sem,
    share_sem,
    ring_sem,
    step_sem,
):
    req_count, kv_count, group_size, head_size, pieces, ahead_of, behind_of = sizes
    ny = kv_count // 2
    shard = x_hbm.shape[0]
    width = x_hbm.shape[1]
    block = out_ref.shape[0]
    w_copy = pltpu.make_async_copy(w_hbm, w_all, local_sem.at[0])
    x_copy = pltpu.make_async_copy(x_hbm, x_all.at[0], local_sem.at[1])
    x_copy.start()
    w_copy.start()
    req, kv = enter(req_count, kv_count)
    x_copy.wait()
    chunk = shard // 2

    def gather_copy(dy, part):
        rows = pl.ds(part * chunk, chunk)
        return pltpu.make_async_remote_copy(
            src_ref=x_all.at[0, rows],
            dst_ref=x_all.at[2 * dy, rows],
            send_sem=gather_sem.at[0, dy, part],
            recv_sem=gather_sem.at[1, dy, part],
            device_id=(req, partner(kv, dy, 0, ny)),
            device_id_type=MESH,
        )

    def share_copy(dy, part):
        rows = pl.ds(part * chunk, chunk)
        return pltpu.make_async_remote_copy(
            src_ref=x_all.at[2 * dy, rows],
            dst_ref=x_all.at[2 * dy + 1, rows],
            send_sem=share_sem.at[0, dy, part],
            recv_sem=share_sem.at[1, dy, part],
            device_id=(req, partner(kv, 0, 1, ny)),
            device_id_type=MESH,
        )

    def square_copy(step):
        return pltpu.make_async_remote_copy(
            src_ref=squares.at[0],
            dst_ref=squares_in.at[step],
            send_sem=square_sem.at[0, step],
            recv_sem=square_sem.at[1, step],
            device_id=(lax.rem(req + step, req_count), kv),
            device_id_type=MESH,
        )

    def total_copy(dy, dc):
        slot = 2 * dy + dc
        return pltpu.make_async_remote_copy(
            src_ref=squares.at[1],
            dst_ref=totals_in.at[slot],
            send_sem=total_sem.at[0, slot],
            recv_sem=total_sem.at[1, slot],
            device_id=(req, partner(kv, dy, dc, ny)),
            device_id_type=MESH,
        )

    for part in range(2):
        for dy in range(1, ny):
            gather_copy(dy, part).start()
    x_own = x_all[0].astype(jnp.float32)
    own = column_to_row(jnp.sum(x_own * x_own, axis=1, keepdims=True))
    squares[0] = jnp.broadcast_to(own, squares.shape[1:])
    for step in range(1, req_count):
        square_copy(step).start()
    for part in range(2):
        share_copy(0, part).start()
    total = squares[0]
    for step in range(1, req_count):
        square_copy(step).wait_recv()
        total = total + squares_in[step]
    squares[1] = total
    others = [(dy, dc) for dy in range(ny) for dc in range(2) if dy or dc]
    for dy, dc in others:
        total_copy(dy, dc).start()
    rate_rows = [None] * kv_count
    rate_rows[0] = lax.rsqrt(total[0:1] / (width * req_count) + epsilon_norm)
    for dy, dc in others:
        total_copy(dy, dc).wait_recv()
        rate_rows[2 * dy + dc] = lax.rsqrt(
            totals_in[2 * dy + dc, 0:1] / (width * req_count) + epsilon_norm
        )
    def pick_rows(k, carry):
        at = pl.ds(pl.multiple_of(k * block, block), block)
        wanted = tok_ref[at, :]
        rate = jnp.zeros((block, 1), jnp.float32)
        for slot in range(kv_count):
            places = lax.broadcasted_iota(jnp.int32, (block, shard), 1) + slot * shard
            pick = wanted == places
            rate = rate + jnp.sum(jnp.where(pick, rate_rows[slot], 0.0), axis=1, keepdims=True)
            picks[at, slot * shard : (slot + 1) * shard] = jnp.where(pick, 1.0, 0.0).astype(
                jnp.bfloat16
            )
        rates[at, :] = rate
        return carry

    lax.fori_loop(0, req_count, pick_rows, 0)
    for part in range(2):
        for dy in range(1, ny):
            gather_copy(dy, part).wait_recv()
            share_copy(dy, part).start()
    for dy in range(ny):
        for part in range(2):
            share_copy(dy, part).wait_recv()
    w_copy.wait()
    rows_of_all = x_all[...].reshape(kv_count * shard, width)

    def normalise(k):
        at = pl.ds(pl.multiple_of(k * block, block), block)
        rows = jnp.dot(picks[at, :], rows_of_all, preferred_element_type=jnp.float32)
        normed[at, :] = (rows * rates[at, :] * gain_ref[...]).astype(jnp.bfloat16)

    def product(k, first, last):
        at = pl.ds(pl.multiple_of(k * block, block), block)
        return jnp.dot(normed[at, :], w_all[:, first:last], preferred_element_type=jnp.float32)

    targets = (chosen_of(req, ahead_of), chosen_of(req, behind_of))

    def ring_copy(step, piece):
        way, first, last = pieces[piece]
        columns = pl.ds(first, last - first)
        return pltpu.make_async_remote_copy(
            src_ref=leave.at[step, :, columns],
            dst_ref=land.at[step, :, columns],
            send_sem=ring_sem.at[0, step, piece],
            recv_sem=ring_sem.at[1, step, piece],
            device_id=(targets[way], kv),
            device_id_type=MESH,
        )

    def step_copy(step, piece):
        return pltpu.make_async_remote_copy(
            src_ref=steps_out.at[step, piece],
            dst_ref=steps_in.at[step, piece],
            send_sem=step_sem.at[0, step, piece],
            recv_sem=step_sem.at[1, step, piece],
            device_id=(targets[pieces[piece][0]], kv),
            device_id_type=MESH,
        )

    def pass_on(step, piece, value):
        way, first, last = pieces[piece]
        top = jnp.maximum(jnp.max(jnp.abs(value), axis=1, keepdims=True), 1e-30)
        steps_out[step, piece] = jnp.broadcast_to(
            column_to_row(top * (1.0 / 32767.0)), steps_out.shape[2:]
        )
        step_copy(step, piece).start()
        codes = jnp.floor(value * (32767.0 / top) + 0.5).astype(jnp.int32)
        leave[step, :, first:last] = codes.astype(jnp.int16)
        ring_copy(step, piece).start()

    def arrived(step, piece):
        way, first, last = pieces[piece]
        step_copy(step, piece).wait_recv()
        unit = row_to_column(steps_in[step, piece, 0:1])
        ring_copy(step, piece).wait_recv()
        codes = land[step, :, first:last].astype(jnp.int32)
        return codes.astype(jnp.float32) * unit

    order = sorted(range(len(pieces)), key=lambda p: p % 2)
    normalise(req_count - 1)
    normalise(1)
    for piece in range(len(pieces)):
        way, first, last = pieces[piece]
        pass_on(0, piece, product(1 if way else req_count - 1, first, last))

    def rest(k, carry):
        normalise(lax.rem(k, req_count))
        return carry

    lax.fori_loop(2, req_count - 1, rest, 0)
    normalise(0)

    def one_step(step, carry):
        for piece in order:
            way, first, last = pieces[piece]
            k = 2 + step if way else req_count - 2 - step
            added = product(k, first, last)
            pass_on(step + 1, piece, arrived(step, piece) + added)
        return carry

    lax.fori_loop(0, req_count - 2, one_step, 0)
    half = head_size // 2
    for piece in order:
        way, first, last = pieces[piece]
        added = product(0, first, last)
        summed = arrived(req_count - 2, piece) + added
        for place in range((last - first) // head_size):
            vector = summed[:, place * head_size : (place + 1) * head_size]
            start = first + place * head_size
            if (start // head_size) % (group_size + 2) <= group_size:
                vector = vector * cos_ref[...] + pltpu.roll(vector, half, 1) * sin_ref[...]
            out_ref[:, start : start + head_size] = vector.astype(jnp.bfloat16)

    for dy in range(1, ny):
        for part in range(2):
            gather_copy(dy, part).wait_send()
    for dy in range(ny):
        for part in range(2):
            share_copy(dy, part).wait_send()
    for step in range(1, req_count):
        square_copy(step).wait_send()
    for dy, dc in others:
        total_copy(dy, dc).wait_send()

    def sent(step, carry):
        for piece in range(len(pieces)):
            ring_copy(step, piece).wait_send()
            step_copy(step, piece).wait_send()
        return carry

    lax.fori_loop(0, req_count - 1, sent, 0)


def qkv_call(x, gain, tok, weight, head_size, cosine, sine, heads, group_size):
    req_count = lax.axis_size("req")
    kv_count = lax.axis_size("kv")
    ring, ahead_of, behind_of, place_of = ring_of(req_count)
    shard, width = x.shape
    columns = heads * (group_size + 2) * head_size
    block = shard * kv_count // req_count
    vectors = columns // head_size
    half = vectors // 2
    pieces = []
    for way in range(2):
        middle = way * half + (half + 1) // 2
        pieces.append((way, way * half * head_size, middle * head_size))
        pieces.append((way, middle * head_size, (way + 1) * half * head_size))
    sizes = (req_count, kv_count, group_size, head_size, pieces, ahead_of, behind_of)
    vmem = pl.BlockSpec(memory_space=pltpu.VMEM)
    anywhere = pl.BlockSpec(memory_space=pl.ANY)
    dma = pltpu.SemaphoreType.DMA
    return pl.pallas_call(
        functools.partial(qkv_kernel, sizes),
        out_shape=jax.ShapeDtypeStruct((block, columns), jnp.bfloat16),
        in_specs=[anywhere, vmem, vmem, anywhere, vmem, vmem],
        out_specs=vmem,
        scratch_shapes=[
            pltpu.VMEM((kv_count, shard, width), jnp.bfloat16),
            pltpu.VMEM((width, columns), jnp.bfloat16),
            pltpu.VMEM((kv_count * shard, kv_count * shard), jnp.bfloat16),
            pltpu.VMEM((kv_count * shard, 1), jnp.float32),
            pltpu.VMEM((kv_count * shard, width), jnp.bfloat16),
            pltpu.VMEM((2, 8, shard), jnp.float32),
            pltpu.VMEM((req_count, 8, shard), jnp.float32),
            pltpu.VMEM((kv_count, 8, shard), jnp.float32),
            pltpu.VMEM((req_count - 1, block, columns), jnp.int16),
            pltpu.VMEM((req_count - 1, block, columns), jnp.int16),
            pltpu.VMEM((req_count - 1, len(pieces), 8, block), jnp.float32),
            pltpu.VMEM((req_count - 1, len(pieces), 8, block), jnp.float32),
            dma((2,)),
            dma((2, req_count)),
            dma((2, kv_count)),
            dma((2, kv_count // 2, 2)),
            dma((2, kv_count // 2, 2)),
            dma((2, req_count - 1, len(pieces))),
            dma((2, req_count - 1, len(pieces))),
        ],
        compiler_params=pltpu.CompilerParams(
            collective_id=0, has_side_effects=True, vmem_limit_bytes=56 << 20
        ),
    )(x, gain, tok, weight, cosine, sine)


def out_kernel(
    sizes,
    att_hbm,
    w_hbm,
    x_ref,
    gain_ref,
    row_ref,
    projected_ref,
    normed_ref,
    att,
    w_all,
    products,
    picks,
    taken,
    mine,
    lent,
    borrowed,
    crossing,
    crossed,
    squares,
    squares_in,
    local_sem,
    ring_sem,
    lend_sem,
    cross_sem,
    square_sem,
):
    req_count, kv_count, ahead_of, behind_of = sizes
    ny = kv_count // 2
    block = att_hbm.shape[0]
    inner = att_hbm.shape[1]
    shard, width = x_ref.shape
    att_copy = pltpu.make_async_copy(att_hbm, att.at[0], local_sem.at[0])
    w_copy = pltpu.make_async_copy(w_hbm, w_all, local_sem.at[1])
    att_copy.start()
    w_copy.start()
    req, kv = enter(req_count, kv_count)
    att_copy.wait()
    targets = (chosen_of(req, ahead_of), chosen_of(req, behind_of))
    half_way = req_count // 2
    wide = inner // 2

    def ring_copy(step, way, part):
        source = (lax.rem(req_count - step + 1, req_count), step - 1)[way]
        target = (req_count - step, step)[way]
        columns = pl.ds(part * wide, wide)
        return pltpu.make_async_remote_copy(
            src_ref=att.at[source, :, columns],
            dst_ref=att.at[target, :, columns],
            send_sem=ring_sem.at[0, step, way, part],
            recv_sem=ring_sem.at[1, step, way, part],
            device_id=(targets[way], kv),
            device_id_type=MESH,
        )

    def multiply(k):
        at = pl.ds(k * block, block)
        products[at, :] = jnp.dot(
            att[k], w_all[...], preferred_element_type=jnp.float32
        ).astype(jnp.bfloat16)

    for part in range(2):
        for way in range(2):
            if half_way > 1 or part == way:
                ring_copy(1, way, part).start()
    w_copy.wait()
    multiply(0)
    rows_total = req_count * block
    groups = [(dy, dc, part) for dy in range(ny) for dc in range(2) for part in range(2)]
    count = shard // 2

    def pick_rows(index, carry):
        wanted = row_ref[pl.ds(pl.multiple_of(index * count, count), count), :]
        places = lax.broadcasted_iota(jnp.int32, (count, rows_total), 1)
        picks[pl.ds(pl.multiple_of(index * count, count), count), :] = jnp.where(
            wanted == places, 1.0, 0.0
        ).astype(jnp.bfloat16)
        return carry

    lax.fori_loop(0, len(groups), pick_rows, 0)
    for step in range(1, half_way):
        for part in range(2):
            for way in range(2):
                ring_copy(step, way, part).wait_recv()
                if step + 1 < half_way or part == way:
                    ring_copy(step + 1, way, part).start()
        multiply(req_count - step)
        multiply(step)
    products[half_way * block : (half_way + 1) * block, :] = jnp.zeros((block, width), jnp.bfloat16)

    def take(index, carry):
        at = pl.ds(pl.multiple_of(index * count, count), count)
        taken[at, :] = jnp.dot(
            picks[at, :], products[...], preferred_element_type=jnp.float32
        )
        return carry

    lax.fori_loop(0, len(groups), take, 0)
    for way in range(2):
        ring_copy(half_way, way, way).wait_recv()
    multiply(half_way)

    def gathered(dy, dc, part):
        at = groups.index((dy, dc, part)) * count
        return taken[at : at + count, :] + jnp.dot(
            picks[at : at + count, half_way * block : (half_way + 1) * block],
            products[half_way * block : (half_way + 1) * block, :],
            preferred_element_type=jnp.float32,
        )

    def lend_copy(dy, part):
        rows = pl.ds(part * count, count)
        return pltpu.make_async_remote_copy(
            src_ref=lent.at[dy, rows],
            dst_ref=borrowed.at[dy, rows],
            send_sem=lend_sem.at[0, dy, part],
            recv_sem=lend_sem.at[1, dy, part],
            device_id=(req, partner(kv, 0, 1, ny)),
            device_id_type=MESH,
        )

    def cross_copy(dy, part):
        rows = pl.ds(part * count, count)
        return pltpu.make_async_remote_copy(
            src_ref=crossing.at[dy, rows],
            dst_ref=crossed.at[dy, rows],
            send_sem=cross_sem.at[0, dy, part],
            recv_sem=cross_sem.at[1, dy, part],
            device_id=(req, partner(kv, dy, 0, ny)),
            device_id_type=MESH,
        )

    def part_rows(part):
        return slice(part * (shard // 2), (part + 1) * (shard // 2))

    turns = [(dy, part) for dy in list(range(1, ny)) + [0] for part in range(2)]
    for dy, part in turns:
        lent[dy, part_rows(part)] = gathered(dy, 1, part).astype(jnp.bfloat16)
        lend_copy(dy, part).start()
        if dy:
            own = gathered(dy, 0, part)
            lend_copy(dy, part).wait_recv()
            crossing[dy, part_rows(part)] = (
                own + borrowed[dy, part_rows(part)].astype(jnp.float32)
            ).astype(jnp.bfloat16)
            cross_copy(dy, part).start()
    for part in range(2):
        mine[part_rows(part)] = gathered(0, 0, part)
    sums = []
    for part in range(2):
        lend_copy(0, part).wait_recv()
        projection = mine[part_rows(part)] + borrowed[0, part_rows(part)].astype(jnp.float32)
        for dy in range(1, ny):
            cross_copy(dy, part).wait_recv()
            projection = projection + crossed[dy, part_rows(part)].astype(jnp.float32)
        projected_ref[part_rows(part)] = projection.astype(jnp.bfloat16)
        residual = x_ref[part_rows(part)].astype(jnp.float32) + projection
        mine[part_rows(part)] = residual
        sums.append(column_to_row(jnp.sum(residual * residual, axis=1, keepdims=True)))
    squares[...] = jnp.broadcast_to(jnp.concatenate(sums, axis=1), squares.shape)

    def square_copy(step):
        return pltpu.make_async_remote_copy(
            src_ref=squares,
            dst_ref=squares_in.at[step],
            send_sem=square_sem.at[0, step],
            recv_sem=square_sem.at[1, step],
            device_id=(lax.rem(req + step, req_count), kv),
            device_id_type=MESH,
        )

    for step in range(1, req_count):
        square_copy(step).start()
    total = squares[...]
    for step in range(1, req_count):
        square_copy(step).wait_recv()
        total = total + squares_in[step]
    rate = row_to_column(lax.rsqrt(total[0:1] / (width * req_count) + epsilon_norm))
    normed_ref[...] = (mine[...] * rate * gain_ref[...]).astype(jnp.bfloat16)

    for step in range(1, half_way + 1):
        for part in range(2):
            for way in range(2):
                if step < half_way or part == way:
                    ring_copy(step, way, part).wait_send()
    for dy, part in turns:
        lend_copy(dy, part).wait_send()
        if dy:
            cross_copy(dy, part).wait_send()
    for step in range(1, req_count):
        square_copy(step).wait_send()


def out_call(attention, weight, x, gain, rows):
    req_count = lax.axis_size("req")
    kv_count = lax.axis_size("kv")
    ring, ahead_of, behind_of, place_of = ring_of(req_count)
    block, inner = attention.shape
    shard, width = x.shape
    ny = kv_count // 2
    vmem = pl.BlockSpec(memory_space=pltpu.VMEM)
    anywhere = pl.BlockSpec(memory_space=pl.ANY)
    dma = pltpu.SemaphoreType.DMA
    made = jax.ShapeDtypeStruct((shard, width), jnp.bfloat16)
    return pl.pallas_call(
        functools.partial(out_kernel, (req_count, kv_count, ahead_of, behind_of)),
        out_shape=(made, made),
        in_specs=[anywhere, anywhere, vmem, vmem, vmem],
        out_specs=(vmem, vmem),
        scratch_shapes=[
            pltpu.VMEM((req_count, block, inner), jnp.bfloat16),
            pltpu.VMEM((inner, width), jnp.bfloat16),
            pltpu.VMEM((req_count * block, width), jnp.bfloat16),
            pltpu.VMEM((kv_count * shard, req_count * block), jnp.bfloat16),
            pltpu.VMEM((kv_count * shard, width), jnp.float32),
            pltpu.VMEM((shard, width), jnp.float32),
            pltpu.VMEM((ny, shard, width), jnp.bfloat16),
            pltpu.VMEM((ny, shard, width), jnp.bfloat16),
            pltpu.VMEM((ny, shard, width), jnp.bfloat16),
            pltpu.VMEM((ny, shard, width), jnp.bfloat16),
            pltpu.VMEM((8, shard), jnp.float32),
            pltpu.VMEM((req_count, 8, shard), jnp.float32),
            dma((2,)),
            dma((2, req_count // 2 + 1, 2, 2)),
            dma((2, ny, 2)),
            dma((2, ny, 2)),
            dma((2, req_count)),
        ],
        compiler_params=pltpu.CompilerParams(
            collective_id=1, has_side_effects=True, vmem_limit_bytes=56 << 20
        ),
    )(attention, weight, x, gain, rows)


def per_device(
    activations,
    input_gain,
    qkv_weight,
    out_weight,
    post_gain,
    cache_entries,
    new_lengths,
    cache_lengths,
    request_slot,
):
    req_count = lax.axis_size("req")
    kv_count = lax.axis_size("kv")
    shard, width_slice = activations.shape
    kvh_local = qkv_weight.shape[1]
    head_size = cache_entries.shape[3] // 2
    vectors = qkv_weight.shape[2] // head_size
    group_size = vectors - 2
    tok_blk = shard * kv_count // req_count
    tok, rows, cosine, sine = plan_call(
        new_lengths, cache_lengths, request_slot, shard, head_size
    )
    rotated = qkv_call(
        activations,
        input_gain.astype(jnp.float32).reshape(1, -1),
        tok,
        qkv_weight.reshape(width_slice, -1),
        head_size,
        cosine,
        sine,
        kvh_local,
        group_size,
    )
    appended = rotated.reshape(tok_blk, kvh_local, vectors, head_size)[
        :, :, group_size:, :
    ].reshape(tok_blk, kvh_local, 2 * head_size)
    attention = block_attention(rotated, cache_entries, new_lengths, cache_lengths, group_size)
    projected, normed = out_call(
        attention,
        out_weight.reshape(-1, width_slice),
        activations,
        post_gain.astype(jnp.float32).reshape(1, -1),
        rows,
    )
    return (projected, normed, appended)


def solution(mesh):
    in_specs = (
        P("kv", "req"),
        P("req"),
        P("req", "kv", None),
        P("kv", None, "req"),
        P("req"),
        P("req", None, "kv", None),
        P(),
        P(),
        P(),
    )
    out_specs = (P("kv", "req"), P("kv", "req"), P("req", "kv", None))
    return jax.shard_map(
        per_device, mesh=mesh, in_specs=in_specs, out_specs=out_specs, check_vma=False
    )
```

```python
import functools
import math

import jax
import jax.numpy as jnp
from jax import lax
from jax.experimental import pallas as pl
from jax.experimental.pallas import tpu as pltpu
from jax.sharding import PartitionSpec as P

epsilon_norm = 1e-05
rope_base = 500000.0


def plan_kernel(
    sizes, lengths_ref, filled_ref, slot_ref, tok_ref, row_ref, cos_ref, sin_ref, begin_ref, arrival_ref, ring_ref
):
    req_count, kv_count, ring, place_of = sizes
    per_block = lengths_ref.shape[1]
    requests = req_count * per_block
    block = cos_ref.shape[0]
    head_size = cos_ref.shape[1]
    shard = row_ref.shape[0] // kv_count
    ny = kv_count // 2
    req = lax.axis_index("req")
    kv = lax.axis_index("kv")
    place = chosen_of(req, place_of)
    for k in range(req_count):
        ring_ref[k] = jnp.int32(ring[k])

    def inside(b, carry):
        start = jnp.int32(0)
        for j in range(per_block):
            begin_ref[b * per_block + j] = start
            start = start + lengths_ref[b, j]
        return carry

    lax.fori_loop(0, req_count, inside, 0)
    lanes = lax.broadcasted_iota(jnp.int32, (1, block), 1)
    count = req_count * block
    rows_of = lax.broadcasted_iota(jnp.int32, (count // block, block), 0)
    token = rows_of * block + lax.broadcasted_iota(jnp.int32, (count // block, block), 1)

    def arrive(q, carry):
        start, found = carry
        slot = slot_ref[q]
        b = slot // per_block
        arrival_ref[slot] = start
        turn = lax.rem(chosen_of(b, place_of) - place + req_count, req_count)
        first = turn * block + begin_ref[slot]
        found = jnp.where(token >= start, first + token - start, found)
        return start + lengths_ref[b, slot - b * per_block], found

    _, ring_row = lax.fori_loop(0, requests, arrive, (jnp.int32(0), jnp.zeros_like(token)))

    def to_column(row):
        size = row.shape[1]
        here = lax.broadcasted_iota(jnp.int32, (size, size), 0)
        there = lax.broadcasted_iota(jnp.int32, (size, size), 1)
        return jnp.sum(jnp.where(here == there, row.astype(jnp.float32), 0.0), axis=1, keepdims=True).astype(jnp.int32)

    columns = [to_column(ring_row[r : r + 1]) for r in range(count // block)]
    each = shard // block
    for dy in range(ny):
        for dc in range(2):
            owner = partner(kv, dy, dc, ny)
            for part in range(each):
                column = columns[part]
                for other in range(1, kv_count):
                    column = jnp.where(owner == other, columns[other * each + part], column)
                row_ref[pl.ds((2 * dy + dc) * shard + part * block, block), :] = column

    def tokens_of(b):
        wanted = jnp.zeros_like(lanes)
        for j in range(per_block):
            at = b * per_block + j
            start = begin_ref[at]
            wanted = jnp.where(lanes >= start, arrival_ref[at] + lanes - start, wanted)
        return wanted

    for k in range(req_count):
        wanted = tokens_of(ring_ref[lax.rem(place + k, req_count)])
        owner = jnp.zeros_like(wanted)
        for other in range(1, kv_count):
            owner = owner + (wanted >= other * shard).astype(jnp.int32)
        turn = kv // 2 - owner // 2
        turn = jnp.where(turn < 0, turn + ny, turn)
        slot = 2 * turn + lax.rem(kv + owner, 2)
        tok_ref[k * block : (k + 1) * block, :] = to_column(wanted + (slot - owner) * shard)
    position = jnp.zeros_like(lanes)
    for j in range(per_block):
        start = begin_ref[req * per_block + j]
        position = jnp.where(lanes >= start, filled_ref[req, j] + lanes - start, position)
    index = lax.broadcasted_iota(jnp.int32, (1, head_size), 1)
    half = head_size // 2
    pair = jnp.where(index >= half, index - half, index).astype(jnp.float32)
    frequency = jnp.exp(-(pair * (2.0 / head_size)) * math.log(rope_base))
    angles = to_column(position).astype(jnp.float32) * frequency
    cos_ref[...] = jnp.cos(angles)
    sine = jnp.sin(angles)
    sin_ref[...] = jnp.where(index >= half, sine, -sine)


def plan_call(new_lengths, cache_lengths, request_slot, shard, head_size):
    req_count = lax.axis_size("req")
    kv_count = lax.axis_size("kv")
    ring, _, _, place_of = ring_of(req_count)
    block = shard * kv_count // req_count
    smem = pl.BlockSpec(memory_space=pltpu.SMEM)
    vmem = pl.BlockSpec(memory_space=pltpu.VMEM)
    requests = request_slot.shape[0]
    angles = jax.ShapeDtypeStruct((block, head_size), jnp.float32)
    return pl.pallas_call(
        functools.partial(plan_kernel, (req_count, kv_count, ring, place_of)),
        out_shape=(
            jax.ShapeDtypeStruct((req_count * block, 1), jnp.int32),
            jax.ShapeDtypeStruct((kv_count * shard, 1), jnp.int32),
            angles,
            angles,
        ),
        in_specs=[smem, smem, smem],
        out_specs=(vmem, vmem, vmem, vmem),
        scratch_shapes=[
            pltpu.SMEM((requests,), jnp.int32),
            pltpu.SMEM((requests,), jnp.int32),
            pltpu.SMEM((req_count,), jnp.int32),
        ],
    )(new_lengths, cache_lengths, request_slot)


def attention_kernel(
    group_size, key_block, small, lengths_ref, filled_ref, rotated_ref, stored_hbm, out_ref,
    raw, staged, keys, values, scores, copy_sem,
):
    slots = stored_hbm.shape[0]
    heads = keys.shape[0]
    block = rotated_ref.shape[0]
    head_size = keys.shape[2]
    stride = 2 * heads
    tokens = min(32, block)
    rows = tokens * group_size
    copied = staged.shape[0] // stride
    here = lax.axis_index("req")
    scale = math.log2(math.e) / math.sqrt(head_size)
    span = (group_size + 2) * head_size
    contract_last = (((1,), (1,)), ((), ()))

    def load(slot, index):
        at = pl.ds(pl.multiple_of(index * copied * stride, copied * stride), copied * stride)
        return pltpu.make_async_copy(
            stored_hbm.at[slot, at], raw.at[slot, at], copy_sem.at[slot, index]
        )

    def blocks_of(slot):
        return (filled_ref[here, slot] + copied - 1) // copied

    def begin(slot, carry):
        def one(index, inner):
            load(slot, index).start()
            return inner

        return lax.fori_loop(0, blocks_of(slot), one, carry)

    lax.fori_loop(0, slots, begin, 0)

    def lane_fold(op, value):
        folded = value[:, :head_size]
        for part in range(1, value.shape[1] // head_size):
            folded = op(folded, value[:, part * head_size : (part + 1) * head_size])
        return folded

    def one_slot(slot, start):
        end = start + lengths_ref[here, slot]
        cached = filled_ref[here, slot]

        def split(index, inner):
            load(slot, index).wait()
            base = pl.multiple_of(index * copied, copied)
            staged[...] = raw[
                slot, pl.ds(pl.multiple_of(base * stride, copied * stride), copied * stride), :
            ].astype(jnp.float32)
            for head in range(heads):
                keys[head, pl.ds(base, copied), :] = staged[
                    pl.ds(head, copied, stride=stride), :
                ].astype(jnp.bfloat16)
                values[head, pl.ds(base, copied), :] = staged[
                    pl.ds(heads + head, copied, stride=stride), :
                ].astype(jnp.bfloat16)
            return inner

        lax.fori_loop(0, blocks_of(slot), split, 0)
        whole = cached // key_block
        first_part = whole * (key_block // small)
        last_part = (cached + small - 1) // small

        def one_chunk(chunk, inner):
            at = pl.ds(pl.multiple_of(chunk * tokens, tokens), tokens)
            token = chunk * tokens + lax.rem(
                lax.broadcasted_iota(jnp.int32, (rows, block), 0), tokens
            )
            other = lax.broadcasted_iota(jnp.int32, (rows, block), 1)
            allowed = (other <= token) & (other >= start)
            queries, owns = [], []
            for head in range(heads):
                query = jnp.concatenate(
                    [
                        rotated_ref[at, head * span + g * head_size : head * span + (g + 1) * head_size]
                        for g in range(group_size)
                    ],
                    axis=0,
                )
                new_key = rotated_ref[:, head * span + group_size * head_size : head * span + (group_size + 1) * head_size]
                own = lax.dot_general(
                    query, new_key, contract_last, preferred_element_type=jnp.float32
                )
                queries.append(query)
                owns.append(jnp.where(allowed, own, -jnp.inf))

            def score(head, first, width):
                return lax.dot_general(
                    queries[head],
                    keys[head, pl.ds(first, width), :],
                    contract_last,
                    preferred_element_type=jnp.float32,
                )

            def fill(index, highest):
                first = pl.multiple_of(index * key_block, key_block)
                found = [score(head, first, key_block) for head in range(heads)]
                for head in range(heads):
                    scores[head, :, pl.ds(first, key_block)] = found[head]
                return tuple(
                    jnp.maximum(highest[head], lane_fold(jnp.maximum, found[head]))
                    for head in range(heads)
                )

            def fill_part(index, highest):
                first = pl.multiple_of(index * small, small)
                places = lax.broadcasted_iota(jnp.int32, (rows, small), 1)
                found = [
                    jnp.where(places < cached - first, score(head, first, small), -jnp.inf)
                    for head in range(heads)
                ]
                for head in range(heads):
                    scores[head, :, pl.ds(first, small)] = found[head]
                return tuple(
                    jnp.maximum(highest[head], lane_fold(jnp.maximum, found[head]))
                    for head in range(heads)
                )

            def finish(state):
                member_token = chunk * tokens + lax.broadcasted_iota(jnp.int32, (tokens, head_size), 0)
                member = (member_token >= start) & (member_token < end)
                for head in range(heads):
                    total = jnp.sum(state[2 * head], axis=1, keepdims=True)
                    made = state[2 * head + 1] / total
                    for g in range(group_size):
                        columns = slice(
                            (head * group_size + g) * head_size, (head * group_size + g + 1) * head_size
                        )
                        old = out_ref[at, columns].astype(jnp.float32)
                        out_ref[at, columns] = jnp.where(
                            member, made[g * tokens : (g + 1) * tokens], old
                        ).astype(jnp.bfloat16)

            @pl.when(cached <= small)
            def _():
                places = lax.broadcasted_iota(jnp.int32, (rows, small), 1)
                state = []
                for head in range(heads):
                    found = jnp.where(places < cached, score(head, 0, small), -jnp.inf)
                    highest = jnp.maximum(
                        lane_fold(jnp.maximum, found), lane_fold(jnp.maximum, owns[head])
                    )
                    top = jnp.max(highest, axis=1, keepdims=True)
                    weights = jnp.exp2((found - top) * scale)
                    own_weights = jnp.exp2((owns[head] - top) * scale)
                    new_value = rotated_ref[:, head * span + (group_size + 1) * head_size : (head + 1) * span]
                    state.append(lane_fold(jnp.add, weights) + lane_fold(jnp.add, own_weights))
                    state.append(
                        jnp.dot(
                            own_weights.astype(jnp.bfloat16),
                            new_value,
                            preferred_element_type=jnp.float32,
                        )
                        + jnp.dot(
                            weights.astype(jnp.bfloat16),
                            values[head, 0:small, :],
                            preferred_element_type=jnp.float32,
                        )
                    )
                finish(state)

            @pl.when(cached > small)
            def _():
                highest = tuple(lane_fold(jnp.maximum, owns[head]) for head in range(heads))
                highest = lax.fori_loop(0, whole, fill, highest)
                highest = lax.fori_loop(first_part, last_part, fill_part, highest)
                tops = [jnp.max(highest[head], axis=1, keepdims=True) for head in range(heads)]
                state = []
                for head in range(heads):
                    weights = jnp.exp2((owns[head] - tops[head]) * scale)
                    new_value = rotated_ref[:, head * span + (group_size + 1) * head_size : (head + 1) * span]
                    state.append(lane_fold(jnp.add, weights))
                    state.append(
                        jnp.dot(
                            weights.astype(jnp.bfloat16), new_value, preferred_element_type=jnp.float32
                        )
                    )

                def accumulate(width):
                    def body(index, state):
                        first = pl.multiple_of(index * width, width)
                        result = []
                        for head in range(heads):
                            weights = jnp.exp2(
                                (scores[head, :, pl.ds(first, width)] - tops[head]) * scale
                            )
                            added = jnp.dot(
                                weights.astype(jnp.bfloat16),
                                values[head, pl.ds(first, width), :],
                                preferred_element_type=jnp.float32,
                            )
                            result.append(state[2 * head] + lane_fold(jnp.add, weights))
                            result.append(state[2 * head + 1] + added)
                        return tuple(result)

                    return body

                state = lax.fori_loop(0, whole, accumulate(key_block), tuple(state))
                state = lax.fori_loop(first_part, last_part, accumulate(small), state)
                finish(state)

            return inner

        lax.fori_loop(start // tokens, (end + tokens - 1) // tokens, one_chunk, 0)
        return end

    lax.fori_loop(0, slots, one_slot, 0)


def block_attention(rotated, cache_entries, new_lengths, cache_lengths, group_size):
    slots, slot_length, heads, both = cache_entries.shape
    head_size = both // 2
    block = rotated.shape[0]
    key_block = min(4096, slot_length)
    small = min(256, key_block)
    copied = min(512, slot_length)
    stored = jnp.transpose(
        cache_entries.reshape(slots, slot_length, heads, 2, head_size), (0, 1, 3, 2, 4)
    ).reshape(slots, slot_length * 2 * heads, head_size)
    rows = min(32, block) * group_size
    grid_spec = pltpu.PrefetchScalarGridSpec(
        num_scalar_prefetch=2,
        grid=(1,),
        in_specs=[
            pl.BlockSpec(rotated.shape, lambda i, s, c: (0, 0)),
            pl.BlockSpec(memory_space=pl.ANY),
        ],
        out_specs=pl.BlockSpec((block, heads * group_size * head_size), lambda i, s, c: (0, 0)),
        scratch_shapes=[
            pltpu.VMEM((slots, slot_length * 2 * heads, head_size), jnp.bfloat16),
            pltpu.VMEM((copied * 2 * heads, head_size), jnp.float32),
            pltpu.VMEM((heads, slot_length, head_size), jnp.bfloat16),
            pltpu.VMEM((heads, slot_length, head_size), jnp.bfloat16),
            pltpu.VMEM((heads, rows, slot_length), jnp.float32),
            pltpu.SemaphoreType.DMA((slots, slot_length // copied)),
        ],
    )
    return pl.pallas_call(
        functools.partial(attention_kernel, group_size, key_block, small),
        grid_spec=grid_spec,
        out_shape=jax.ShapeDtypeStruct((block, heads * group_size * head_size), jnp.bfloat16),
        compiler_params=pltpu.CompilerParams(vmem_limit_bytes=56 << 20),
    )(new_lengths, cache_lengths, rotated, stored)


MESH = pl.DeviceIdType.MESH


def chosen_of(index, table):
    found = jnp.int32(table[0])
    for place in range(1, len(table)):
        found = jnp.where(index == place, jnp.int32(table[place]), found)
    return found


def ring_of(count):
    across = 1
    while 4 * across * across <= count:
        across *= 2
    along = count // across
    ring = [place * across for place in range(along)]
    for turn, place in enumerate(reversed(range(along))):
        row = [place * across + step for step in range(1, across)]
        ring += row if turn % 2 == 0 else row[::-1]
    ahead = [0] * count
    behind = [0] * count
    place_of = [0] * count
    for i in range(count):
        ahead[ring[i]] = ring[(i + 1) % count]
        behind[ring[i]] = ring[(i - 1) % count]
        place_of[ring[i]] = i
    return ring, ahead, behind, place_of


def enter(req_count, kv_count):
    req = lax.axis_index("req")
    kv = lax.axis_index("kv")
    barrier = pltpu.get_barrier_semaphore()
    for step in range(1, req_count):
        pl.semaphore_signal(
            barrier, inc=1, device_id=(lax.rem(req + step, req_count), kv), device_id_type=MESH
        )
    for step in range(1, kv_count):
        pl.semaphore_signal(
            barrier, inc=1, device_id=(req, lax.rem(kv + step, kv_count)), device_id_type=MESH
        )
    pl.semaphore_wait(barrier, req_count + kv_count - 2)
    return req, kv


def column_to_row(column):
    count = column.shape[0]
    here = lax.broadcasted_iota(jnp.int32, (count, count), 0)
    there = lax.broadcasted_iota(jnp.int32, (count, count), 1)
    return jnp.sum(jnp.where(here == there, column, 0.0), axis=0, keepdims=True)


def row_to_column(row):
    count = row.shape[1]
    here = lax.broadcasted_iota(jnp.int32, (count, count), 0)
    there = lax.broadcasted_iota(jnp.int32, (count, count), 1)
    return jnp.sum(jnp.where(here == there, row, 0.0), axis=1, keepdims=True)


def partner(kv, dy, dc, ny):
    return lax.rem(kv // 2 + dy, ny) * 2 + lax.rem(kv + dc, 2)


def qkv_kernel(
    sizes,
    x_hbm,
    gain_ref,
    tok_ref,
    w_hbm,
    cos_ref,
    sin_ref,
    out_ref,
    x_all,
    w_all,
    picks,
    rates,
    normed,
    squares,
    squares_in,
    totals_in,
    land,
    leave,
    steps_in,
    steps_out,
    local_sem,
    square_sem,
    total_sem,
    gather_sem,
    share_sem,
    ring_sem,
    step_sem,
):
    req_count, kv_count, group_size, head_size, pieces, ahead_of, behind_of = sizes
    ny = kv_count // 2
    shard = x_hbm.shape[0]
    width = x_hbm.shape[1]
    block = out_ref.shape[0]
    w_copy = pltpu.make_async_copy(w_hbm, w_all, local_sem.at[0])
    x_copy = pltpu.make_async_copy(x_hbm, x_all.at[0], local_sem.at[1])
    x_copy.start()
    w_copy.start()
    req, kv = enter(req_count, kv_count)
    x_copy.wait()
    chunk = shard // 2

    def gather_copy(dy, part):
        rows = pl.ds(part * chunk, chunk)
        return pltpu.make_async_remote_copy(
            src_ref=x_all.at[0, rows],
            dst_ref=x_all.at[2 * dy, rows],
            send_sem=gather_sem.at[0, dy, part],
            recv_sem=gather_sem.at[1, dy, part],
            device_id=(req, partner(kv, dy, 0, ny)),
            device_id_type=MESH,
        )

    def share_copy(dy, part):
        rows = pl.ds(part * chunk, chunk)
        return pltpu.make_async_remote_copy(
            src_ref=x_all.at[2 * dy, rows],
            dst_ref=x_all.at[2 * dy + 1, rows],
            send_sem=share_sem.at[0, dy, part],
            recv_sem=share_sem.at[1, dy, part],
            device_id=(req, partner(kv, 0, 1, ny)),
            device_id_type=MESH,
        )

    def square_copy(step):
        return pltpu.make_async_remote_copy(
            src_ref=squares.at[0],
            dst_ref=squares_in.at[step],
            send_sem=square_sem.at[0, step],
            recv_sem=square_sem.at[1, step],
            device_id=(lax.rem(req + step, req_count), kv),
            device_id_type=MESH,
        )

    def total_copy(dy, dc):
        slot = 2 * dy + dc
        return pltpu.make_async_remote_copy(
            src_ref=squares.at[1],
            dst_ref=totals_in.at[slot],
            send_sem=total_sem.at[0, slot],
            recv_sem=total_sem.at[1, slot],
            device_id=(req, partner(kv, dy, dc, ny)),
            device_id_type=MESH,
        )

    for part in range(2):
        for dy in range(1, ny):
            gather_copy(dy, part).start()
    x_own = x_all[0].astype(jnp.float32)
    own = column_to_row(jnp.sum(x_own * x_own, axis=1, keepdims=True))
    squares[0] = jnp.broadcast_to(own, squares.shape[1:])
    for step in range(1, req_count):
        square_copy(step).start()
    for part in range(2):
        share_copy(0, part).start()
    total = squares[0]
    for step in range(1, req_count):
        square_copy(step).wait_recv()
        total = total + squares_in[step]
    squares[1] = total
    others = [(dy, dc) for dy in range(ny) for dc in range(2) if dy or dc]
    for dy, dc in others:
        total_copy(dy, dc).start()
    rate_rows = [None] * kv_count
    rate_rows[0] = lax.rsqrt(total[0:1] / (width * req_count) + epsilon_norm)
    for dy, dc in others:
        total_copy(dy, dc).wait_recv()
        rate_rows[2 * dy + dc] = lax.rsqrt(
            totals_in[2 * dy + dc, 0:1] / (width * req_count) + epsilon_norm
        )
    def pick_rows(k, carry):
        at = pl.ds(pl.multiple_of(k * block, block), block)
        wanted = tok_ref[at, :]
        rate = jnp.zeros((block, 1), jnp.float32)
        for slot in range(kv_count):
            places = lax.broadcasted_iota(jnp.int32, (block, shard), 1) + slot * shard
            pick = wanted == places
            rate = rate + jnp.sum(jnp.where(pick, rate_rows[slot], 0.0), axis=1, keepdims=True)
            picks[at, slot * shard : (slot + 1) * shard] = jnp.where(pick, 1.0, 0.0).astype(
                jnp.bfloat16
            )
        rates[at, :] = rate
        return carry

    lax.fori_loop(0, req_count, pick_rows, 0)
    for part in range(2):
        for dy in range(1, ny):
            gather_copy(dy, part).wait_recv()
            share_copy(dy, part).start()
    for dy in range(ny):
        for part in range(2):
            share_copy(dy, part).wait_recv()
    w_copy.wait()
    rows_of_all = x_all[...].reshape(kv_count * shard, width)

    def normalise(k):
        at = pl.ds(pl.multiple_of(k * block, block), block)
        rows = jnp.dot(picks[at, :], rows_of_all, preferred_element_type=jnp.float32)
        normed[at, :] = (rows * rates[at, :] * gain_ref[...]).astype(jnp.bfloat16)

    def product(k, first, last):
        at = pl.ds(pl.multiple_of(k * block, block), block)
        return jnp.dot(normed[at, :], w_all[:, first:last], preferred_element_type=jnp.float32)

    targets = (chosen_of(req, ahead_of), chosen_of(req, behind_of))

    def ring_copy(step, piece):
        way, first, last = pieces[piece]
        columns = pl.ds(first, last - first)
        return pltpu.make_async_remote_copy(
            src_ref=leave.at[step, :, columns],
            dst_ref=land.at[step, :, columns],
            send_sem=ring_sem.at[0, step, piece],
            recv_sem=ring_sem.at[1, step, piece],
            device_id=(targets[way], kv),
            device_id_type=MESH,
        )

    def step_copy(step, piece):
        return pltpu.make_async_remote_copy(
            src_ref=steps_out.at[step, piece],
            dst_ref=steps_in.at[step, piece],
            send_sem=step_sem.at[0, step, piece],
            recv_sem=step_sem.at[1, step, piece],
            device_id=(targets[pieces[piece][0]], kv),
            device_id_type=MESH,
        )

    def pass_on(step, piece, value):
        way, first, last = pieces[piece]
        top = jnp.maximum(jnp.max(jnp.abs(value), axis=1, keepdims=True), 1e-30)
        steps_out[step, piece] = jnp.broadcast_to(
            column_to_row(top * (1.0 / 32767.0)), steps_out.shape[2:]
        )
        step_copy(step, piece).start()
        codes = jnp.floor(value * (32767.0 / top) + 0.5).astype(jnp.int32)
        leave[step, :, first:last] = codes.astype(jnp.int16)
        ring_copy(step, piece).start()

    def arrived(step, piece):
        way, first, last = pieces[piece]
        step_copy(step, piece).wait_recv()
        unit = row_to_column(steps_in[step, piece, 0:1])
        ring_copy(step, piece).wait_recv()
        codes = land[step, :, first:last].astype(jnp.int32)
        return codes.astype(jnp.float32) * unit

    order = sorted(range(len(pieces)), key=lambda p: p % 2)
    normalise(req_count - 1)
    normalise(1)
    for piece in range(len(pieces)):
        way, first, last = pieces[piece]
        pass_on(0, piece, product(1 if way else req_count - 1, first, last))

    def rest(k, carry):
        normalise(lax.rem(k, req_count))
        return carry

    lax.fori_loop(2, req_count - 1, rest, 0)
    normalise(0)

    def one_step(step, carry):
        for piece in order:
            way, first, last = pieces[piece]
            k = 2 + step if way else req_count - 2 - step
            added = product(k, first, last)
            pass_on(step + 1, piece, arrived(step, piece) + added)
        return carry

    lax.fori_loop(0, req_count - 2, one_step, 0)
    half = head_size // 2
    for piece in order:
        way, first, last = pieces[piece]
        added = product(0, first, last)
        summed = arrived(req_count - 2, piece) + added
        for place in range((last - first) // head_size):
            vector = summed[:, place * head_size : (place + 1) * head_size]
            start = first + place * head_size
            if (start // head_size) % (group_size + 2) <= group_size:
                vector = vector * cos_ref[...] + pltpu.roll(vector, half, 1) * sin_ref[...]
            out_ref[:, start : start + head_size] = vector.astype(jnp.bfloat16)

    for dy in range(1, ny):
        for part in range(2):
            gather_copy(dy, part).wait_send()
    for dy in range(ny):
        for part in range(2):
            share_copy(dy, part).wait_send()
    for step in range(1, req_count):
        square_copy(step).wait_send()
    for dy, dc in others:
        total_copy(dy, dc).wait_send()

    def sent(step, carry):
        for piece in range(len(pieces)):
            ring_copy(step, piece).wait_send()
            step_copy(step, piece).wait_send()
        return carry

    lax.fori_loop(0, req_count - 1, sent, 0)


def qkv_call(x, gain, tok, weight, head_size, cosine, sine, heads, group_size):
    req_count = lax.axis_size("req")
    kv_count = lax.axis_size("kv")
    ring, ahead_of, behind_of, place_of = ring_of(req_count)
    shard, width = x.shape
    columns = heads * (group_size + 2) * head_size
    block = shard * kv_count // req_count
    vectors = columns // head_size
    half = vectors // 2
    pieces = []
    for way in range(2):
        middle = way * half + (half + 1) // 2
        pieces.append((way, way * half * head_size, middle * head_size))
        pieces.append((way, middle * head_size, (way + 1) * half * head_size))
    sizes = (req_count, kv_count, group_size, head_size, pieces, ahead_of, behind_of)
    vmem = pl.BlockSpec(memory_space=pltpu.VMEM)
    anywhere = pl.BlockSpec(memory_space=pl.ANY)
    dma = pltpu.SemaphoreType.DMA
    return pl.pallas_call(
        functools.partial(qkv_kernel, sizes),
        out_shape=jax.ShapeDtypeStruct((block, columns), jnp.bfloat16),
        in_specs=[anywhere, vmem, vmem, anywhere, vmem, vmem],
        out_specs=vmem,
        scratch_shapes=[
            pltpu.VMEM((kv_count, shard, width), jnp.bfloat16),
            pltpu.VMEM((width, columns), jnp.bfloat16),
            pltpu.VMEM((kv_count * shard, kv_count * shard), jnp.bfloat16),
            pltpu.VMEM((kv_count * shard, 1), jnp.float32),
            pltpu.VMEM((kv_count * shard, width), jnp.bfloat16),
            pltpu.VMEM((2, 8, shard), jnp.float32),
            pltpu.VMEM((req_count, 8, shard), jnp.float32),
            pltpu.VMEM((kv_count, 8, shard), jnp.float32),
            pltpu.VMEM((req_count - 1, block, columns), jnp.int16),
            pltpu.VMEM((req_count - 1, block, columns), jnp.int16),
            pltpu.VMEM((req_count - 1, len(pieces), 8, block), jnp.float32),
            pltpu.VMEM((req_count - 1, len(pieces), 8, block), jnp.float32),
            dma((2,)),
            dma((2, req_count)),
            dma((2, kv_count)),
            dma((2, kv_count // 2, 2)),
            dma((2, kv_count // 2, 2)),
            dma((2, req_count - 1, len(pieces))),
            dma((2, req_count - 1, len(pieces))),
        ],
        compiler_params=pltpu.CompilerParams(
            collective_id=0, has_side_effects=True, vmem_limit_bytes=56 << 20
        ),
    )(x, gain, tok, weight, cosine, sine)


def out_kernel(
    sizes,
    att_hbm,
    w_hbm,
    x_ref,
    gain_ref,
    row_ref,
    projected_ref,
    normed_ref,
    att,
    w_all,
    products,
    picks,
    taken,
    mine,
    lent,
    borrowed,
    crossing,
    crossed,
    squares,
    squares_in,
    local_sem,
    ring_sem,
    lend_sem,
    cross_sem,
    square_sem,
):
    req_count, kv_count, ahead_of, behind_of = sizes
    ny = kv_count // 2
    block = att_hbm.shape[0]
    inner = att_hbm.shape[1]
    shard, width = x_ref.shape
    att_copy = pltpu.make_async_copy(att_hbm, att.at[0], local_sem.at[0])
    w_copy = pltpu.make_async_copy(w_hbm, w_all, local_sem.at[1])
    att_copy.start()
    w_copy.start()
    req, kv = enter(req_count, kv_count)
    att_copy.wait()
    targets = (chosen_of(req, ahead_of), chosen_of(req, behind_of))
    half_way = req_count // 2
    wide = inner // 2

    def ring_copy(step, way, part):
        source = (lax.rem(req_count - step + 1, req_count), step - 1)[way]
        target = (req_count - step, step)[way]
        columns = pl.ds(part * wide, wide)
        return pltpu.make_async_remote_copy(
            src_ref=att.at[source, :, columns],
            dst_ref=att.at[target, :, columns],
            send_sem=ring_sem.at[0, step, way, part],
            recv_sem=ring_sem.at[1, step, way, part],
            device_id=(targets[way], kv),
            device_id_type=MESH,
        )

    def multiply(k):
        at = pl.ds(k * block, block)
        products[at, :] = jnp.dot(
            att[k], w_all[...], preferred_element_type=jnp.float32
        ).astype(jnp.bfloat16)

    for part in range(2):
        for way in range(2):
            if half_way > 1 or part == way:
                ring_copy(1, way, part).start()
    w_copy.wait()
    multiply(0)
    rows_total = req_count * block
    groups = [(dy, dc, part) for dy in range(ny) for dc in range(2) for part in range(2)]
    count = shard // 2

    def pick_rows(index, carry):
        wanted = row_ref[pl.ds(pl.multiple_of(index * count, count), count), :]
        places = lax.broadcasted_iota(jnp.int32, (count, rows_total), 1)
        picks[pl.ds(pl.multiple_of(index * count, count), count), :] = jnp.where(
            wanted == places, 1.0, 0.0
        ).astype(jnp.bfloat16)
        return carry

    lax.fori_loop(0, len(groups), pick_rows, 0)
    for step in range(1, half_way):
        for part in range(2):
            for way in range(2):
                ring_copy(step, way, part).wait_recv()
                if step + 1 < half_way or part == way:
                    ring_copy(step + 1, way, part).start()
        multiply(req_count - step)
        multiply(step)
    products[half_way * block : (half_way + 1) * block, :] = jnp.zeros((block, width), jnp.bfloat16)

    def take(index, carry):
        at = pl.ds(pl.multiple_of(index * count, count), count)
        taken[at, :] = jnp.dot(
            picks[at, :], products[...], preferred_element_type=jnp.float32
        )
        return carry

    lax.fori_loop(0, len(groups), take, 0)
    for way in range(2):
        ring_copy(half_way, way, way).wait_recv()
    multiply(half_way)

    def gathered(dy, dc, part):
        at = groups.index((dy, dc, part)) * count
        return taken[at : at + count, :] + jnp.dot(
            picks[at : at + count, half_way * block : (half_way + 1) * block],
            products[half_way * block : (half_way + 1) * block, :],
            preferred_element_type=jnp.float32,
        )

    def lend_copy(dy, part):
        rows = pl.ds(part * count, count)
        return pltpu.make_async_remote_copy(
            src_ref=lent.at[dy, rows],
            dst_ref=borrowed.at[dy, rows],
            send_sem=lend_sem.at[0, dy, part],
            recv_sem=lend_sem.at[1, dy, part],
            device_id=(req, partner(kv, 0, 1, ny)),
            device_id_type=MESH,
        )

    def cross_copy(dy, part):
        rows = pl.ds(part * count, count)
        return pltpu.make_async_remote_copy(
            src_ref=crossing.at[dy, rows],
            dst_ref=crossed.at[dy, rows],
            send_sem=cross_sem.at[0, dy, part],
            recv_sem=cross_sem.at[1, dy, part],
            device_id=(req, partner(kv, dy, 0, ny)),
            device_id_type=MESH,
        )

    def part_rows(part):
        return slice(part * (shard // 2), (part + 1) * (shard // 2))

    turns = [(dy, part) for dy in list(range(1, ny)) + [0] for part in range(2)]
    for dy, part in turns:
        lent[dy, part_rows(part)] = gathered(dy, 1, part).astype(jnp.bfloat16)
        lend_copy(dy, part).start()
        if dy:
            own = gathered(dy, 0, part)
            lend_copy(dy, part).wait_recv()
            crossing[dy, part_rows(part)] = (
                own + borrowed[dy, part_rows(part)].astype(jnp.float32)
            ).astype(jnp.bfloat16)
            cross_copy(dy, part).start()
    for part in range(2):
        mine[part_rows(part)] = gathered(0, 0, part)
    sums = []
    for part in range(2):
        lend_copy(0, part).wait_recv()
        projection = mine[part_rows(part)] + borrowed[0, part_rows(part)].astype(jnp.float32)
        for dy in range(1, ny):
            cross_copy(dy, part).wait_recv()
            projection = projection + crossed[dy, part_rows(part)].astype(jnp.float32)
        projected_ref[part_rows(part)] = projection.astype(jnp.bfloat16)
        residual = x_ref[part_rows(part)].astype(jnp.float32) + projection
        mine[part_rows(part)] = residual
        sums.append(column_to_row(jnp.sum(residual * residual, axis=1, keepdims=True)))
    squares[...] = jnp.broadcast_to(jnp.concatenate(sums, axis=1), squares.shape)

    def square_copy(step):
        return pltpu.make_async_remote_copy(
            src_ref=squares,
            dst_ref=squares_in.at[step],
            send_sem=square_sem.at[0, step],
            recv_sem=square_sem.at[1, step],
            device_id=(lax.rem(req + step, req_count), kv),
            device_id_type=MESH,
        )

    for step in range(1, req_count):
        square_copy(step).start()
    total = squares[...]
    for step in range(1, req_count):
        square_copy(step).wait_recv()
        total = total + squares_in[step]
    rate = row_to_column(lax.rsqrt(total[0:1] / (width * req_count) + epsilon_norm))
    normed_ref[...] = (mine[...] * rate * gain_ref[...]).astype(jnp.bfloat16)

    for step in range(1, half_way + 1):
        for part in range(2):
            for way in range(2):
                if step < half_way or part == way:
                    ring_copy(step, way, part).wait_send()
    for dy, part in turns:
        lend_copy(dy, part).wait_send()
        if dy:
            cross_copy(dy, part).wait_send()
    for step in range(1, req_count):
        square_copy(step).wait_send()


def out_call(attention, weight, x, gain, rows):
    req_count = lax.axis_size("req")
    kv_count = lax.axis_size("kv")
    ring, ahead_of, behind_of, place_of = ring_of(req_count)
    block, inner = attention.shape
    shard, width = x.shape
    ny = kv_count // 2
    vmem = pl.BlockSpec(memory_space=pltpu.VMEM)
    anywhere = pl.BlockSpec(memory_space=pl.ANY)
    dma = pltpu.SemaphoreType.DMA
    made = jax.ShapeDtypeStruct((shard, width), jnp.bfloat16)
    return pl.pallas_call(
        functools.partial(out_kernel, (req_count, kv_count, ahead_of, behind_of)),
        out_shape=(made, made),
        in_specs=[anywhere, anywhere, vmem, vmem, vmem],
        out_specs=(vmem, vmem),
        scratch_shapes=[
            pltpu.VMEM((req_count, block, inner), jnp.bfloat16),
            pltpu.VMEM((inner, width), jnp.bfloat16),
            pltpu.VMEM((req_count * block, width), jnp.bfloat16),
            pltpu.VMEM((kv_count * shard, req_count * block), jnp.bfloat16),
            pltpu.VMEM((kv_count * shard, width), jnp.float32),
            pltpu.VMEM((shard, width), jnp.float32),
            pltpu.VMEM((ny, shard, width), jnp.bfloat16),
            pltpu.VMEM((ny, shard, width), jnp.bfloat16),
            pltpu.VMEM((ny, shard, width), jnp.bfloat16),
            pltpu.VMEM((ny, shard, width), jnp.bfloat16),
            pltpu.VMEM((8, shard), jnp.float32),
            pltpu.VMEM((req_count, 8, shard), jnp.float32),
            dma((2,)),
            dma((2, req_count // 2 + 1, 2, 2)),
            dma((2, ny, 2)),
            dma((2, ny, 2)),
            dma((2, req_count)),
        ],
        compiler_params=pltpu.CompilerParams(
            collective_id=1, has_side_effects=True, vmem_limit_bytes=56 << 20
        ),
    )(attention, weight, x, gain, rows)


def per_device(
    activations,
    input_gain,
    qkv_weight,
    out_weight,
    post_gain,
    cache_entries,
    new_lengths,
    cache_lengths,
    request_slot,
):
    req_count = lax.axis_size("req")
    kv_count = lax.axis_size("kv")
    shard, width_slice = activations.shape
    kvh_local = qkv_weight.shape[1]
    head_size = cache_entries.shape[3] // 2
    vectors = qkv_weight.shape[2] // head_size
    group_size = vectors - 2
    tok_blk = shard * kv_count // req_count
    tok, rows, cosine, sine = plan_call(
        new_lengths, cache_lengths, request_slot, shard, head_size
    )
    rotated = qkv_call(
        activations,
        input_gain.astype(jnp.float32).reshape(1, -1),
        tok,
        qkv_weight.reshape(width_slice, -1),
        head_size,
        cosine,
        sine,
        kvh_local,
        group_size,
    )
    appended = rotated.reshape(tok_blk, kvh_local, vectors, head_size)[
        :, :, group_size:, :
    ].reshape(tok_blk, kvh_local, 2 * head_size)
    attention = block_attention(rotated, cache_entries, new_lengths, cache_lengths, group_size)
    projected, normed = out_call(
        attention,
        out_weight.reshape(-1, width_slice),
        activations,
        post_gain.astype(jnp.float32).reshape(1, -1),
        rows,
    )
    return (projected, normed, appended)


def solution(mesh):
    in_specs = (
        P("kv", "req"),
        P("req"),
        P("req", "kv", None),
        P("kv", None, "req"),
        P("req"),
        P("req", None, "kv", None),
        P(),
        P(),
        P(),
    )
    out_specs = (P("kv", "req"), P("kv", "req"), P("req", "kv", None))
    return jax.shard_map(
        per_device, mesh=mesh, in_specs=in_specs, out_specs=out_specs, check_vma=False
    )
```
